32 devices in a mesh: rep: 8 (over z, y), shard: 4 (over x, core).
Axes of the slice: x: 2, y: 2, z: 4, core: 2. Of those that a mesh axis runs over, the one named last changes fastest.
Arguments:
- tokens: bfloat16 [8192, 2048], P(('rep', 'shard')), may hold values from -6 to 6
- w_query: bfloat16 [2048, 2048], P('shard'), may hold values from -0.125 to 0.125
- w_key: bfloat16 [2048, 2048], P('shard'), may hold values from -0.125 to 0.125
- w_value: bfloat16 [2048, 2048], P('shard'), may hold values from -0.125 to 0.125
- w_out: bfloat16 [2048, 2048], P('shard'), may hold values from -0.75 to 0.75
- w_router: bfloat16 [2048, 16], P('shard'), may hold values from -0.0625 to 0.0625
- norm_attn: bfloat16 [2048], P('shard'), may hold values from 0.5 to 1.5
- norm_ffn: bfloat16 [2048], P('shard'), may hold values from 0.5 to 1.5
- norm_query: bfloat16 [128], P('shard'), may hold values from 0.099609375 to 1.8984375
- norm_key: bfloat16 [128], P('shard'), may hold values from 0.099609375 to 1.8984375
- w_gate: bfloat16 [16, 2048, 1024], P('rep', 'shard'), may hold values from -0.125 to 0.125
- w_up: bfloat16 [16, 2048, 1024], P('rep', 'shard'), may hold values from -0.125 to 0.125
- w_down: bfloat16 [16, 1024, 2048], P('rep', 'shard'), may hold values from -0.75 to 0.75
- segments: int32 [8, 1024], P('rep'), may hold values from 0 to 3, never falling along the last dimension, each value on 1 to 800 neighbouring positions
- routes: int32 [8192, 8], P(('rep', 'shard')), may hold values from 0 to 15, all different within a row; in each aligned block of 256 rows (0 to 255, 256 to 511, ...) at most 144 rows name the same one
- cotangent: bfloat16 [8192, 2048], P(('rep', 'shard')), may hold values from -6 to 6
Outputs:
- output: bfloat16 [8192, 2048], P(('rep', 'shard'))
- tokens_grad: bfloat16 [8192, 2048], P(('rep', 'shard'))
- w_query_grad: float32 [2048, 2048], P('shard')
- w_key_grad: float32 [2048, 2048], P('shard')
- w_value_grad: float32 [2048, 2048], P('shard')
- w_out_grad: float32 [2048, 2048], P('shard')
- w_router_grad: float32 [2048, 16], P('shard')
- norm_attn_grad: float32 [2048], P('shard')
- norm_ffn_grad: float32 [2048], P('shard')
- norm_query_grad: float32 [128], P('shard')
- norm_key_grad: float32 [128], P('shard')
- w_gate_grad: float32 [16, 2048, 1024], P('rep', 'shard')
- w_up_grad: float32 [16, 2048, 1024], P('rep', 'shard')
- w_down_grad: float32 [16, 1024, 2048], P('rep', 'shard')
The draws below stay inside these ranges and needn't reach their ends.
Inputs may be any that keep to these rules, and one draw needn't show every extreme that they name: `segments`: segment numbers never fall along a sequence; each segment holds 1 to 800 positions, one exactly 800. `routes`: each token names 8 different experts. Among the 256 tokens of one device no expert is named more than 144 times, and in every draw some expert is named exactly 144 times by the tokens of some device.
All inputs are finite; a program needn't handle non-finite values.
Results may differ from the reference program's by a relative error of at most 0.025.
Values may be sent and summed in bfloat16 or wider, within the bound.
No kernel may reach another device: no remote copies, remote signals or barrier semaphores. Data moves between devices by JAX's collectives and lax.ppermute only.
A program may use at most 384 MiB of HBM per device.

```python
import math
import jax
import jax.numpy as jnp
import numpy as np
from jax import lax

D = 2048
HEADS = 16
HD = 128
FF = 1024
TOP = 8
TOK_DEV = 256
EXPERTS = 16
LENGTH = 1024
SEQS = 8
TOKENS = 8192
CAP = 144
SEG_COUNT = 4
SEG_MOST = 800
N_REP = 8
N_SHARD = 4


def level_of(rng, dims, shards, least, top_value):
    def one(dim, blocks):
        draws = jax.random.uniform(jax.random.fold_in(jax.random.fold_in(rng, 6), dim), (blocks,), jnp.float32, least / len(shards), top_value / len(shards))
        return jnp.repeat(jnp.exp(draws), dims[dim] // blocks).reshape((-1,) + (1,) * (len(dims) - dim - 1))

    level = one(*shards[0])
    for cut in shards[1:]:
        level = level * one(*cut)
    return level


def split_up(number_of, total, bound, skew):
    loads = [(1 << 20) // math.isqrt(rank ** skew) + 1 for rank in range(2, number_of + 1)]
    surplus, holding = total - bound - (number_of - 1), [1] * (number_of - 1)
    while surplus > 0:
        movable = [i for i in range(number_of - 1) if holding[i] < bound]
        mass, left = sum([loads[i] for i in movable]), surplus
        for i in movable:
            extra = min(bound - holding[i], max(1, left * loads[i] // mass), surplus)
            holding[i] = holding[i] + extra
            surplus = surplus - extra
    return np.array([bound] + holding)


def ragged(own_key, number_of, total, reach, lean):
    if number_of == 2:
        one = jax.random.randint(own_key, (), max(1, total - reach), min(reach, total - 1) + 1)
        return jnp.stack([one, total - one])
    sizes = jnp.asarray(split_up(number_of, total, reach, lean), jnp.int32)
    twos = (number_of - 1) // 2
    source_of, sink = sizes[1:1 + 2 * twos:2], sizes[2:2 + 2 * twos:2]
    slack = jnp.minimum(source_of - 1, reach - sink)
    passed = jax.random.randint(jax.random.fold_in(own_key, 1), (twos,), 0, 1 << 20) % (slack + 1)
    sizes = sizes.at[1:1 + 2 * twos:2].set(source_of - passed).at[2:2 + 2 * twos:2].set(sink + passed)
    return sizes[jax.random.permutation(jax.random.fold_in(own_key, 2), number_of)]


def shared_out(rng, own, number, rows, number_of, top, bound, slope):
    ranking = jax.random.permutation(rng, number_of)
    crowded, ordinary = portions_of(number_of, rows * top, bound, slope, True), portions_of(number_of, rows * top, bound, slope, False)
    places = jnp.arange(number_of)

    def named(lengths, rotation):
        used = int((lengths > 0).sum())
        fixed = max(1, used // 4)
        moved = fixed + (places - fixed + rotation * (used - fixed)) % max(1, number_of - fixed)
        return jnp.zeros((number_of,), jnp.int32).at[ranking[jnp.where(places < fixed, places, moved)]].set(jnp.asarray(lengths, jnp.int32))

    lengths = jnp.where(number % 4 == 0, named(crowded, number // 4), named(ordinary, number - number // 4 - 1))
    mixed = jax.random.permutation(jax.random.fold_in(own, 3), number_of)
    giver, taker = mixed[0:number_of // 2 * 2:2], mixed[1:number_of // 2 * 2:2]
    room = jnp.minimum(lengths[giver] - 1, bound - lengths[taker]) // 2
    room = jnp.where((giver == ranking[0]) | (taker == ranking[0]) | (lengths[taker] == 0), 0, jnp.maximum(room, 0))
    moved = jax.random.randint(jax.random.fold_in(own, 4), (number_of // 2,), 0, 1 << 20) % (room + 1)
    lengths = lengths.at[giver].add(-moved).at[taker].add(moved)
    members = jnp.searchsorted(jnp.cumsum(lengths), jnp.arange(rows * top), side="right").astype(jnp.int32)
    listing = members.reshape(top, rows).T
    listing = listing[jax.random.permutation(jax.random.fold_in(own, 1), rows)]
    rotation = jax.random.randint(jax.random.fold_in(own, 2), (rows, 1), 0, top)
    return jnp.take_along_axis(listing, (jnp.arange(top)[None, :] + rotation) % top, axis=1)


def portions_of(amount, total, limit, slope, full):
    weights = [(1 << 20) // math.isqrt(grade ** slope) + 1 for grade in range(1, amount + 1)]
    largest = limit if full else min(limit, max(-(-total // amount), total * weights[0] // sum(weights)))
    least = 1 if total - largest >= amount - 1 else 0
    given, spare = [largest] + [least] * (amount - 1), total - largest - least * (amount - 1)
    while spare > 0:
        candidates = [i for i in range(1, amount) if given[i] < largest] or [i for i in range(1, amount) if given[i] < limit]
        pool, left = sum([weights[i] for i in candidates]), spare
        for i in candidates:
            addition = min(limit - given[i], max(1, left * weights[i] // pool), spare)
            given[i] = given[i] + addition
            spare = spare - addition
    return np.array(given)


def noise(own_key, dims, scale, bound, shards=(), held_as=jnp.bfloat16):
    values = jax.random.normal(own_key, dims, jnp.float32) * scale
    if len(shards) > 0:
        values = level_of(own_key, dims, shards, -0.22, 0.18) * values
    return jnp.clip(values, min=-bound, max=bound).astype(held_as)


def setup_inputs(seed: int = 0) -> dict:
    streams_of = jax.random.split(jax.random.key(seed), 17)
    tokens = noise(streams_of[0], (TOKENS, D), 1.0, 6.0, ((0, 32),))
    w_query = noise(streams_of[1], (D, HEADS * HD), D ** -0.5, 0.125, ((0, 4),))
    w_key = noise(streams_of[2], (D, HEADS * HD), D ** -0.5, 0.125, ((0, 4),))
    w_value = noise(streams_of[3], (D, HEADS * HD), D ** -0.5, 0.125, ((0, 4),))
    w_out = noise(streams_of[4], (HEADS * HD, D), (HEADS * HD // 32) ** -0.5, 0.75, ((0, 4),))
    w_router = noise(streams_of[5], (D, EXPERTS), (4 * D) ** -0.5, 0.0625, ((0, 4),))
    norm_attn = jnp.clip(1.0 + 0.1 * jax.random.normal(streams_of[6], (D,), jnp.float32), 0.5, 1.5).astype(jnp.bfloat16)
    norm_ffn = jnp.clip(1.0 + 0.1 * jax.random.normal(streams_of[7], (D,), jnp.float32), 0.5, 1.5).astype(jnp.bfloat16)
    norm_query = jnp.clip(1.0 + 0.18 * jax.random.normal(streams_of[8], (HD,), jnp.float32), 0.099609375, 1.8984375).astype(jnp.bfloat16)
    norm_key = jnp.clip(1.0 + 0.18 * jax.random.normal(streams_of[9], (HD,), jnp.float32), 0.099609375, 1.8984375).astype(jnp.bfloat16)
    w_gate = noise(streams_of[10], (EXPERTS, D, FF), D ** -0.5, 0.125, ((0, 8), (1, 4)))
    w_up = noise(streams_of[11], (EXPERTS, D, FF), D ** -0.5, 0.125, ((0, 8), (1, 4)))
    w_down = noise(streams_of[12], (EXPERTS, FF, D), (FF // 16) ** -0.5, 0.75, ((0, 8), (1, 4)))
    segments = jax.vmap(lambda own: jnp.searchsorted(jnp.cumsum(ragged(own, SEG_COUNT, LENGTH, SEG_MOST, 1)), jnp.arange(LENGTH), side="right"))(jax.random.split(streams_of[13], SEQS)).reshape((SEQS, LENGTH)).astype(jnp.int32)
    routes_keys = jax.random.split(jax.random.fold_in(streams_of[14], 1), TOKENS // TOK_DEV)
    routes_turns = jax.random.permutation(jax.random.fold_in(streams_of[14], 3), TOKENS // TOK_DEV)
    routes = jax.vmap(lambda own, number: shared_out(jax.random.fold_in(streams_of[14], 2), own, number, TOK_DEV, EXPERTS, TOP, CAP, 1))(routes_keys, routes_turns).reshape((TOKENS, TOP))
    cotangent = noise(streams_of[15], (TOKENS, D), 1.0, 6.0, ((0, 32),))
    return dict(tokens=tokens, w_query=w_query, w_key=w_key, w_value=w_value, w_out=w_out, w_router=w_router, norm_attn=norm_attn, norm_ffn=norm_ffn, norm_query=norm_query, norm_key=norm_key, w_gate=w_gate, w_up=w_up, w_down=w_down, segments=segments, routes=routes, cotangent=cotangent)


EPSILON = 1e-05
THETA = 50000.0
MASKED = -1e+30
HIGHEST = lax.Precision.HIGHEST

@jax.custom_vjp
def low(v):
    return lax.optimization_barrier(v.astype(jnp.bfloat16)).astype(jnp.float32)

@jax.custom_vjp
def low_back(v):
    return v

def low_keep(v):
    return (low(v), None)

def low_pass(kept, grad):
    return (grad,)

def back_keep(v):
    return (v, None)

def back_low(kept, grad):
    return (low(grad),)
low.defvjp(low_keep, low_pass)
low_back.defvjp(back_keep, back_low)

def matmul(left, right):
    return jnp.dot(left, right, precision=HIGHEST, preferred_element_type=jnp.float32)

def rms_norm(values, gain):
    return values * lax.rsqrt(lax.optimization_barrier(jnp.mean(values * values, axis=-1, keepdims=True)) + EPSILON) * gain

def softmax_rows(scores):
    shifted = jnp.exp(scores - lax.optimization_barrier(jnp.max(scores, axis=-1, keepdims=True)))
    return shifted / lax.optimization_barrier(jnp.sum(shifted, axis=-1, keepdims=True))

def rope_tables(start, count, width):
    position = (start + jnp.arange(count, dtype=jnp.int32)).astype(jnp.float32)
    inverse = THETA ** (-jnp.arange(width // 2, dtype=jnp.float32) * 2.0 / width)
    angles = position[:, None] * inverse[None, :]
    angles = jnp.concatenate([angles, angles], axis=-1)
    return (jnp.cos(angles)[:, None, :], jnp.sin(angles)[:, None, :])

def rotate(values, cosine, sine):
    half = values.shape[-1] // 2
    turned = jnp.concatenate([-values[..., half:], values[..., :half]], axis=-1)
    return values * cosine + turned * sine

def slot_numbers(route_rows, experts):
    flat_routes = route_rows.reshape(-1)
    onehot = (flat_routes[:, None] == jnp.arange(experts, dtype=jnp.int32)[None, :]).astype(jnp.int32)
    before = jnp.cumsum(onehot, axis=0) - onehot
    return lax.optimization_barrier(jnp.sum(before * onehot, axis=1))

def attend(block):
    query, key_rows, value_rows, segment = block
    scores = jnp.einsum('ihd,jhd->hij', query, key_rows, precision=HIGHEST) * HD ** (-0.5)
    same = segment[:, None] == segment[None, :]
    scores = low_back(jnp.where(same[None, :, :], scores, MASKED))
    weights = low(softmax_rows(scores))
    return jnp.einsum('hij,jhd->ihd', weights, value_rows, precision=HIGHEST)

def expert_block(block):
    rows, gate_w, up_w, down_w = block
    gate_pre = low_back(matmul(rows, gate_w))
    up_pre = low_back(matmul(rows, up_w))
    hidden = low(gate_pre / (1.0 + jnp.exp(-gate_pre)) * up_pre)
    return matmul(hidden, down_w)

def expert_slots(route_rows):
    return slot_numbers(route_rows, EXPERTS)

def forward(tokens, w_query, w_key, w_value, w_out, w_router, norm_attn, norm_ffn, norm_query, norm_key, w_gate, w_up, w_down, segments, routes):
    normed_in = low(rms_norm(tokens, norm_attn))
    query_raw = low_back(matmul(normed_in, w_query))
    key_raw = low_back(matmul(normed_in, w_key))
    value_raw = low(low_back(matmul(normed_in, w_value)))
    cosine, sine = rope_tables(0, LENGTH, HD)
    query_heads = low(rotate(rms_norm(query_raw.reshape(SEQS, LENGTH, HEADS, HD), norm_query), cosine, sine))
    key_heads = low(rotate(rms_norm(key_raw.reshape(SEQS, LENGTH, HEADS, HD), norm_key), cosine, sine))
    value_heads = value_raw.reshape(SEQS, LENGTH, HEADS, HD)
    attended = lax.map(jax.checkpoint(attend), (query_heads, key_heads, value_heads, segments))
    mixed = low(low_back(attended.reshape(TOKENS, HEADS * HD)))
    hidden_state = tokens + low_back(matmul(mixed, w_out))
    normed_mid = low(rms_norm(hidden_state, norm_ffn))
    probs = softmax_rows(low_back(matmul(normed_mid, w_router)))
    chosen = jnp.take_along_axis(probs, routes, axis=1)
    gates = chosen / lax.optimization_barrier(jnp.sum(chosen, axis=1, keepdims=True))
    devices = N_REP * N_SHARD
    per_device = routes.reshape(devices, TOK_DEV * TOP)
    slot = jax.vmap(expert_slots)(per_device)
    owner = jnp.arange(devices, dtype=jnp.int32)[:, None] * CAP
    place = (per_device * (devices * CAP) + owner + slot).reshape(-1).astype(jnp.int32)
    token_index = (jnp.arange(TOKENS * TOP, dtype=jnp.int32) // TOP).astype(jnp.int32)
    table = jnp.full((EXPERTS * devices * CAP,), TOKENS, jnp.int32).at[place].set(token_index)
    padded = jnp.concatenate([normed_mid, jnp.zeros((1, D), jnp.float32)], axis=0)
    rows = low_back(padded[table].reshape(EXPERTS, devices * CAP, D))
    results = lax.map(jax.checkpoint(expert_block), (rows, w_gate, w_up, w_down))
    results = low(low_back(results)).reshape(EXPERTS * devices * CAP, D)
    picked = results[place].reshape(TOKENS, TOP, D)
    return hidden_state + lax.optimization_barrier(jnp.sum(gates[:, :, None] * picked, axis=1))

def reference(tokens, w_query, w_key, w_value, w_out, w_router, norm_attn, norm_ffn, norm_query, norm_key, w_gate, w_up, w_down, segments, routes, cotangent):
    floats = tuple((member.astype(jnp.float32) for member in (tokens, w_query, w_key, w_value, w_out, w_router, norm_attn, norm_ffn, norm_query, norm_key, w_gate, w_up, w_down)))

    def whole_layer(*params):
        return forward(*params, segments, routes)
    output, pullback = jax.vjp(whole_layer, *floats)
    grads = pullback(cotangent.astype(jnp.float32))
    return (output.astype(jnp.bfloat16), grads[0].astype(jnp.bfloat16), grads[1], grads[2], grads[3], grads[4], grads[5], grads[6], grads[7], grads[8], grads[9], grads[10], grads[11], grads[12])
```

```python
import functools

import jax
import jax.numpy as jnp
from jax import lax
from jax.experimental import pallas as pl
from jax.experimental.pallas import tpu as pltpu
from jax.sharding import PartitionSpec as P

HEADS = 16
HD = 128
TOP = 8

EPSILON = 1e-05
THETA = 50000.0
MASKED = -1e30
BF = jnp.bfloat16
F32 = jnp.float32
QCHUNK = 256


def rms_scale(values):
    return lax.rsqrt(jnp.mean(values * values, axis=-1, keepdims=True) + EPSILON)


def norm_back(grad, normed, scale):
    return scale * (grad - normed * jnp.mean(grad * normed, axis=-1, keepdims=True))


def dot_t(left, right):
    return lax.dot_general(left, right, (((1,), (1,)), ((), ())), preferred_element_type=F32)


def t_dot(left, right):
    return lax.dot_general(left, right, (((0,), (0,)), ((), ())), preferred_element_type=F32)


def attend_forward(q_ref, k_ref, v_ref, cos_ref, sin_ref, gq_ref, gk_ref, segc_ref, segr_ref, o_ref, kb_ref):
    length = q_ref.shape[0]
    k_raw = k_ref[...]
    k_gained = k_raw * rms_scale(k_raw) * gk_ref[...]
    kb_ref[...] = (
        k_gained * cos_ref[...] + pltpu.roll(k_gained, HD // 2, 1) * sin_ref[...]
    ).astype(BF)

    def step(i, carry):
        rows = pl.ds(pl.multiple_of(i * QCHUNK, QCHUNK), QCHUNK)
        q_raw = q_ref[rows, :]
        gained = q_raw * rms_scale(q_raw) * gq_ref[...]
        qb = (gained * cos_ref[rows, :] + pltpu.roll(gained, HD // 2, 1) * sin_ref[rows, :]).astype(BF)
        scores = dot_t(qb, kb_ref[...]) * (HD**-0.5)
        scores = jnp.where(segc_ref[rows, :] == segr_ref[...], scores, MASKED)
        shifted = jnp.exp(scores - jnp.max(scores, axis=-1, keepdims=True))
        total = jnp.sum(shifted, axis=-1, keepdims=True)
        probs = (shifted * (1.0 / total)).astype(BF)
        o_ref[rows, :] = jnp.dot(probs, v_ref[...], preferred_element_type=F32).astype(BF)
        return carry

    lax.fori_loop(0, length // QCHUNK, step, 0)


def attend_backward(
    q_ref,
    k_ref,
    v_ref,
    do_ref,
    cos_ref,
    sin_ref,
    gq_ref,
    gk_ref,
    segc_ref,
    segr_ref,
    dq_ref,
    dk_ref,
    dv_ref,
    gains_ref,
    kb_ref,
    dk_acc,
    dv_acc,
):
    length = q_ref.shape[0]
    scale = HD**-0.5

    @pl.when(pl.program_id(0) == 0)
    def _():
        gains_ref[...] = jnp.zeros_like(gains_ref)

    k_raw = k_ref[...]
    k_scale = rms_scale(k_raw)
    k_norm = k_raw * k_scale
    k_gained = k_norm * gk_ref[...]
    kb_ref[...] = (
        k_gained * cos_ref[...] + pltpu.roll(k_gained, HD // 2, 1) * sin_ref[...]
    ).astype(BF)
    dk_acc[...] = jnp.zeros_like(dk_acc)
    dv_acc[...] = jnp.zeros_like(dv_acc)

    def step(i, carry):
        rows = pl.ds(pl.multiple_of(i * QCHUNK, QCHUNK), QCHUNK)
        cosine, sine = cos_ref[rows, :], sin_ref[rows, :]
        q_raw = q_ref[rows, :]
        q_scale = rms_scale(q_raw)
        q_norm = q_raw * q_scale
        gained = q_norm * gq_ref[...]
        qb = (gained * cosine + pltpu.roll(gained, HD // 2, 1) * sine).astype(BF)
        scores = dot_t(qb, kb_ref[...]) * scale
        scores = jnp.where(segc_ref[rows, :] == segr_ref[...], scores, MASKED)
        shifted = jnp.exp(scores - jnp.max(scores, axis=-1, keepdims=True))
        total = jnp.sum(shifted, axis=-1, keepdims=True)
        probs = shifted * (1.0 / total)
        grad_o = do_ref[rows, :]
        grad_probs = dot_t(grad_o, v_ref[...])
        dv_acc[...] += t_dot(probs.astype(BF), grad_o)
        weighted = probs * grad_probs
        grad_scores = (weighted - probs * jnp.sum(weighted, axis=-1, keepdims=True)).astype(BF)
        dk_acc[...] += t_dot(grad_scores, qb)
        grad_q = jnp.dot(grad_scores, kb_ref[...], preferred_element_type=F32) * scale
        eq = grad_q * cosine - pltpu.roll(grad_q, HD // 2, 1) * sine
        gains_ref[0:1, :] += jnp.sum(eq * q_norm, axis=0, keepdims=True)
        dq_ref[rows, :] = norm_back(eq * gq_ref[...], q_norm, q_scale).astype(BF)
        return carry

    lax.fori_loop(0, length // QCHUNK, step, 0)
    grad_k = dk_acc[...] * scale
    ek = grad_k * cos_ref[...] - pltpu.roll(grad_k, HD // 2, 1) * sin_ref[...]
    k_raw = k_ref[...]
    k_scale = rms_scale(k_raw)
    k_norm = k_raw * k_scale
    gains_ref[1:2, :] += jnp.sum(ek * k_norm, axis=0, keepdims=True)
    dk_ref[...] = norm_back(ek * gk_ref[...], k_norm, k_scale).astype(BF)
    dv_ref[...] = dv_acc[...].astype(BF)


def attention_specs(length):
    head = pl.BlockSpec((length, HD), lambda h: (0, h))
    table = pl.BlockSpec((length, HD), lambda h: (0, 0))
    gain = pl.BlockSpec((1, HD), lambda h: (0, 0))
    column = pl.BlockSpec((length, 1), lambda h: (0, 0))
    row = pl.BlockSpec((1, length), lambda h: (0, 0))
    return head, table, gain, column, row


def attention_forward(query, key, value, cosine, sine, gain_q, gain_k, seg_column, seg_row):
    length, width = query.shape
    head, table, gain, column, row = attention_specs(length)
    heads = width // HD
    return pl.pallas_call(
        attend_forward,
        grid=(heads,),
        in_specs=[head, head, head, table, table, gain, gain, column, row],
        out_specs=head,
        out_shape=jax.ShapeDtypeStruct((length, width), BF),
        scratch_shapes=[pltpu.VMEM((length, HD), BF)],
        compiler_params=pltpu.CompilerParams(vmem_limit_bytes=40 << 20),
        cost_estimate=pl.CostEstimate(
            flops=4 * heads * length * length * HD * 4,
            bytes_accessed=length * width * 12,
            transcendentals=heads * length * length,
        ),
    )(query, key, value, cosine, sine, gain_q, gain_k, seg_column, seg_row)


def attention_backward(query, key, value, grad_o, cosine, sine, gain_q, gain_k, seg_column, seg_row):
    length, width = query.shape
    head, table, gain, column, row = attention_specs(length)
    heads = width // HD
    out = jax.ShapeDtypeStruct((length, width), BF)
    return pl.pallas_call(
        attend_backward,
        grid=(heads,),
        in_specs=[head, head, head, head, table, table, gain, gain, column, row],
        out_specs=[head, head, head, pl.BlockSpec((8, HD), lambda h: (0, 0))],
        out_shape=[out, out, out, jax.ShapeDtypeStruct((8, HD), F32)],
        scratch_shapes=[
            pltpu.VMEM((length, HD), BF),
            pltpu.VMEM((length, HD), F32),
            pltpu.VMEM((length, HD), F32),
        ],
        compiler_params=pltpu.CompilerParams(vmem_limit_bytes=48 << 20),
        cost_estimate=pl.CostEstimate(
            flops=10 * heads * length * length * HD * 4,
            bytes_accessed=length * width * 18,
            transcendentals=heads * length * length,
        ),
    )(query, key, value, grad_o, cosine, sine, gain_q, gain_k, seg_column, seg_row)


def pick_rows(slots_ref, x_ref, out_ref):
    experts, capacity = out_ref.shape[0], out_ref.shape[2]
    count = x_ref.shape[1]
    for j in range(experts):
        wanted = lax.broadcasted_iota(jnp.int32, (capacity, count), 0)
        hot = (wanted == slots_ref[0, j : j + 1, :]).astype(BF)
        out_ref[j, 0] = jnp.dot(hot, x_ref[0], preferred_element_type=F32).astype(BF)


def pick_scaled(slots_ref, gates_ref, x_ref, out_ref):
    experts, capacity = out_ref.shape[0], out_ref.shape[2]
    count = x_ref.shape[1]
    for j in range(experts):
        wanted = lax.broadcasted_iota(jnp.int32, (capacity, count), 0)
        hot = wanted == slots_ref[0, j : j + 1, :]
        gate = jnp.sum(jnp.where(hot, gates_ref[0, j : j + 1, :], 0.0), axis=1, keepdims=True)
        rows = jnp.dot(hot.astype(BF), x_ref[0], preferred_element_type=F32)
        out_ref[j, 0] = (rows * gate).astype(BF)


def pick(slots, x, capacity, gates=None):
    blocks, count, width = x.shape
    experts = slots.shape[1]
    small = pl.BlockSpec((1, experts, count), lambda b: (b, 0, 0))
    specs = [small] + ([small] if gates is not None else [])
    operands = (slots,) + ((gates,) if gates is not None else ())
    return pl.pallas_call(
        pick_rows if gates is None else pick_scaled,
        grid=(blocks,),
        in_specs=specs + [pl.BlockSpec((1, count, width), lambda b: (b, 0, 0))],
        out_specs=pl.BlockSpec((experts, 1, capacity, width), lambda b: (0, b, 0, 0)),
        out_shape=jax.ShapeDtypeStruct((experts, blocks, capacity, width), BF),
        compiler_params=pltpu.CompilerParams(vmem_limit_bytes=40 << 20),
        cost_estimate=pl.CostEstimate(
            flops=2 * blocks * experts * capacity * count * width,
            bytes_accessed=2 * blocks * width * (count + experts * capacity),
            transcendentals=0,
        ),
    )(*operands, x)


def merge_results(slots_ref, gates_ref, rows_ref, grad_ref, out_ref, dgate_ref):
    experts, capacity = rows_ref.shape[0], rows_ref.shape[2]
    count = out_ref.shape[1]
    grad = grad_ref[0].astype(F32)
    total = None
    dgates = []
    for j in range(experts):
        place = lax.broadcasted_iota(jnp.int32, (count, capacity), 1)
        hot = (place == slots_ref[0, :, j : j + 1]).astype(BF)
        rows = jnp.dot(hot, rows_ref[j, 0], preferred_element_type=F32)
        dgates.append(jnp.sum(rows * grad, axis=1, keepdims=True))
        gated = rows * gates_ref[0, :, j : j + 1]
        total = gated if total is None else total + gated
    out_ref[0] = total.astype(BF)
    dgate_ref[0] = jnp.concatenate(dgates, axis=1)


def merge_rows(slots_ref, rows_ref, out_ref):
    experts, capacity = rows_ref.shape[0], rows_ref.shape[2]
    count = out_ref.shape[1]
    total = None
    for j in range(experts):
        place = lax.broadcasted_iota(jnp.int32, (count, capacity), 1)
        hot = (place == slots_ref[0, :, j : j + 1]).astype(BF)
        rows = jnp.dot(hot, rows_ref[j, 0], preferred_element_type=F32)
        total = rows if total is None else total + rows
    out_ref[0] = total.astype(BF)


def merge(slots, rows, gates=None, grad=None):
    experts, blocks, capacity, width = rows.shape
    count = slots.shape[1]
    small = pl.BlockSpec((1, count, experts), lambda b: (b, 0, 0))
    row_spec = pl.BlockSpec((experts, 1, capacity, width), lambda b: (0, b, 0, 0))
    token_spec = pl.BlockSpec((1, count, width), lambda b: (b, 0, 0))
    token_shape = jax.ShapeDtypeStruct((blocks, count, width), BF)
    cost = pl.CostEstimate(
        flops=2 * blocks * experts * capacity * count * width,
        bytes_accessed=2 * blocks * width * (2 * count + experts * capacity),
        transcendentals=0,
    )
    params = pltpu.CompilerParams(vmem_limit_bytes=40 << 20)
    if gates is None:
        return pl.pallas_call(
            merge_rows,
            grid=(blocks,),
            in_specs=[small, row_spec],
            out_specs=token_spec,
            out_shape=token_shape,
            compiler_params=params,
            cost_estimate=cost,
        )(slots, rows)
    return pl.pallas_call(
        merge_results,
        grid=(blocks,),
        in_specs=[small, small, row_spec, token_spec],
        out_specs=[token_spec, small],
        out_shape=[token_shape, jax.ShapeDtypeStruct((blocks, count, experts), F32)],
        compiler_params=params,
        cost_estimate=cost,
    )(slots, gates, rows, grad)


def swap_core(value):
    return lax.ppermute(value, "shard", [(i, i ^ 1) for i in range(4)])


def swap_x(value):
    return lax.ppermute(value, "shard", [(i, i ^ 2) for i in range(4)])


def shard_order(position):
    return [position, position ^ 1, position ^ 2, position ^ 3]


def shard_gather(value):
    far = swap_x(value)
    near = swap_core(value)
    return [value, near, far, swap_core(far)]


def shard_reduce(blocks):
    far = blocks[2].astype(F32) + swap_core(blocks[3].astype(BF)).astype(F32)
    far = swap_x(far.astype(BF))
    near = blocks[0].astype(F32) + swap_core(blocks[1].astype(BF)).astype(F32)
    return near + far.astype(F32)


def ring_next(count):
    return [(z * 2 + y, ((z + 1) % (count // 2)) * 2 + y) for z in range(count // 2) for y in range(2)]


def swap_y(value, count):
    return lax.ppermute(value, "rep", [(i, i ^ 1) for i in range(count)])


def turn_z(value, count):
    return lax.ppermute(value, "rep", ring_next(count))


def rep_order(rep, count):
    planes = count // 2
    z, y = rep // 2, rep % 2
    return [((z + planes - k) % planes) * 2 + (y ^ w) for k in range(planes) for w in range(2)]


def rep_gather(value, count):
    blocks = []
    held = value
    for k in range(count // 2):
        if k > 0:
            held = turn_z(held, count)
        blocks += [held, swap_y(held, count)]
    return blocks


def rep_reduce(blocks, count):
    planes = count // 2

    def pair(k):
        return blocks[2 * k].astype(F32) + swap_y(blocks[2 * k + 1].astype(BF), count).astype(F32)

    total = pair(1)
    for k in list(range(2, planes)) + [0]:
        total = turn_z(total.astype(BF), count).astype(F32) + pair(k)
    return total


def on_device(
    tokens,
    w_query,
    w_key,
    w_value,
    w_out,
    w_router,
    norm_attn,
    norm_ffn,
    norm_query,
    norm_key,
    w_gate,
    w_up,
    w_down,
    segments,
    routes,
    cotangent,
):
    rows_count, width = tokens.shape
    experts = w_router.shape[1]
    local_experts = w_gate.shape[0]
    rep_count = lax.axis_size("rep")
    shard_count = lax.axis_size("shard")
    position = lax.axis_index("shard")
    rep = lax.axis_index("rep")
    head_width = HEADS * HD // shard_count
    length = rows_count * shard_count
    capacity = max(2, rows_count * TOP * 9 // (8 * experts))
    capacity = -(-capacity // 16) * 16
    rows = w_query.shape[0]

    gains = jnp.concatenate([norm_attn, norm_ffn, norm_query, norm_key])
    gains = lax.all_gather(gains, "shard", axis=0, tiled=False)
    gain_attn = gains[:, :rows].reshape(-1).astype(F32)
    gain_ffn = gains[:, rows : 2 * rows].reshape(-1).astype(F32)
    tail = gains[:, 2 * rows :].reshape(shard_count, 2, -1)
    gain_query = tail[:, 0].reshape(1, HD).astype(F32)
    gain_key = tail[:, 1].reshape(1, HD).astype(F32)
    full_router = lax.all_gather(w_router, "shard", axis=0, tiled=True)

    tokens_f = tokens.astype(F32)
    scale_in = rms_scale(tokens_f)
    normed_in = tokens_f * scale_in
    input_own = (normed_in * gain_attn).astype(BF)
    input_b = jnp.concatenate(shard_gather(input_own), axis=0)

    def columns(weight):
        return lax.all_to_all(weight, "shard", split_axis=1, concat_axis=0, tiled=True)

    cols_query, cols_key, cols_value = columns(w_query), columns(w_key), columns(w_value)

    full_gate = lax.all_gather(w_gate, "shard", axis=1, tiled=True)
    full_up = lax.all_gather(w_up, "shard", axis=1, tiled=True)
    full_down = lax.all_gather(w_down, "shard", axis=1, tiled=True)
    grad_blocks = jnp.stack(rep_gather(cotangent, rep_count))

    order = jnp.stack(rep_order(rep, rep_count))
    route_all = lax.all_gather(routes, "rep", axis=0, tiled=False)[order]
    expert_ids = jnp.arange(experts, dtype=jnp.int32)
    named_all = jnp.any(route_all[:, :, :, None] == expert_ids, axis=2)
    mine = lambda a: lax.dynamic_slice_in_dim(a, rep * local_experts, local_experts, axis=2)
    named_mine = mine(named_all)
    before = jnp.tril(jnp.ones((rows_count, rows_count), BF), -1)
    slot_mine = jnp.einsum("ts,bsj->btj", before, named_mine.astype(BF), preferred_element_type=F32)
    slot_tokens = jnp.where(named_mine, slot_mine.astype(jnp.int32), -1)
    slot_lanes = jnp.swapaxes(slot_tokens, 1, 2)

    query_raw = jnp.dot(input_b, cols_query, preferred_element_type=F32)
    key_raw = jnp.dot(input_b, cols_key, preferred_element_type=F32)
    value_b = jnp.dot(input_b, cols_value, preferred_element_type=F32).astype(BF)
    order_in = shard_order(position)
    places = jnp.concatenate([p * rows_count + jnp.arange(rows_count, dtype=jnp.int32) for p in order_in])
    inverse = THETA ** (-jnp.arange(HD // 2, dtype=F32) * 2.0 / HD)
    angles = places.astype(F32)[:, None] * inverse[None, :]
    cosine, sine = jnp.cos(angles), jnp.sin(angles)
    cosine = jnp.concatenate([cosine, cosine], axis=-1)
    sine = jnp.concatenate([-sine, sine], axis=-1)
    segment_all = jnp.concatenate(
        [lax.dynamic_slice_in_dim(segments[0], p * rows_count, rows_count) for p in order_in]
    )
    attn_args = (cosine, sine, gain_query, gain_key, segment_all[:, None], segment_all[None, :])
    mixed_b = attention_forward(query_raw, key_raw, value_b, *attn_args)
    projected = jnp.dot(mixed_b, w_out, preferred_element_type=F32).astype(BF)
    projected = projected.reshape(shard_count, rows_count, width)
    hidden_state = tokens_f + shard_reduce([projected[i] for i in range(shard_count)])

    scale_mid = rms_scale(hidden_state)
    normed_mid = hidden_state * scale_mid
    mid_b = (normed_mid * gain_ffn).astype(BF)
    mid_blocks = jnp.stack(rep_gather(mid_b, rep_count))

    def router(inputs):
        logits = jnp.einsum("...d,de->...e", inputs, full_router, preferred_element_type=F32)
        exps = jnp.exp(logits - jnp.max(logits, axis=-1, keepdims=True))
        return exps / jnp.sum(exps, axis=-1, keepdims=True)

    probs_all = router(mid_blocks)
    chosen_all = jnp.where(named_all, probs_all, 0.0)
    gates_all = chosen_all / jnp.sum(chosen_all, axis=-1, keepdims=True)
    gate_tokens = mine(gates_all)
    gate_lanes = jnp.swapaxes(gate_tokens, 1, 2)

    expert_rows = pick(slot_lanes, mid_blocks, capacity)
    grad_rows = pick(slot_lanes, grad_blocks, capacity, gate_lanes)
    count = rep_count * capacity
    expert_rows = expert_rows.reshape(local_experts, count, width)
    grad_rows = grad_rows.reshape(local_experts, count, width)
    results, grad_ins, kept = [], [], []
    for j in range(local_experts):
        x = expert_rows[j]
        gate_pre = jnp.dot(x, full_gate[j], preferred_element_type=F32)
        up_pre = jnp.dot(x, full_up[j], preferred_element_type=F32)
        sigmoid = 1.0 / (1.0 + jnp.exp(-gate_pre))
        activated = gate_pre * sigmoid
        hidden_b = (activated * up_pre).astype(BF)
        results.append(jnp.dot(hidden_b, full_down[j], preferred_element_type=F32).astype(BF))
        grad_hidden = dot_t(grad_rows[j], full_down[j])
        grad_gate_pre = (
            grad_hidden * up_pre * sigmoid * (1.0 + gate_pre * (1.0 - sigmoid))
        ).astype(BF)
        grad_up_pre = (grad_hidden * activated).astype(BF)
        grad_in = dot_t(grad_gate_pre, full_gate[j]) + dot_t(grad_up_pre, full_up[j])
        grad_ins.append(grad_in.astype(BF))
        kept.append((x, hidden_b, grad_rows[j], grad_gate_pre, grad_up_pre))
    shape = (local_experts, rep_count, capacity, width)
    grad_parts = merge(slot_tokens, jnp.stack(grad_ins).reshape(shape))
    result_parts, dgate_parts = merge(
        slot_tokens, jnp.stack(results).reshape(shape), gate_tokens, grad_blocks
    )
    grad_mid_moe = rep_reduce([grad_parts[i] for i in range(rep_count)], rep_count)
    expert_sum = rep_reduce([result_parts[i] for i in range(rep_count)], rep_count)
    output = (hidden_state + expert_sum).astype(BF)

    def owned_part(parts):
        return lax.psum_scatter(
            jnp.stack(parts), "shard", scatter_dimension=1, tiled=True
        ).astype(F32)

    grad_gate = owned_part([t_dot(x, dg).astype(BF) for x, _, _, dg, _ in kept])
    grad_up = owned_part([t_dot(x, du).astype(BF) for x, _, _, _, du in kept])
    grad_down = owned_part([t_dot(h, dy).astype(BF) for _, h, dy, _, _ in kept])

    inverse_order = jnp.zeros((rep_count,), jnp.int32).at[order].set(
        jnp.arange(rep_count, dtype=jnp.int32)
    )
    dgates = lax.all_to_all(
        jnp.swapaxes(dgate_parts, 1, 2)[inverse_order], "rep", split_axis=0, concat_axis=0, tiled=True
    )
    dgates = dgates.reshape(experts, rows_count).T
    named_own = jnp.any(routes[:, :, None] == expert_ids, axis=1)
    probs_own = router(mid_b)
    chosen_total = jnp.sum(jnp.where(named_own, probs_own, 0.0), axis=1, keepdims=True)
    gates_own = jnp.where(named_own, probs_own, 0.0) / chosen_total
    grad_probs = jnp.where(
        named_own, dgates - jnp.sum(dgates * gates_own, axis=1, keepdims=True), 0.0
    ) / chosen_total
    grad_logits = (
        probs_own * (grad_probs - jnp.sum(probs_own * grad_probs, axis=1, keepdims=True))
    ).astype(BF)
    grad_mid = grad_mid_moe + dot_t(grad_logits, full_router)
    grad_gain_ffn = jnp.sum(grad_mid * normed_mid, axis=0)
    grad_router = t_dot(mid_b, grad_logits)
    grad_out = cotangent.astype(F32)
    grad_state = grad_out + norm_back(grad_mid * gain_ffn, normed_mid, scale_mid)
    grad_state_b = grad_state.astype(BF)

    grad_state_all = jnp.concatenate(shard_gather(grad_state_b), axis=0)
    grad_mixed = dot_t(grad_state_all, w_out).astype(BF)
    grad_out_proj = t_dot(mixed_b, grad_state_all)
    grad_query_raw, grad_key_raw, grad_value_raw, grad_head_gains = attention_backward(
        query_raw, key_raw, value_b, grad_mixed, *attn_args
    )
    grad_input = (
        dot_t(grad_query_raw, cols_query)
        + dot_t(grad_key_raw, cols_key)
        + dot_t(grad_value_raw, cols_value)
    ).astype(BF)
    grad_input = grad_input.reshape(shard_count, rows_count, width)
    grad_input = shard_reduce([grad_input[i] for i in range(shard_count)])
    grad_gain_attn = jnp.sum(grad_input * normed_in, axis=0)
    tokens_grad = (grad_state + norm_back(grad_input * gain_attn, normed_in, scale_in)).astype(BF)

    part = rows // rep_count

    def spread(grad):
        view = grad.astype(BF).reshape(shard_count, rep_count, part, -1)
        return [
            lax.dynamic_index_in_dim(view, r, axis=1, keepdims=False) for r in rep_order(rep, rep_count)
        ]

    def collected(part_sum):
        whole = jnp.stack(rep_gather(part_sum, rep_count))[inverse_order]
        return whole.reshape(rows, -1).astype(F32)

    def summed_columns(grad):
        mine_part = rep_reduce(spread(grad), rep_count).astype(BF)
        mine_part = lax.all_to_all(mine_part, "shard", split_axis=0, concat_axis=0, tiled=True)
        mine_part = jnp.swapaxes(mine_part, 0, 1).reshape(part, -1)
        return collected(mine_part)

    view = grad_out_proj.astype(BF).reshape(rep_count, part, width)
    out_part = rep_reduce(
        [lax.dynamic_index_in_dim(view, r, axis=0, keepdims=False) for r in rep_order(rep, rep_count)],
        rep_count,
    ).astype(BF)
    sum_out = collected(out_part)
    sum_query = summed_columns(t_dot(input_b, grad_query_raw))
    sum_key = summed_columns(t_dot(input_b, grad_key_raw))
    sum_value = summed_columns(t_dot(input_b, grad_value_raw))

    first = jnp.concatenate([grad_router.reshape(-1), grad_gain_ffn])
    first = lax.psum(first, ("rep", "shard"))
    second = jnp.concatenate([grad_gain_attn, grad_head_gains[0], grad_head_gains[1]])
    second = lax.psum(second, ("rep", "shard"))

    def own_slice(vector, start, size):
        piece = size // shard_count
        return lax.dynamic_slice_in_dim(vector, start + position * piece, piece)

    sum_router = own_slice(first, 0, width * experts).reshape(rows, experts)
    sum_ffn = own_slice(first, width * experts, width)
    sum_attn = own_slice(second, 0, width)
    sum_hquery = own_slice(second, width, HD)
    sum_hkey = own_slice(second, width + HD, HD)
    return (
        output,
        tokens_grad,
        sum_query,
        sum_key,
        sum_value,
        sum_out,
        sum_router,
        sum_attn,
        sum_ffn,
        sum_hquery,
        sum_hkey,
        grad_gate,
        grad_up,
        grad_down,
    )


def solution(mesh):
    return jax.shard_map(
        on_device,
        mesh=mesh,
        in_specs=(
            P(("rep", "shard"), None),
            P("shard", None),
            P("shard", None),
            P("shard", None),
            P("shard", None),
            P("shard", None),
            P("shard"),
            P("shard"),
            P("shard"),
            P("shard"),
            P("rep", "shard", None),
            P("rep", "shard", None),
            P("rep", "shard", None),
            P("rep", None),
            P(("rep", "shard"), None),
            P(("rep", "shard"), None),
        ),
        out_specs=(
            P(("rep", "shard"), None),
            P(("rep", "shard"), None),
            P("shard", None),
            P("shard", None),
            P("shard", None),
            P("shard", None),
            P("shard", None),
            P("shard"),
            P("shard"),
            P("shard"),
            P("shard"),
            P("rep", "shard", None),
            P("rep", "shard", None),
            P("rep", "shard", None),
        ),
        check_vma=False,
    )
```

```python
import functools

import jax
import jax.numpy as jnp
from jax import lax
from jax.experimental import pallas as pl
from jax.experimental.pallas import tpu as pltpu
from jax.sharding import PartitionSpec as P

HEADS = 16
HD = 128
TOP = 8

EPSILON = 1e-05
THETA = 50000.0
MASKED = -1e30
BF = jnp.bfloat16
F32 = jnp.float32
QCHUNK = 256


def rms_scale(values):
    return lax.rsqrt(jnp.mean(values * values, axis=-1, keepdims=True) + EPSILON)


def norm_back(grad, normed, scale):
    return scale * (grad - normed * jnp.mean(grad * normed, axis=-1, keepdims=True))


def dot(left, right):
    return jnp.dot(left, right, preferred_element_type=F32)


def dot_t(left, right):
    return lax.dot_general(left, right, (((1,), (1,)), ((), ())), preferred_element_type=F32)


def t_dot(left, right):
    return lax.dot_general(left, right, (((0,), (0,)), ((), ())), preferred_element_type=F32)


def params(mib):
    return pltpu.CompilerParams(vmem_limit_bytes=mib << 20)


def cost(flops, size, transcendentals=0):
    return pl.CostEstimate(
        flops=int(flops), bytes_accessed=int(size), transcendentals=int(transcendentals)
    )


def after(value, *others):
    return lax.optimization_barrier((value,) + others)[0]


def pack_columns(q_ref, k_ref, v_ref, out_ref):
    for h in range(q_ref.shape[1] // HD):
        for m, ref in enumerate((q_ref, k_ref, v_ref)):
            start = (3 * h + m) * HD
            out_ref[0, :, start : start + HD] = ref[:, h * HD : (h + 1) * HD]


def packed_columns(w_query, w_key, w_value, shards):
    rows, width = w_query.shape
    part = width // shards
    spec = pl.BlockSpec((rows, part), lambda s: (0, s))
    return pl.pallas_call(
        pack_columns,
        grid=(shards,),
        in_specs=[spec, spec, spec],
        out_specs=pl.BlockSpec((1, rows, 3 * part), lambda s: (s, 0, 0)),
        out_shape=jax.ShapeDtypeStruct((shards, rows, 3 * part), BF),
        compiler_params=params(32),
        cost_estimate=cost(0, 12 * rows * width),
    )(w_query, w_key, w_value)


def turned(values, cosine, sine):
    return values * cosine + pltpu.roll(values, HD // 2, 1) * sine


def turned_back(grad, cosine, sine):
    return grad * cosine - pltpu.roll(grad, HD // 2, 1) * sine


def weights_of(qb, keys, seg_column, seg_row):
    scores = dot_t(qb, keys) * (HD**-0.5)
    scores = jnp.where(seg_column == seg_row, scores, MASKED)
    shifted = jnp.exp(scores - jnp.max(scores, axis=-1, keepdims=True))
    return shifted * (1.0 / jnp.sum(shifted, axis=-1, keepdims=True))


def attend_forward(qkv_ref, cos_ref, sin_ref, gq_ref, gk_ref, segc_ref, segr_ref, o_ref, kb_ref, vb_ref):
    length = qkv_ref.shape[0]
    k_raw = qkv_ref[:, HD : 2 * HD]
    kb_ref[...] = turned(k_raw * rms_scale(k_raw) * gk_ref[...], cos_ref[...], sin_ref[...]).astype(BF)
    vb_ref[...] = qkv_ref[:, 2 * HD :].astype(BF)

    def step(i, carry):
        rows = pl.ds(pl.multiple_of(i * QCHUNK, QCHUNK), QCHUNK)
        q_raw = qkv_ref[rows, :HD]
        qb = turned(q_raw * rms_scale(q_raw) * gq_ref[...], cos_ref[rows, :], sin_ref[rows, :]).astype(BF)
        probs = weights_of(qb, kb_ref[...], segc_ref[rows, :], segr_ref[...])
        o_ref[rows, :] = dot(probs.astype(BF), vb_ref[...]).astype(BF)
        return carry

    lax.fori_loop(0, length // QCHUNK, step, 0)


def attend_backward(
    qkv_ref,
    do_ref,
    cos_ref,
    sin_ref,
    gq_ref,
    gk_ref,
    segc_ref,
    segr_ref,
    grad_ref,
    gains_ref,
    kb_ref,
    vb_ref,
    dk_acc,
    dv_acc,
):
    length = qkv_ref.shape[0]
    scale = HD**-0.5

    @pl.when(pl.program_id(0) == 0)
    def _():
        gains_ref[...] = jnp.zeros_like(gains_ref)

    k_raw = qkv_ref[:, HD : 2 * HD]
    kb_ref[...] = turned(k_raw * rms_scale(k_raw) * gk_ref[...], cos_ref[...], sin_ref[...]).astype(BF)
    vb_ref[...] = qkv_ref[:, 2 * HD :].astype(BF)
    dk_acc[...] = jnp.zeros_like(dk_acc)
    dv_acc[...] = jnp.zeros_like(dv_acc)

    def step(i, carry):
        rows = pl.ds(pl.multiple_of(i * QCHUNK, QCHUNK), QCHUNK)
        cosine, sine = cos_ref[rows, :], sin_ref[rows, :]
        q_raw = qkv_ref[rows, :HD]
        q_scale = rms_scale(q_raw)
        q_norm = q_raw * q_scale
        qb = turned(q_norm * gq_ref[...], cosine, sine).astype(BF)
        probs = weights_of(qb, kb_ref[...], segc_ref[rows, :], segr_ref[...])
        grad_o = do_ref[rows, :]
        grad_probs = dot_t(grad_o, vb_ref[...])
        dv_acc[...] += t_dot(probs.astype(BF), grad_o)
        weighted = probs * grad_probs
        grad_scores = (weighted - probs * jnp.sum(weighted, axis=-1, keepdims=True)).astype(BF)
        dk_acc[...] += t_dot(grad_scores, qb)
        eq = turned_back(dot(grad_scores, kb_ref[...]) * scale, cosine, sine)
        gains_ref[0:1, :] += jnp.sum(eq * q_norm, axis=0, keepdims=True)
        grad_ref[rows, :HD] = norm_back(eq * gq_ref[...], q_norm, q_scale).astype(BF)
        return carry

    lax.fori_loop(0, length // QCHUNK, step, 0)
    ek = turned_back(dk_acc[...] * scale, cos_ref[...], sin_ref[...])
    k_raw = qkv_ref[:, HD : 2 * HD]
    k_scale = rms_scale(k_raw)
    k_norm = k_raw * k_scale
    gains_ref[1:2, :] += jnp.sum(ek * k_norm, axis=0, keepdims=True)
    grad_ref[:, HD : 2 * HD] = norm_back(ek * gk_ref[...], k_norm, k_scale).astype(BF)
    grad_ref[:, 2 * HD :] = dv_acc[...].astype(BF)


def attention_specs(length):
    table = pl.BlockSpec((length, HD), lambda h: (0, 0))
    gain = pl.BlockSpec((1, HD), lambda h: (0, 0))
    column = pl.BlockSpec((length, 1), lambda h: (0, 0))
    row = pl.BlockSpec((1, length), lambda h: (0, 0))
    return [table, table, gain, gain, column, row]


def attention_forward(qkv, attn_args):
    length = qkv.shape[0]
    heads = qkv.shape[1] // (3 * HD)
    return pl.pallas_call(
        attend_forward,
        grid=(heads,),
        in_specs=[pl.BlockSpec((length, 3 * HD), lambda h: (0, h))] + attention_specs(length),
        out_specs=pl.BlockSpec((length, HD), lambda h: (0, h)),
        out_shape=jax.ShapeDtypeStruct((length, heads * HD), BF),
        scratch_shapes=[pltpu.VMEM((length, HD), BF)] * 2,
        compiler_params=params(40),
        cost_estimate=cost(16 * heads * length * length * HD, qkv.size * 5, heads * length * length),
    )(qkv, *attn_args)


def attention_backward(qkv, grad_o, attn_args):
    length = qkv.shape[0]
    heads = qkv.shape[1] // (3 * HD)
    wide = pl.BlockSpec((length, 3 * HD), lambda h: (0, h))
    return pl.pallas_call(
        attend_backward,
        grid=(heads,),
        in_specs=[wide, pl.BlockSpec((length, HD), lambda h: (0, h))] + attention_specs(length),
        out_specs=[wide, pl.BlockSpec((8, HD), lambda h: (0, 0))],
        out_shape=[
            jax.ShapeDtypeStruct(qkv.shape, BF),
            jax.ShapeDtypeStruct((8, HD), F32),
        ],
        scratch_shapes=[pltpu.VMEM((length, HD), BF)] * 2 + [pltpu.VMEM((length, HD), F32)] * 2,
        compiler_params=params(48),
        cost_estimate=cost(40 * heads * length * length * HD, qkv.size * 7, heads * length * length),
    )(qkv, grad_o, *attn_args)


def pick_rows(has_input, number_ref, slots_ref, named_ref, router_ref, x_ref, grad_ref, *refs):
    rows_ref, grad_rows_ref, gates_ref = refs[2 * has_input :]
    experts, capacity = slots_ref.shape[1], rows_ref.shape[2]
    count = x_ref.shape[0]
    x = x_ref[...]
    named = named_ref[0]
    logits = dot(x, router_ref[...])
    lane = lax.broadcasted_iota(jnp.int32, logits.shape, 1)
    logits = jnp.where(lane < number_ref[2], logits, MASKED)
    exps = jnp.exp(logits - jnp.max(logits, axis=-1, keepdims=True))
    probs = exps / jnp.sum(exps, axis=-1, keepdims=True)
    chosen = jnp.where(named > 0.0, probs, 0.0)
    gates = chosen / jnp.sum(chosen, axis=-1, keepdims=True)
    grad = grad_ref[0].astype(F32)
    wanted = lax.broadcasted_iota(jnp.int32, (capacity, count), 0)
    columns = []
    for j in range(experts):
        gate = jnp.sum(jnp.where(lane == number_ref[1] + j, gates, 0.0), axis=1, keepdims=True)
        hot = (wanted == slots_ref[0, j : j + 1, :]).astype(BF)
        rows_ref[j, 0] = dot(hot, x).astype(BF)
        grad_rows_ref[j, 0] = dot(hot, (grad * gate).astype(BF)).astype(BF)
        columns.append(gate)
    gates_ref[...] = jnp.concatenate(columns, axis=1)


def pick(number, slots, named, router, x, grads, held, place, blocks, capacity):
    count, width = x.shape
    experts = slots.shape[1]
    lanes = router.shape[1]
    shape = jax.ShapeDtypeStruct((experts, blocks, capacity, width), BF)
    whole = pl.BlockSpec(memory_space=pl.ANY)
    out = pl.BlockSpec((experts, 1, capacity, width), lambda i, n: (0, place, 0, 0))
    return pl.pallas_call(
        functools.partial(pick_rows, held is not None),
        grid_spec=pltpu.PrefetchScalarGridSpec(
            num_scalar_prefetch=1,
            grid=(1,),
            in_specs=[
                pl.BlockSpec((1, experts, count), lambda i, n: (n[0], 0, 0)),
                pl.BlockSpec((1, count, lanes), lambda i, n: (n[0], 0, 0)),
                pl.BlockSpec((width, lanes), lambda i, n: (0, 0)),
                pl.BlockSpec((count, width), lambda i, n: (0, 0)),
                pl.BlockSpec((1, count, width), lambda i, n: (n[0], 0, 0)),
            ]
            + [whole, whole] * (held is not None),
            out_specs=[out, out, pl.BlockSpec((count, experts), lambda i, n: (0, 0))],
        ),
        out_shape=[shape, shape, jax.ShapeDtypeStruct((count, experts), F32)],
        input_output_aliases={} if held is None else {6: 0, 7: 1},
        compiler_params=params(40),
        cost_estimate=cost(
            4 * experts * capacity * count * width, 4 * width * (count + experts * capacity)
        ),
    )(number, slots, named, router, x, grads, *(held or ()))


def merge_rows(blocks, ids_ref, slots_ref, *refs):
    experts = slots_ref.shape[2]
    rows_refs, out_refs = refs[:experts], refs[experts:]
    capacity = rows_refs[0].shape[0]
    count = out_refs[0].shape[0]
    place = lax.broadcasted_iota(jnp.int32, (count, capacity), 1)
    total = None
    for j in range(experts):
        hot = (place == slots_ref[0, :, j : j + 1]).astype(BF)
        rows = dot(hot, rows_refs[j][...])
        total = rows if total is None else total + rows
    for i in range(blocks):

        @pl.when(pl.program_id(0) == i)
        def _(i=i):
            out_refs[i][...] = total.astype(BF)


def merge_results(blocks, ids_ref, slots_ref, grad_ref, *refs):
    experts = slots_ref.shape[2]
    gates_refs, refs = refs[:blocks], refs[blocks:]
    rows_refs, out_refs, dgate_ref = refs[:experts], refs[experts:-1], refs[-1]
    capacity = rows_refs[0].shape[0]
    count = out_refs[0].shape[0]
    place = lax.broadcasted_iota(jnp.int32, (count, capacity), 1)
    grad = grad_ref[0].astype(F32)
    gates = gates_refs[0][...]
    for i in range(1, blocks):
        gates = jnp.where(pl.program_id(0) == i, gates_refs[i][...], gates)
    total = None
    dgates = []
    for j in range(experts):
        hot = (place == slots_ref[0, :, j : j + 1]).astype(BF)
        rows = dot(hot, rows_refs[j][...])
        dgates.append(jnp.sum(rows * grad, axis=1, keepdims=True))
        gated = rows * gates[:, j : j + 1]
        total = gated if total is None else total + gated
    dgate_ref[0] = jnp.concatenate(dgates, axis=1)
    for i in range(blocks):

        @pl.when(pl.program_id(0) == i)
        def _(i=i):
            out_refs[i][...] = total.astype(BF)


def merge(ids, slots, rows, gates=None, grads=None):
    blocks = ids.shape[0]
    count, experts = slots.shape[1:]
    capacity = rows[0].shape[0] // blocks
    width = rows[0].shape[1]
    small = pl.BlockSpec((1, count, experts), lambda b, n: (n[b], 0, 0))
    in_specs = [small]
    operands = [slots]
    out_specs = [pl.BlockSpec((count, width), lambda b, n: (0, 0))] * blocks
    out_shape = [jax.ShapeDtypeStruct((count, width), BF)] * blocks
    if gates is not None:
        in_specs += [pl.BlockSpec((1, count, width), lambda b, n: (n[b], 0, 0))]
        in_specs += [pl.BlockSpec((count, experts), lambda b, n: (0, 0))] * blocks
        operands += [grads] + list(gates)
        out_specs = out_specs + [pl.BlockSpec((1, count, experts), lambda b, n: (b, 0, 0))]
        out_shape = out_shape + [jax.ShapeDtypeStruct((blocks, count, experts), F32)]
    in_specs += [pl.BlockSpec((capacity, width), lambda b, n: (b, 0))] * experts
    return pl.pallas_call(
        functools.partial(merge_rows if gates is None else merge_results, blocks),
        grid_spec=pltpu.PrefetchScalarGridSpec(
            num_scalar_prefetch=1, grid=(blocks,), in_specs=in_specs, out_specs=out_specs
        ),
        out_shape=out_shape,
        compiler_params=params(40),
        cost_estimate=cost(
            2 * blocks * experts * capacity * count * width,
            2 * blocks * width * (2 * count + experts * capacity),
        ),
    )(ids, *operands, *rows)


def expert_body(
    sub,
    x_ref,
    dy_ref,
    wg_ref,
    wu_ref,
    wd_ref,
    y_ref,
    dx_ref,
    h_ref,
    dg_ref,
    du_ref,
    y_acc,
    dx_acc,
):
    f = pl.program_id(0)
    last = pl.num_programs(0) - 1

    def step(i, carry):
        r = pl.ds(pl.multiple_of(i * sub, sub), sub)
        x = x_ref[r, :]
        gate = dot(x, wg_ref[...])
        up = dot(x, wu_ref[...])
        sigmoid = 1.0 / (1.0 + jnp.exp(-gate))
        activated = gate * sigmoid
        hidden = (activated * up).astype(BF)
        h_ref[r, :] = hidden
        grad_hidden = dot_t(dy_ref[r, :], wd_ref[...])
        grad_gate = (grad_hidden * up * sigmoid * (1.0 + gate * (1.0 - sigmoid))).astype(BF)
        grad_up = (grad_hidden * activated).astype(BF)
        dg_ref[r, :] = grad_gate
        du_ref[r, :] = grad_up
        y = dot(hidden, wd_ref[...])
        dx = dot_t(grad_gate, wg_ref[...]) + dot_t(grad_up, wu_ref[...])

        @pl.when(f == 0)
        def _():
            y_acc[r, :] = y
            dx_acc[r, :] = dx

        @pl.when((f > 0) & (f < last))
        def _():
            y_acc[r, :] += y
            dx_acc[r, :] += dx

        @pl.when(f == last)
        def _():
            y_ref[r, :] = (y_acc[r, :] + y).astype(BF)
            dx_ref[r, :] = (dx_acc[r, :] + dx).astype(BF)

        return carry

    lax.fori_loop(0, x_ref.shape[0] // sub, step, 0)


def expert(j, x, dy, w_gate, w_up, w_down):
    _, rows, width = x.shape
    hidden = w_gate.shape[2]
    tile = hidden // 2
    rows_in = pl.BlockSpec((None, rows, width), lambda f: (j, 0, 0))
    rows_out = pl.BlockSpec((rows, width), lambda f: (0, 0))
    part = pl.BlockSpec((rows, tile), lambda f: (0, f))
    wide = jax.ShapeDtypeStruct((rows, width), BF)
    thin = jax.ShapeDtypeStruct((rows, hidden), BF)
    return pl.pallas_call(
        functools.partial(expert_body, rows // 2),
        grid=(2,),
        in_specs=[
            rows_in,
            rows_in,
            pl.BlockSpec((None, width, tile), lambda f: (j, 0, f)),
            pl.BlockSpec((None, width, tile), lambda f: (j, 0, f)),
            pl.BlockSpec((None, tile, width), lambda f: (j, f, 0)),
        ],
        out_specs=[rows_out, rows_out, part, part, part],
        out_shape=[wide, wide, thin, thin, thin],
        scratch_shapes=[pltpu.VMEM((rows, width), F32)] * 2,
        compiler_params=params(58),
        cost_estimate=cost(
            12 * rows * width * hidden,
            8 * rows * width + 6 * rows * hidden + 6 * width * hidden,
            rows * hidden,
        ),
    )(x, dy, w_gate, w_up, w_down)


def weight_grads_body(groups, count, *refs):
    left, rights, outs = refs[:groups], refs[groups : groups + groups * count], refs[-count:]
    for n in range(count):
        total = None
        for g in range(groups):
            part = t_dot(left[g][...], rights[n * groups + g][...])
            total = part if total is None else total + part
        outs[n][...] = total.astype(BF)


def weight_grads(lefts, rights, left_index, right_index):
    groups, count = len(lefts), len(rights)

    def tiled(array, index, tile):
        if array.ndim == 3:
            return pl.BlockSpec((None, array.shape[1], tile), lambda d: (index, 0, d))
        return pl.BlockSpec((array.shape[0], tile), lambda d: (0, d))

    def fixed(array, index):
        if array.ndim == 3:
            return pl.BlockSpec((None,) + array.shape[1:], lambda d: (index, 0, 0))
        return pl.BlockSpec(array.shape, lambda d: (0, 0))

    tall = lefts[0].shape[-1]
    wide = rights[0][0].shape[-1]
    tile = 256
    flat = [r for one in rights for r in one]
    total_rows = sum(a.shape[-2] for a in lefts)
    return pl.pallas_call(
        functools.partial(weight_grads_body, groups, count),
        grid=(tall // tile,),
        in_specs=[tiled(a, left_index, tile) for a in lefts] + [fixed(a, right_index) for a in flat],
        out_specs=[pl.BlockSpec((tile, wide), lambda d: (d, 0))] * count,
        out_shape=[jax.ShapeDtypeStruct((tall, wide), BF)] * count,
        compiler_params=params(48),
        cost_estimate=cost(
            2 * count * total_rows * tall * wide,
            2 * total_rows * (tall + count * wide) + 2 * count * tall * wide,
        ),
    )(*lefts, *flat)


def swap_core(value):
    return lax.ppermute(value, "shard", [(i, i ^ 1) for i in range(4)])


def swap_x(value):
    return lax.ppermute(value, "shard", [(i, i ^ 2) for i in range(4)])


def shard_order(position):
    return [position, position ^ 1, position ^ 2, position ^ 3]


def shard_gather(value):
    far = swap_x(value)
    near = swap_core(value)
    return [value, near, far, swap_core(far)]


def shard_reduce(blocks):
    far = blocks[2].astype(F32) + swap_core(blocks[3].astype(BF)).astype(F32)
    far = swap_x(far.astype(BF))
    near = blocks[0].astype(F32) + swap_core(blocks[1].astype(BF)).astype(F32)
    return near + far.astype(F32)


def ring_next(count):
    return [(z * 2 + y, ((z + 1) % (count // 2)) * 2 + y) for z in range(count // 2) for y in range(2)]


def swap_y(value, count):
    return lax.ppermute(value, "rep", [(i, i ^ 1) for i in range(count)])


def turn_z(value, count):
    return lax.ppermute(value, "rep", ring_next(count))


def rep_order(rep, count):
    planes = count // 2
    z, y = rep // 2, rep % 2
    return [((z + planes - k) % planes) * 2 + (y ^ w) for k in range(planes) for w in range(2)]


def rep_gather(value, count):
    blocks = []
    held = value
    for k in range(count // 2):
        if k > 0:
            held = turn_z(held, count)
        blocks += [held, swap_y(held, count)]
    return blocks


def rep_reduce(blocks, count):
    planes = count // 2

    def pair(k):
        return blocks[2 * k].astype(F32) + swap_y(blocks[2 * k + 1].astype(BF), count).astype(F32)

    total = pair(1)
    for k in list(range(2, planes)) + [0]:
        total = turn_z(total.astype(BF), count).astype(F32) + pair(k)
    return total


def write_sums_body(blocks, shards, ids_ref, wq_ref, wk_ref, wv_ref, gain_ref, *refs):
    in_refs, (q_ref, k_ref, v_ref, o_ref, extra_ref) = refs[:blocks], refs[blocks:]
    width = q_ref.shape[1]
    heads = width // HD
    for i in range(blocks):

        @pl.when(pl.program_id(0) == i)
        def _(i=i):
            ref = in_refs[i]
            attn = None
            for m, (out, weight) in enumerate(((q_ref, wq_ref), (k_ref, wk_ref), (v_ref, wv_ref))):
                for h in range(heads):
                    start = (3 * h + m) * HD
                    piece = ref[:, start : start + HD].astype(F32)
                    out[:, h * HD : (h + 1) * HD] = piece
                    term = piece * weight[:, h * HD : (h + 1) * HD].astype(F32)
                    attn = term if attn is None else attn + term
            o_ref[...] = ref[:, 3 * width : 4 * width].astype(F32)
            extra = ref[:, 4 * width :].astype(F32)
            attn = jnp.sum(attn, axis=1, keepdims=True) / gain_ref[...]
            lane = lax.broadcasted_iota(jnp.int32, extra.shape, 1)
            extra_ref[...] = jnp.where(lane == extra.shape[1] - 1, attn, extra)


def write_sums(ids, w_query, w_key, w_value, gain, gathered, shards):
    blocks = len(gathered)
    part, total = gathered[0].shape
    rows, width = w_query.shape
    own = pl.BlockSpec((part, width), lambda b, n: (n[b], 0))
    extra = pl.BlockSpec((part, HD), lambda b, n: (n[b], 0))
    big = jax.ShapeDtypeStruct((rows, width), F32)
    return pl.pallas_call(
        functools.partial(write_sums_body, blocks, shards),
        grid_spec=pltpu.PrefetchScalarGridSpec(
            num_scalar_prefetch=1,
            grid=(blocks,),
            in_specs=[own, own, own, pl.BlockSpec((part, 1), lambda b, n: (n[b], 0))]
            + [pl.BlockSpec((part, total), lambda b, n: (0, 0))] * blocks,
            out_specs=[own, own, own, own, extra],
        ),
        out_shape=[big, big, big, big, jax.ShapeDtypeStruct((rows, HD), F32)],
        compiler_params=params(52),
        cost_estimate=cost(0, rows * width * 30),
    )(ids, w_query, w_key, w_value, gain, *gathered)


def on_device(
    tokens,
    w_query,
    w_key,
    w_value,
    w_out,
    w_router,
    norm_attn,
    norm_ffn,
    norm_query,
    norm_key,
    w_gate,
    w_up,
    w_down,
    segments,
    routes,
    cotangent,
):
    rows_count, width = tokens.shape
    experts = w_router.shape[1]
    local_experts = w_gate.shape[0]
    rep_count = lax.axis_size("rep")
    shard_count = lax.axis_size("shard")
    position = lax.axis_index("shard")
    rep = lax.axis_index("rep")
    length = rows_count * shard_count
    capacity = max(2, rows_count * TOP * 9 // (8 * experts))
    capacity = -(-capacity // 16) * 16
    rows = w_query.shape[0]
    order = rep_order(rep, rep_count)
    order_in = shard_order(position)
    group_size = 4
    groups = [list(range(s, s + group_size)) for s in range(0, rep_count, group_size)]

    token_blocks = shard_gather(tokens)
    packed = packed_columns(w_query, w_key, w_value, shard_count)
    columns = lax.all_to_all(packed, "shard", split_axis=0, concat_axis=0, tiled=True)
    columns = columns.reshape(width, -1)
    routes_b = jnp.pad(routes.astype(BF), ((0, 0), (0, HD - TOP)))
    grads = lax.all_gather(jnp.concatenate([cotangent, routes_b], axis=1), "rep", axis=0, tiled=False)

    small = jnp.concatenate(
        [
            w_router,
            norm_attn[:, None],
            norm_ffn[:, None],
            jnp.pad(norm_query, (0, rows - norm_query.shape[0]))[:, None],
            jnp.pad(norm_key, (0, rows - norm_key.shape[0]))[:, None],
        ],
        axis=1,
    )
    small = jnp.pad(small, ((0, 0), (0, HD - small.shape[1])))
    small = jnp.stack(shard_gather(small))
    order_in_array = jnp.stack(order_in)
    small = jnp.zeros_like(small).at[order_in_array].set(small)
    head_gains = small[:, : norm_query.shape[0], experts + 2 : experts + 4].astype(F32)
    gain_query = head_gains[:, :, 0].reshape(1, HD)
    gain_key = head_gains[:, :, 1].reshape(1, HD)
    small = small.reshape(width, HD)
    gain_attn = small[:, experts].astype(F32)
    gain_ffn = small[:, experts + 1].astype(F32)
    full_router = small[:, :experts]

    full_gate = lax.all_gather(after(w_gate, columns), "shard", axis=1, tiled=True)
    full_up = lax.all_gather(after(w_up, columns), "shard", axis=1, tiled=True)
    full_down = lax.all_gather(after(w_down, columns), "shard", axis=1, tiled=True)

    expert_ids = jnp.arange(experts, dtype=jnp.int32)
    named_all = jnp.any(
        grads[:, :, width : width + TOP].astype(jnp.int32)[:, :, :, None] == expert_ids, axis=2
    )
    first_expert = rep * local_experts
    named_mine = lax.dynamic_slice_in_dim(named_all, first_expert, local_experts, axis=2)
    before = jnp.tril(jnp.ones((rows_count, rows_count), BF), -1)
    slot_mine = jnp.einsum("ts,bsj->btj", before, named_mine.astype(BF), preferred_element_type=F32)
    slot_tokens = jnp.where(named_mine, slot_mine.astype(jnp.int32), -1)
    slot_lanes = jnp.swapaxes(slot_tokens, 1, 2)
    named_lanes = jnp.pad(named_all.astype(F32), ((0, 0), (0, 0), (0, HD - experts)))

    tokens_all = jnp.concatenate(token_blocks, axis=0).astype(F32)
    input_b = (tokens_all * rms_scale(tokens_all) * gain_attn).astype(BF)
    qkv = dot(input_b, columns)
    places = jnp.concatenate([p * rows_count + jnp.arange(rows_count, dtype=jnp.int32) for p in order_in])
    inverse = THETA ** (-jnp.arange(HD // 2, dtype=F32) * 2.0 / HD)
    angles = places.astype(F32)[:, None] * inverse[None, :]
    cosine, sine = jnp.cos(angles), jnp.sin(angles)
    cosine = jnp.concatenate([cosine, cosine], axis=-1)
    sine = jnp.concatenate([-sine, sine], axis=-1)
    segment_all = jnp.concatenate(
        [lax.dynamic_slice_in_dim(segments[0], p * rows_count, rows_count) for p in order_in]
    )
    attn_args = (cosine, sine, gain_query, gain_key, segment_all[:, None], segment_all[None, :])
    mixed_b = attention_forward(qkv, attn_args)
    projected = dot(mixed_b, w_out).astype(BF)
    projected = [projected[i * rows_count : (i + 1) * rows_count] for i in range(shard_count)]
    tokens_f = tokens.astype(F32)
    hidden_state = tokens_f + shard_reduce(projected)

    scale_mid = rms_scale(hidden_state)
    normed_mid = hidden_state * scale_mid
    mid_b = (normed_mid * gain_ffn).astype(BF)
    mid_blocks = rep_gather(mid_b, rep_count)
    router_lanes = jnp.pad(full_router, ((0, 0), (0, HD - experts)))
    expert_rows, grad_rows, kept, result_parts, grad_parts, dgate_parts = [], [], [], [], [], []
    for group in groups:
        held, gates = None, []
        for place, b in enumerate(group):
            number = jnp.stack([order[b], first_expert, jnp.int32(experts)])
            x, dy, gate = pick(
                number,
                slot_lanes,
                named_lanes,
                router_lanes,
                mid_blocks[b],
                grads,
                held,
                place,
                len(group),
                capacity,
            )
            held = (x, dy)
            gates.append(gate)
        x, dy = [a.reshape(local_experts, len(group) * capacity, width) for a in held]
        done = [expert(j, x, dy, full_gate, full_up, full_down) for j in range(local_experts)]
        ids = jnp.stack([order[b] for b in group])
        grad_parts += merge(ids, slot_tokens, [d[1] for d in done])
        *parts, dgate = merge(ids, slot_tokens, [d[0] for d in done], gates, grads)
        result_parts += parts
        dgate_parts.append(dgate)
        expert_rows.append(x)
        grad_rows.append(dy)
        kept.append(done)
    grad_mid_moe = rep_reduce(grad_parts, rep_count)
    expert_sum = rep_reduce(result_parts, rep_count)
    output = (hidden_state + expert_sum).astype(BF)

    def owned_part(grad):
        return lax.psum_scatter(grad, "shard", scatter_dimension=0, tiled=True)

    sums_gate, sums_up, sums_down = [], [], []
    for j in range(local_experts):
        down, = weight_grads([k[j][2] for k in kept], [grad_rows], None, j)
        gate, up = weight_grads(
            expert_rows, [[k[j][3] for k in kept], [k[j][4] for k in kept]], j, None
        )
        sums_down.append(owned_part(down))
        sums_gate.append(owned_part(gate))
        sums_up.append(owned_part(up))
    grad_gate = jnp.stack(sums_gate).astype(F32)
    grad_up = jnp.stack(sums_up).astype(F32)
    grad_down = jnp.stack(sums_down).astype(F32)

    order_array = jnp.stack(order)
    dgates = jnp.swapaxes(jnp.concatenate(dgate_parts), 1, 2)
    dgates = jnp.zeros_like(dgates).at[order_array].set(dgates)
    dgates = lax.all_to_all(dgates, "rep", split_axis=0, concat_axis=0, tiled=True)
    dgates = dgates.reshape(experts, rows_count).T
    named_own = jnp.any(routes[:, :, None] == expert_ids, axis=1)
    logits = dot(mid_b, full_router)
    exps = jnp.exp(logits - jnp.max(logits, axis=-1, keepdims=True))
    probs_own = exps / jnp.sum(exps, axis=-1, keepdims=True)
    chosen_total = jnp.sum(jnp.where(named_own, probs_own, 0.0), axis=1, keepdims=True)
    gates_own = jnp.where(named_own, probs_own, 0.0) / chosen_total
    grad_probs = jnp.where(
        named_own, dgates - jnp.sum(dgates * gates_own, axis=1, keepdims=True), 0.0
    ) / chosen_total
    grad_logits = (
        probs_own * (grad_probs - jnp.sum(probs_own * grad_probs, axis=1, keepdims=True))
    ).astype(BF)
    grad_mid = grad_mid_moe + dot_t(grad_logits, full_router)
    grad_gain_ffn = jnp.sum(grad_mid * normed_mid, axis=0)
    grad_router = t_dot(mid_b, grad_logits)
    grad_out = cotangent.astype(F32)
    grad_state = grad_out + norm_back(grad_mid * gain_ffn, normed_mid, scale_mid)
    grad_state_b = grad_state.astype(BF)

    grad_state_all = jnp.concatenate(shard_gather(grad_state_b), axis=0)
    grad_mixed = dot_t(grad_state_all, w_out).astype(BF)
    grad_out_proj = t_dot(mixed_b, grad_state_all).astype(BF)
    grad_qkv, grad_head_gains = attention_backward(qkv, grad_mixed, attn_args)
    grad_columns = t_dot(input_b, grad_qkv).astype(BF)
    grad_input = dot_t(grad_qkv, columns).astype(BF)
    grad_input = shard_reduce(
        [grad_input[i * rows_count : (i + 1) * rows_count] for i in range(shard_count)]
    )
    normed_in = tokens_f * rms_scale(tokens_f)
    tokens_grad = (
        grad_state + norm_back(grad_input * gain_attn, normed_in, rms_scale(tokens_f))
    ).astype(BF)

    part = rows // rep_count
    piece = HD // shard_count
    head_columns = jnp.pad(
        grad_head_gains[:2].reshape(2, shard_count, piece), ((0, 0), (0, 0), (0, rows - piece))
    ).reshape(2, width)
    extras = jnp.concatenate(
        [grad_router, grad_gain_ffn[:, None], head_columns.T], axis=1
    )
    extras = jnp.pad(extras, ((0, 0), (0, HD - extras.shape[1]))).astype(BF)
    out_columns = jnp.swapaxes(grad_out_proj.reshape(rows, shard_count, -1), 0, 1)
    out_columns = out_columns.reshape(shard_count, rep_count, part, -1)
    column_parts = grad_columns.reshape(shard_count, rep_count, part, -1)
    extra_parts = extras.reshape(shard_count, rep_count, part, -1)
    to_sum = jnp.concatenate([column_parts, extra_parts, out_columns], axis=3)
    to_sum = [lax.dynamic_index_in_dim(to_sum, r, axis=1, keepdims=False) for r in order]
    part_sum = rep_reduce(to_sum, rep_count).astype(BF)
    split = grad_columns.shape[1] + HD
    mine = lax.all_to_all(part_sum[:, :, :split], "shard", split_axis=0, concat_axis=0, tiled=True)
    wide = jnp.swapaxes(mine[:, :, : split - HD], 0, 1).reshape(part, -1)
    extra = jnp.sum(mine[:, :, split - HD :].astype(F32), axis=0).astype(BF)
    out_part = jnp.swapaxes(part_sum[:, :, split:], 0, 1).reshape(part, -1)
    gathered = rep_gather(jnp.concatenate([wide, out_part, extra], axis=1), rep_count)
    sum_query, sum_key, sum_value, sum_out, extra = write_sums(
        order_array,
        w_query,
        w_key,
        w_value,
        norm_attn.astype(F32)[:, None],
        gathered,
        shard_count,
    )
    return (
        output,
        tokens_grad,
        sum_query,
        sum_key,
        sum_value,
        sum_out,
        extra[:, :experts],
        extra[:, HD - 1],
        extra[:, experts],
        extra[:piece, experts + 1],
        extra[:piece, experts + 2],
        grad_gate,
        grad_up,
        grad_down,
    )


def solution(mesh):
    return jax.shard_map(
        on_device,
        mesh=mesh,
        in_specs=(
            P(("rep", "shard"), None),
            P("shard", None),
            P("shard", None),
            P("shard", None),
            P("shard", None),
            P("shard", None),
            P("shard"),
            P("shard"),
            P("shard"),
            P("shard"),
            P("rep", "shard", None),
            P("rep", "shard", None),
            P("rep", "shard", None),
            P("rep", None),
            P(("rep", "shard"), None),
            P(("rep", "shard"), None),
        ),
        out_specs=(
            P(("rep", "shard"), None),
            P(("rep", "shard"), None),
            P("shard", None),
            P("shard", None),
            P("shard", None),
            P("shard", None),
            P("shard", None),
            P("shard"),
            P("shard"),
            P("shard"),
            P("shard"),
            P("rep", "shard", None),
            P("rep", "shard", None),
            P("rep", "shard", None),
        ),
        check_vma=False,
    )
```

```python
import functools

import jax
import jax.numpy as jnp
from jax import lax
from jax.experimental import pallas as pl
from jax.experimental.pallas import tpu as pltpu
from jax.sharding import PartitionSpec as P

HEADS = 16
HD = 128
TOP = 8

EPSILON = 1e-05
THETA = 50000.0
MASKED = -1e30
BF = jnp.bfloat16
F32 = jnp.float32
QCHUNK = 256
VMEM = 58 << 20


def rms_scale(values):
    return lax.rsqrt(jnp.mean(values * values, axis=-1, keepdims=True) + EPSILON)


def norm_back(grad, normed, scale):
    return scale * (grad - normed * jnp.mean(grad * normed, axis=-1, keepdims=True))


def dot(left, right):
    return jnp.dot(left, right, preferred_element_type=F32)


def dot_t(left, right):
    return lax.dot_general(left, right, (((1,), (1,)), ((), ())), preferred_element_type=F32)


def t_dot(left, right):
    return lax.dot_general(left, right, (((0,), (0,)), ((), ())), preferred_element_type=F32)


def params(mib=40):
    return pltpu.CompilerParams(vmem_limit_bytes=mib << 20)


def cost(flops, size, transcendentals=0):
    return pl.CostEstimate(
        flops=int(flops), bytes_accessed=int(size), transcendentals=int(transcendentals)
    )


def after(value, *others):
    return lax.optimization_barrier((value,) + others)[0]


def together(*values):
    return lax.optimization_barrier(values)


def pack_columns(q_ref, k_ref, v_ref, out_ref):
    for h in range(q_ref.shape[1] // HD):
        for m, ref in enumerate((q_ref, k_ref, v_ref)):
            start = (3 * h + m) * HD
            out_ref[0, :, start : start + HD] = ref[:, h * HD : (h + 1) * HD]


def packed_columns(w_query, w_key, w_value, shards):
    rows, width = w_query.shape
    part = width // shards
    spec = pl.BlockSpec((rows, part), lambda s: (0, s))
    return pl.pallas_call(
        pack_columns,
        grid=(shards,),
        in_specs=[spec, spec, spec],
        out_specs=pl.BlockSpec((1, rows, 3 * part), lambda s: (s, 0, 0)),
        out_shape=jax.ShapeDtypeStruct((shards, rows, 3 * part), BF),
        compiler_params=params(),
        cost_estimate=cost(0, 12 * rows * width),
    )(w_query, w_key, w_value)


def pack_part(place_ref, q_ref, k_ref, v_ref, out_ref):
    pack_columns(q_ref, k_ref, v_ref, out_ref)


def packed_part(place, w_query, w_key, w_value, shards, part):
    width = w_query.shape[1] // shards
    spec = pl.BlockSpec((part, width), lambda s, n: (n[0], 2 * n[1] + s))
    return pl.pallas_call(
        pack_part,
        grid_spec=pltpu.PrefetchScalarGridSpec(
            num_scalar_prefetch=1,
            grid=(2,),
            in_specs=[spec, spec, spec],
            out_specs=pl.BlockSpec((1, part, 3 * width), lambda s, n: (s, 0, 0)),
        ),
        out_shape=jax.ShapeDtypeStruct((2, part, 3 * width), BF),
        compiler_params=params(),
        cost_estimate=cost(0, 24 * part * width),
    )(place, w_query, w_key, w_value)


def project_body(parts, order_ref, shard_ref, gain_ref, packed_ref, near_ref, *refs):
    token_refs, far_refs = refs[:4], refs[4 : 4 + parts]
    input_ref, columns_ref, qkv_ref, sem = refs[4 + parts :]
    rows = near_ref.shape[0]
    count = token_refs[0].shape[0]
    part = rows // parts

    def place(start, size):
        return columns_ref.at[pl.ds(pl.multiple_of(start, 16), size)]

    copies = [
        pltpu.make_async_copy(packed_ref.at[shard_ref[0]], place(shard_ref[0] * rows, rows), sem.at[0]),
        pltpu.make_async_copy(near_ref, place(shard_ref[1] * rows, rows), sem.at[1]),
    ]
    for i in range(parts):
        for m in range(2):
            start = shard_ref[2 + m] * rows + order_ref[i] * part
            copies.append(
                pltpu.make_async_copy(
                    far_refs[i].at[m, pl.ds(0, part)], place(start, part), sem.at[2 + 2 * i + m]
                )
            )
    for copy in copies:
        copy.start()
    for i in range(4):
        x = token_refs[i][...].astype(F32)
        input_ref[i * count : (i + 1) * count, :] = (x * rms_scale(x) * gain_ref[...]).astype(BF)
    for copy in copies:
        copy.wait()

    def step(i, carry):
        r = pl.ds(pl.multiple_of(i * count, count), count)
        qkv_ref[r, :] = dot(input_ref[r, :], columns_ref[...])
        return carry

    lax.fori_loop(0, 4, step, 0)


def project(order, shards, gain, packed, near, token_blocks, fars):
    count, width = token_blocks[0].shape
    columns = near.shape[1]
    length = count * len(token_blocks)
    anywhere = pl.BlockSpec(memory_space=pl.ANY)
    whole = lambda *shape: pl.BlockSpec(shape, lambda i, a, b: (0, 0))
    return pl.pallas_call(
        functools.partial(project_body, len(fars)),
        grid_spec=pltpu.PrefetchScalarGridSpec(
            num_scalar_prefetch=2,
            grid=(1,),
            in_specs=[whole(1, width), anywhere, anywhere]
            + [whole(count, width)] * 4
            + [anywhere] * len(fars),
            out_specs=[whole(length, width), whole(width, columns), whole(length, columns)],
            scratch_shapes=[pltpu.SemaphoreType.DMA((2 + 2 * len(fars),))],
        ),
        out_shape=[
            jax.ShapeDtypeStruct((length, width), BF),
            jax.ShapeDtypeStruct((width, columns), BF),
            jax.ShapeDtypeStruct((length, columns), F32),
        ],
        compiler_params=params(56),
        cost_estimate=cost(
            2 * length * width * columns, 4 * length * width + 4 * width * columns + 4 * length * columns
        ),
    )(order, shards, gain, packed, near, *token_blocks, *fars)


def turned(values, cosine, sine):
    return values * cosine + pltpu.roll(values, HD // 2, 1) * sine


def turned_back(grad, cosine, sine):
    return grad * cosine - pltpu.roll(grad, HD // 2, 1) * sine


def weights_of(qb, keys, seg_column, seg_row):
    scores = dot_t(qb, keys) * (HD**-0.5)
    scores = jnp.where(seg_column == seg_row, scores, MASKED)
    shifted = jnp.exp(scores - jnp.max(scores, axis=-1, keepdims=True))
    return shifted * (1.0 / jnp.sum(shifted, axis=-1, keepdims=True))


def attend_forward(qkv_ref, cos_ref, sin_ref, gq_ref, gk_ref, segc_ref, segr_ref, o_ref, kb_ref, vb_ref):
    length = qkv_ref.shape[0]
    k_raw = qkv_ref[:, HD : 2 * HD]
    kb_ref[...] = turned(k_raw * rms_scale(k_raw) * gk_ref[...], cos_ref[...], sin_ref[...]).astype(BF)
    vb_ref[...] = qkv_ref[:, 2 * HD :].astype(BF)

    def step(i, carry):
        rows = pl.ds(pl.multiple_of(i * QCHUNK, QCHUNK), QCHUNK)
        q_raw = qkv_ref[rows, :HD]
        qb = turned(q_raw * rms_scale(q_raw) * gq_ref[...], cos_ref[rows, :], sin_ref[rows, :]).astype(BF)
        probs = weights_of(qb, kb_ref[...], segc_ref[rows, :], segr_ref[...])
        o_ref[rows, :] = dot(probs.astype(BF), vb_ref[...]).astype(BF)
        return carry

    lax.fori_loop(0, length // QCHUNK, step, 0)


def attend_backward(
    qkv_ref,
    do_ref,
    cos_ref,
    sin_ref,
    gq_ref,
    gk_ref,
    segc_ref,
    segr_ref,
    *refs,
):
    grad_ref, gains_ref, kb_ref, vb_ref, dk_acc, dv_acc = refs[-6:]
    length = qkv_ref.shape[0]
    scale = HD**-0.5

    @pl.when(pl.program_id(0) == 0)
    def _():
        gains_ref[...] = jnp.zeros_like(gains_ref)

    k_raw = qkv_ref[:, HD : 2 * HD]
    kb_ref[...] = turned(k_raw * rms_scale(k_raw) * gk_ref[...], cos_ref[...], sin_ref[...]).astype(BF)
    vb_ref[...] = qkv_ref[:, 2 * HD :].astype(BF)
    dk_acc[...] = jnp.zeros_like(dk_acc)
    dv_acc[...] = jnp.zeros_like(dv_acc)

    def step(i, carry):
        rows = pl.ds(pl.multiple_of(i * QCHUNK, QCHUNK), QCHUNK)
        cosine, sine = cos_ref[rows, :], sin_ref[rows, :]
        q_raw = qkv_ref[rows, :HD]
        q_scale = rms_scale(q_raw)
        q_norm = q_raw * q_scale
        qb = turned(q_norm * gq_ref[...], cosine, sine).astype(BF)
        probs = weights_of(qb, kb_ref[...], segc_ref[rows, :], segr_ref[...])
        grad_o = do_ref[rows, :]
        grad_probs = dot_t(grad_o, vb_ref[...])
        dv_acc[...] += t_dot(probs.astype(BF), grad_o)
        weighted = probs * grad_probs
        grad_scores = (weighted - probs * jnp.sum(weighted, axis=-1, keepdims=True)).astype(BF)
        dk_acc[...] += t_dot(grad_scores, qb)
        eq = turned_back(dot(grad_scores, kb_ref[...]) * scale, cosine, sine)
        gains_ref[0:1, :] += jnp.sum(eq * q_norm, axis=0, keepdims=True)
        grad_ref[rows, :HD] = norm_back(eq * gq_ref[...], q_norm, q_scale).astype(BF)
        return carry

    lax.fori_loop(0, length // QCHUNK, step, 0)
    ek = turned_back(dk_acc[...] * scale, cos_ref[...], sin_ref[...])
    k_raw = qkv_ref[:, HD : 2 * HD]
    k_scale = rms_scale(k_raw)
    k_norm = k_raw * k_scale
    gains_ref[1:2, :] += jnp.sum(ek * k_norm, axis=0, keepdims=True)
    grad_ref[:, HD : 2 * HD] = norm_back(ek * gk_ref[...], k_norm, k_scale).astype(BF)
    grad_ref[:, 2 * HD :] = dv_acc[...].astype(BF)


def attention_specs(length):
    table = pl.BlockSpec((length, HD), lambda h: (0, 0))
    gain = pl.BlockSpec((1, HD), lambda h: (0, 0))
    column = pl.BlockSpec((length, 1), lambda h: (0, 0))
    row = pl.BlockSpec((1, length), lambda h: (0, 0))
    return [table, table, gain, gain, column, row]


def attention_forward(qkv, attn_args):
    length = qkv.shape[0]
    heads = qkv.shape[1] // (3 * HD)
    return pl.pallas_call(
        attend_forward,
        grid=(heads,),
        in_specs=[pl.BlockSpec((length, 3 * HD), lambda h: (0, h))] + attention_specs(length),
        out_specs=pl.BlockSpec((length, HD), lambda h: (0, h)),
        out_shape=jax.ShapeDtypeStruct((length, heads * HD), BF),
        scratch_shapes=[pltpu.VMEM((length, HD), BF)] * 2,
        compiler_params=params(),
        cost_estimate=cost(16 * heads * length * length * HD, qkv.size * 5, heads * length * length),
    )(qkv, *attn_args)


def attention_backward(qkv, grad_o, attn_args, first, heads, held=None):
    length = qkv.shape[0]
    wide = pl.BlockSpec((length, 3 * HD), lambda h: (0, first + h))
    return pl.pallas_call(
        attend_backward,
        grid=(heads,),
        in_specs=[wide, pl.BlockSpec((length, HD), lambda h: (0, first + h))]
        + attention_specs(length)
        + [pl.BlockSpec(memory_space=pl.ANY)] * (held is not None),
        out_specs=[wide, pl.BlockSpec((8, HD), lambda h: (0, 0))],
        out_shape=[
            jax.ShapeDtypeStruct(qkv.shape, BF),
            jax.ShapeDtypeStruct((8, HD), F32),
        ],
        scratch_shapes=[pltpu.VMEM((length, HD), BF)] * 2 + [pltpu.VMEM((length, HD), F32)] * 2,
        input_output_aliases={} if held is None else {8: 0},
        compiler_params=params(48),
        cost_estimate=cost(40 * heads * length * length * HD, qkv.size * 3, heads * length * length),
    )(qkv, grad_o, *attn_args, *(() if held is None else (held,)))


def pick_rows(has_input, number_ref, slots_ref, named_ref, router_ref, x_ref, grad_ref, *refs):
    rows_ref, grad_rows_ref, gates_ref = refs[2 * has_input :]
    experts, capacity = slots_ref.shape[1], rows_ref.shape[2]
    count = x_ref.shape[0]
    x = x_ref[...]
    logits = dot(x, router_ref[...])
    lane = lax.broadcasted_iota(jnp.int32, logits.shape, 1)
    logits = jnp.where(lane < number_ref[1], logits, MASKED)
    exps = jnp.exp(logits - jnp.max(logits, axis=-1, keepdims=True))
    probs = exps / jnp.sum(exps, axis=-1, keepdims=True)
    chosen = jnp.where(named_ref[0] > 0.0, probs, 0.0)
    gates = chosen / jnp.sum(chosen, axis=-1, keepdims=True)
    grad = grad_ref[...].astype(F32)
    wanted = lax.broadcasted_iota(jnp.int32, (capacity, count), 0)
    columns = []
    for j in range(experts):
        gate = jnp.sum(jnp.where(lane == number_ref[0] + j, gates, 0.0), axis=1, keepdims=True)
        hot = (wanted == slots_ref[0, j : j + 1, :]).astype(BF)
        rows_ref[j, 0] = dot(hot, x).astype(BF)
        grad_rows_ref[j, 0] = dot(hot, (grad * gate).astype(BF)).astype(BF)
        columns.append(gate)
    gates_ref[...] = jnp.concatenate(columns, axis=1)


def pick(number, slots, named, router, x, grad, held, block, place, blocks, capacity):
    count, width = x.shape
    experts = slots.shape[1]
    lanes = router.shape[1]
    shape = jax.ShapeDtypeStruct((experts, blocks, capacity, width), BF)
    whole = pl.BlockSpec(memory_space=pl.ANY)
    out = pl.BlockSpec((experts, 1, capacity, width), lambda i, n: (0, place, 0, 0))
    return pl.pallas_call(
        functools.partial(pick_rows, held is not None),
        grid_spec=pltpu.PrefetchScalarGridSpec(
            num_scalar_prefetch=1,
            grid=(1,),
            in_specs=[
                pl.BlockSpec((1, experts, count), lambda i, n: (block, 0, 0)),
                pl.BlockSpec((1, count, lanes), lambda i, n: (block, 0, 0)),
                pl.BlockSpec((width, lanes), lambda i, n: (0, 0)),
                pl.BlockSpec((count, width), lambda i, n: (0, 0)),
                pl.BlockSpec((count, width), lambda i, n: (0, 0)),
            ]
            + [whole, whole] * (held is not None),
            out_specs=[out, out, pl.BlockSpec((count, experts), lambda i, n: (0, 0))],
        ),
        out_shape=[shape, shape, jax.ShapeDtypeStruct((count, experts), F32)],
        input_output_aliases={} if held is None else {6: 0, 7: 1},
        compiler_params=params(58),
        cost_estimate=cost(
            4 * experts * capacity * count * width, 4 * width * (count + experts * capacity)
        ),
    )(number, slots, named, router, x, grad, *(held or ()))


def merge_rows_body(blocks, slots_ref, *refs):
    experts = slots_ref.shape[2]
    rows_refs, out_refs = refs[:experts], refs[experts:]
    capacity = rows_refs[0].shape[0]
    count = out_refs[0].shape[0]
    place = lax.broadcasted_iota(jnp.int32, (count, capacity), 1)
    total = None
    for j in range(experts):
        hot = (place == slots_ref[0, :, j : j + 1]).astype(BF)
        rows = dot(hot, rows_refs[j][...])
        total = rows if total is None else total + rows
    for i in range(blocks):

        @pl.when(pl.program_id(0) == i)
        def _(i=i):
            out_refs[i][...] = total.astype(BF)


def merge_rows(slots, first, rows, blocks):
    count, experts = slots.shape[1:]
    capacity = rows[0].shape[0] // blocks
    width = rows[0].shape[1]
    return pl.pallas_call(
        functools.partial(merge_rows_body, blocks),
        grid=(blocks,),
        in_specs=[pl.BlockSpec((1, count, experts), lambda b: (first + b, 0, 0))]
        + [pl.BlockSpec((capacity, width), lambda b: (b, 0))] * experts,
        out_specs=[pl.BlockSpec((count, width), lambda b: (0, 0))] * blocks,
        out_shape=[jax.ShapeDtypeStruct((count, width), BF)] * blocks,
        compiler_params=params(),
        cost_estimate=cost(
            2 * blocks * experts * capacity * count * width,
            2 * blocks * width * (count + experts * capacity),
        ),
    )(slots, *rows)


def merge_results_body(blocks, slots_ref, *refs):
    experts = slots_ref.shape[2]
    gates_refs, grad_refs, refs = refs[:blocks], refs[blocks : 2 * blocks], refs[2 * blocks :]
    rows_refs, out_refs, dgate_ref = refs[:experts], refs[experts:-1], refs[-1]
    capacity = rows_refs[0].shape[0]
    count = out_refs[0].shape[0]
    place = lax.broadcasted_iota(jnp.int32, (count, capacity), 1)
    for i in range(blocks):

        @pl.when(pl.program_id(0) == i)
        def _(i=i):
            grad = grad_refs[i][...].astype(F32)
            total = None
            dgates = []
            for j in range(experts):
                hot = (place == slots_ref[0, :, j : j + 1]).astype(BF)
                rows = dot(hot, rows_refs[j][...])
                dgates.append(jnp.sum(rows * grad, axis=1, keepdims=True))
                gated = rows * gates_refs[i][:, j : j + 1]
                total = gated if total is None else total + gated
            out_refs[i][...] = total.astype(BF)
            dgate_ref[0] = jnp.concatenate(dgates, axis=1)


def merge_results(slots, first, gates, grads, rows):
    blocks = len(gates)
    count, experts = slots.shape[1:]
    capacity = rows[0].shape[0] // blocks
    width = rows[0].shape[1]
    tokens = pl.BlockSpec((count, width), lambda b: (0, 0))
    return pl.pallas_call(
        functools.partial(merge_results_body, blocks),
        grid=(blocks,),
        in_specs=[pl.BlockSpec((1, count, experts), lambda b: (first + b, 0, 0))]
        + [pl.BlockSpec((count, experts), lambda b: (0, 0))] * blocks
        + [tokens] * blocks
        + [pl.BlockSpec((capacity, width), lambda b: (b, 0))] * experts,
        out_specs=[tokens] * blocks + [pl.BlockSpec((1, count, experts), lambda b: (b, 0, 0))],
        out_shape=[jax.ShapeDtypeStruct((count, width), BF)] * blocks
        + [jax.ShapeDtypeStruct((blocks, count, experts), F32)],
        compiler_params=params(),
        cost_estimate=cost(
            2 * blocks * experts * capacity * count * width,
            2 * blocks * width * (2 * count + experts * capacity),
        ),
    )(slots, *gates, *grads, *rows)


def expert_body(
    sub,
    x_ref,
    dy_ref,
    wg_ref,
    wu_ref,
    wd_ref,
    y_ref,
    dx_ref,
    h_ref,
    dg_ref,
    du_ref,
    y_acc,
    dx_acc,
):
    f = pl.program_id(0)
    last = pl.num_programs(0) - 1

    def step(i, carry):
        r = pl.ds(pl.multiple_of(i * sub, sub), sub)
        x = x_ref[r, :]
        gate = dot(x, wg_ref[...])
        up = dot(x, wu_ref[...])
        sigmoid = 1.0 / (1.0 + jnp.exp(-gate))
        activated = gate * sigmoid
        hidden = (activated * up).astype(BF)
        h_ref[r, :] = hidden
        grad_hidden = dot_t(dy_ref[r, :], wd_ref[...])
        grad_gate = (grad_hidden * up * sigmoid * (1.0 + gate * (1.0 - sigmoid))).astype(BF)
        grad_up = (grad_hidden * activated).astype(BF)
        dg_ref[r, :] = grad_gate
        du_ref[r, :] = grad_up
        y = dot(hidden, wd_ref[...])
        dx = dot_t(grad_gate, wg_ref[...]) + dot_t(grad_up, wu_ref[...])

        @pl.when(f == 0)
        def _():
            y_acc[r, :] = y
            dx_acc[r, :] = dx

        @pl.when((f > 0) & (f < last))
        def _():
            y_acc[r, :] += y
            dx_acc[r, :] += dx

        @pl.when(f == last)
        def _():
            y_ref[r, :] = (y_acc[r, :] + y).astype(BF)
            dx_ref[r, :] = (dx_acc[r, :] + dx).astype(BF)

        return carry

    lax.fori_loop(0, x_ref.shape[0] // sub, step, 0)


def expert(j, x, dy, w_gate, w_up, w_down):
    _, rows, width = x.shape
    hidden = w_gate.shape[2]
    tile = hidden // 2
    rows_in = pl.BlockSpec((None, rows, width), lambda f: (j, 0, 0))
    rows_out = pl.BlockSpec((rows, width), lambda f: (0, 0))
    part = pl.BlockSpec((rows, tile), lambda f: (0, f))
    wide = jax.ShapeDtypeStruct((rows, width), BF)
    thin = jax.ShapeDtypeStruct((rows, hidden), BF)
    return pl.pallas_call(
        functools.partial(expert_body, rows // 2),
        grid=(2,),
        in_specs=[
            rows_in,
            rows_in,
            pl.BlockSpec((None, width, tile), lambda f: (j, 0, f)),
            pl.BlockSpec((None, width, tile), lambda f: (j, 0, f)),
            pl.BlockSpec((None, tile, width), lambda f: (j, f, 0)),
        ],
        out_specs=[rows_out, rows_out, part, part, part],
        out_shape=[wide, wide, thin, thin, thin],
        scratch_shapes=[pltpu.VMEM((rows, width), F32)] * 2,
        compiler_params=params(58),
        cost_estimate=cost(
            12 * rows * width * hidden,
            8 * rows * width + 6 * rows * hidden + 6 * width * hidden,
            rows * hidden,
        ),
    )(x, dy, w_gate, w_up, w_down)


def weight_grads_body(groups, count, *refs):
    left, rights, outs = refs[:groups], refs[groups : groups + groups * count], refs[-count:]
    for n in range(count):
        total = None
        for g in range(groups):
            part = t_dot(left[g][...], rights[n * groups + g][...])
            total = part if total is None else total + part
        outs[n][...] = total.astype(BF)


def weight_grads(lefts, rights, left_index, right_index):
    groups, count = len(lefts), len(rights)

    def tiled(array, index, tile):
        if array.ndim == 3:
            return pl.BlockSpec((None, array.shape[1], tile), lambda d: (index, 0, d))
        return pl.BlockSpec((array.shape[0], tile), lambda d: (0, d))

    def fixed(array, index):
        if array.ndim == 3:
            return pl.BlockSpec((None,) + array.shape[1:], lambda d: (index, 0, 0))
        return pl.BlockSpec(array.shape, lambda d: (0, 0))

    tall = lefts[0].shape[-1]
    wide = rights[0][0].shape[-1]
    tile = 256
    flat = [r for one in rights for r in one]
    total_rows = sum(a.shape[-2] for a in lefts)
    return pl.pallas_call(
        functools.partial(weight_grads_body, groups, count),
        grid=(tall // tile,),
        in_specs=[tiled(a, left_index, tile) for a in lefts] + [fixed(a, right_index) for a in flat],
        out_specs=[pl.BlockSpec((tile, wide), lambda d: (d, 0))] * count,
        out_shape=[jax.ShapeDtypeStruct((tall, wide), BF)] * count,
        compiler_params=params(48),
        cost_estimate=cost(
            2 * count * total_rows * tall * wide,
            2 * total_rows * (tall + count * wide) + 2 * count * tall * wide,
        ),
    )(*lefts, *flat)


def swap_core(value):
    return lax.ppermute(value, "shard", [(i, i ^ 1) for i in range(4)])


def swap_x(value):
    return lax.ppermute(value, "shard", [(i, i ^ 2) for i in range(4)])


def shard_order(position):
    return [position, position ^ 1, position ^ 2, position ^ 3]


def shard_gather(value):
    far = swap_x(value)
    near = swap_core(value)
    return [value, near, far, swap_core(far)]


def added(*terms):
    total = terms[0].astype(F32)
    for term in terms[1:]:
        total = total + term.astype(F32)
    return total


def shard_reduce(blocks):
    far = added(blocks[2], swap_core(blocks[3])).astype(BF)
    far = swap_x(far)
    near = added(blocks[0], swap_core(blocks[1]))
    return near + far.astype(F32)


def ring_next(count):
    return [(z * 2 + y, ((z + 1) % (count // 2)) * 2 + y) for z in range(count // 2) for y in range(2)]


def swap_y(value, count):
    return lax.ppermute(value, "rep", [(i, i ^ 1) for i in range(count)])


def turn_z(value, count):
    return lax.ppermute(value, "rep", ring_next(count))


def rep_order(rep, count):
    planes = count // 2
    z, y = rep // 2, rep % 2
    return [((z + planes - k) % planes) * 2 + (y ^ w) for k in range(planes) for w in range(2)]


def turn_and_cross(value, count):
    return together(turn_z(value, count), swap_y(value, count))


def rep_gather(value, count):
    blocks = []
    held = value
    for k in range(count // 2):
        if k < count // 2 - 1:
            nexts, crossed = together(turn_z(held, count), swap_y(held, count))
        else:
            nexts, crossed = None, swap_y(held, count)
        blocks += [held, crossed]
        held = nexts
    return blocks


class RepReduce:
    def __init__(self, blocks, count, *ready):
        self.blocks, self.count = blocks, count
        self.order = list(range(2, count // 2)) + [0]
        self.arrived = (swap_y(after(blocks[3], *ready), count),)
        self.total = None
        self.k = 1

    def step(self, *ready):
        arrived = together(*self.arrived, *ready)[: len(self.arrived)]
        total = added(self.blocks[2 * self.k], *arrived)
        if not self.order:
            return total
        self.k = self.order.pop(0)
        self.arrived = together(
            swap_y(after(self.blocks[2 * self.k + 1], arrived[0]), self.count),
            turn_z(total.astype(BF), self.count),
        )
        return None


def rep_reduce(blocks, count, *ready):
    reduce = RepReduce(blocks, count, *ready)
    while True:
        total = reduce.step()
        if total is not None:
            return total


def write_sums_body(blocks, ids_ref, wq_ref, wk_ref, wv_ref, gain_ref, *refs):
    in_refs, (q_ref, k_ref, v_ref, o_ref, extra_ref) = refs[:blocks], refs[-5:]
    width = q_ref.shape[1]
    heads = width // HD
    for i in range(blocks):

        @pl.when(pl.program_id(0) == i)
        def _(i=i):
            ref = in_refs[i]
            attn = None
            for m, (out, weight) in enumerate(((q_ref, wq_ref), (k_ref, wk_ref), (v_ref, wv_ref))):
                for h in range(heads):
                    start = (3 * h + m) * HD
                    piece = ref[:, start : start + HD].astype(F32)
                    out[:, h * HD : (h + 1) * HD] = piece
                    term = piece * weight[:, h * HD : (h + 1) * HD].astype(F32)
                    attn = term if attn is None else attn + term
            o_ref[...] = ref[:, 3 * width : 4 * width].astype(F32)
            extra = ref[:, 4 * width :].astype(F32)
            attn = jnp.sum(attn, axis=1, keepdims=True) / gain_ref[...]
            lane = lax.broadcasted_iota(jnp.int32, extra.shape, 1)
            extra_ref[...] = jnp.where(lane == extra.shape[1] - 1, attn, extra)


def write_sums(ids, w_query, w_key, w_value, gain, gathered, held=()):
    blocks = len(gathered)
    part, total = gathered[0].shape
    rows, width = w_query.shape
    own = pl.BlockSpec((part, width), lambda b, n: (n[b], 0))
    extra = pl.BlockSpec((part, HD), lambda b, n: (n[b], 0))
    big = jax.ShapeDtypeStruct((rows, width), F32)
    return pl.pallas_call(
        functools.partial(write_sums_body, blocks),
        grid_spec=pltpu.PrefetchScalarGridSpec(
            num_scalar_prefetch=1,
            grid=(blocks,),
            in_specs=[own, own, own, pl.BlockSpec((part, 1), lambda b, n: (n[b], 0))]
            + [pl.BlockSpec((part, total), lambda b, n: (0, 0))] * blocks
            + [pl.BlockSpec(memory_space=pl.ANY)] * len(held),
            out_specs=[own, own, own, own, extra],
        ),
        out_shape=[big, big, big, big, jax.ShapeDtypeStruct((rows, HD), F32)],
        input_output_aliases={5 + blocks + i: i for i in range(len(held))},
        compiler_params=params(52),
        cost_estimate=cost(0, blocks * part * width * 30),
    )(ids, w_query, w_key, w_value, gain, *gathered, *held)


def on_device(
    tokens,
    w_query,
    w_key,
    w_value,
    w_out,
    w_router,
    norm_attn,
    norm_ffn,
    norm_query,
    norm_key,
    w_gate,
    w_up,
    w_down,
    segments,
    routes,
    cotangent,
):
    rows_count, width = tokens.shape
    experts = w_router.shape[1]
    local_experts = w_gate.shape[0]
    rep_count = lax.axis_size("rep")
    shard_count = lax.axis_size("shard")
    position = lax.axis_index("shard")
    rep = lax.axis_index("rep")
    length = rows_count * shard_count
    capacity = max(2, rows_count * TOP * 9 // (8 * experts))
    capacity = -(-capacity // 16) * 16
    rows = w_query.shape[0]
    order = rep_order(rep, rep_count)
    order_in = shard_order(position)
    group_size = 4

    order_array = jnp.stack(order)
    order_in_array = jnp.stack(order_in)
    part = rows // rep_count
    core = position % 2

    far = packed_part(
        jnp.stack([rep, 1 - position // 2]), w_query, w_key, w_value, shard_count, part
    )
    far = swap_x(far)
    far_tokens = swap_x(tokens)
    grad_blocks = [cotangent]
    grad_held, crossed = turn_and_cross(grad_blocks[0], rep_count)
    grad_blocks += [crossed, grad_held]
    full_gate = lax.all_gather(after(w_gate, far, far_tokens, grad_held), "shard", axis=1, tiled=True)
    far = jnp.stack(
        [
            lax.dynamic_index_in_dim(far, core, 0, keepdims=False),
            swap_core(lax.dynamic_index_in_dim(far, 1 - core, 0, keepdims=False)),
        ]
    )
    routes_b = routes.astype(BF).reshape(2, 16, -1)
    routes_b = jnp.pad(routes_b, ((0, 0), (0, 0), (0, far.shape[2] - routes_b.shape[2])))
    full_up = lax.all_gather(after(w_up, far, far_tokens, grad_held), "shard", axis=1, tiled=True)
    fars = rep_gather(jnp.concatenate([far, routes_b], axis=1), rep_count)
    packed = packed_columns(after(w_query, fars[1]), w_key, w_value, shard_count)
    near = swap_core(lax.dynamic_index_in_dim(packed, position ^ 1, 0, keepdims=False))
    token_blocks = [tokens, swap_core(tokens), far_tokens, swap_core(far_tokens)]
    small = jnp.concatenate(
        [
            w_router,
            norm_attn[:, None],
            norm_ffn[:, None],
            jnp.pad(norm_query, (0, rows - norm_query.shape[0]))[:, None],
            jnp.pad(norm_key, (0, rows - norm_key.shape[0]))[:, None],
        ],
        axis=1,
    )
    small = jnp.pad(small, ((0, 0), (0, HD - small.shape[1])))
    small = jnp.stack(shard_gather(small))
    small = jnp.zeros_like(small).at[order_in_array].set(small)
    head_gains = small[:, : norm_query.shape[0], experts + 2 : experts + 4].astype(F32)
    gain_query = head_gains[:, :, 0].reshape(1, HD)
    gain_key = head_gains[:, :, 1].reshape(1, HD)
    small = small.reshape(width, HD)
    gain_attn = small[:, experts].astype(F32)
    gain_ffn = small[:, experts + 1].astype(F32)
    full_router = small[:, :experts]

    input_b, columns, qkv = project(
        order_array, order_in_array, gain_attn[None, :], packed, near, token_blocks, fars
    )
    places = jnp.concatenate([p * rows_count + jnp.arange(rows_count, dtype=jnp.int32) for p in order_in])
    inverse = THETA ** (-jnp.arange(HD // 2, dtype=F32) * 2.0 / HD)
    angles = places.astype(F32)[:, None] * inverse[None, :]
    cosine, sine = jnp.cos(angles), jnp.sin(angles)
    cosine = jnp.concatenate([cosine, cosine], axis=-1)
    sine = jnp.concatenate([-sine, sine], axis=-1)
    segment_all = jnp.concatenate(
        [lax.dynamic_slice_in_dim(segments[0], p * rows_count, rows_count) for p in order_in]
    )
    attn_args = (cosine, sine, gain_query, gain_key, segment_all[:, None], segment_all[None, :])
    mixed_b = attention_forward(qkv, attn_args)
    planes = rep_count // 2
    for k in range(1, planes - 1):
        grad_held, crossed = turn_and_cross(after(grad_held, fars[-1]), rep_count)
        grad_blocks += [crossed, grad_held]
        if k == 1:
            mixed_b = after(mixed_b, grad_held)
    projected = dot(mixed_b, w_out).astype(BF)
    projected = [projected[i * rows_count : (i + 1) * rows_count] for i in range(shard_count)]
    tokens_f = tokens.astype(F32)
    attended = shard_reduce(projected)
    full_down = lax.all_gather(
        after(w_down, attended, grad_held), "shard", axis=1, tiled=True
    )
    hidden_state = tokens_f + attended

    scale_mid = rms_scale(hidden_state)
    normed_mid = hidden_state * scale_mid
    mid_b = (normed_mid * gain_ffn).astype(BF)
    expert_ids = jnp.arange(experts, dtype=jnp.int32)
    first_expert = rep * local_experts
    before = jnp.tril(jnp.ones((rows_count, rows_count), BF), -1)

    route_all = jnp.stack([block[:, part:, : rows_count * TOP // 32] for block in fars])
    route_all = route_all.reshape(rep_count, rows_count, TOP).astype(jnp.int32)
    named_all = jnp.any(route_all[:, :, :, None] == expert_ids, axis=2)
    named_mine = lax.dynamic_slice_in_dim(named_all, first_expert, local_experts, axis=2)
    slots = jnp.einsum("ts,bsj->btj", before, named_mine.astype(BF), preferred_element_type=F32)
    slots = jnp.where(named_mine, slots.astype(jnp.int32), -1)
    slot_lanes = jnp.swapaxes(slots, 1, 2)
    named_lanes = jnp.pad(named_all.astype(F32), ((0, 0), (0, 0), (0, HD - experts)))

    router_lanes = jnp.pad(full_router, ((0, 0), (0, HD - experts)))
    number = jnp.stack([first_expert, jnp.int32(experts)])
    picked, groups = [], []
    mid_b = after(mid_b, grad_held, slots, slot_lanes, named_lanes)

    def pick_next(block):
        b = len(picked)
        place = b % group_size
        held = picked[-1][:2] if place else None
        picked.append(
            pick(
                number,
                slot_lanes,
                named_lanes,
                router_lanes,
                block,
                grad_blocks[b],
                held,
                b,
                place,
                group_size,
                capacity,
            )
        )
        if place == group_size - 1:
            x, dy = [
                a.reshape(local_experts, group_size * capacity, width) for a in picked[-1][:2]
            ]
            groups.append((x, dy, []))

    def run_expert(group, j, *others):
        x, dy, done = groups[group]
        done.append(expert(j, after(x, *others), dy, full_gate, full_up, full_down))
        return done[-1][0]

    def merge_grads(group):
        return merge_rows(slots, group * group_size, [d[1] for d in groups[group][2]], group_size)

    def merge_group(group, *ready):
        members = slice(group * group_size, (group + 1) * group_size)
        *parts, dgate = merge_results(
            after(slots, *ready),
            group * group_size,
            [p[2] for p in picked[members]],
            grad_blocks[members],
            [d[0] for d in groups[group][2]],
        )
        return parts, dgate

    held, crossed, ready = mid_b, None, ()
    for k in range(planes):
        held = after(held, *ready)
        if k < planes - 1:
            nexts, crossing = turn_and_cross(held, rep_count)
        else:
            nexts, crossing = None, swap_y(held, rep_count)
        if k > 0:
            pick_next(crossed)
        pick_next(held)
        ready = (picked[-1][0],)
        held, crossed = nexts, crossing
    grad_blocks.append(swap_y(after(grad_held, crossed), rep_count))
    grad_parts, result_parts, dgate_parts = [], [], []
    last = rep_count // group_size - 1
    ready = ()
    for g in range(last):
        for j in range(local_experts):
            ready = (run_expert(g, j, *ready),)
        grad_parts += merge_grads(g)
        ready = (grad_parts[-1],)
    cross_first = swap_y(grad_parts[3], rep_count)
    cross_zero = swap_y(after(grad_parts[1], grad_parts[3]), rep_count)
    pick_next(after(crossed, *ready))
    y = run_expert(last, 0)
    cross_first, cross_zero = together(cross_first, cross_zero, y)[:2]
    total = turn_z(added(grad_parts[2], cross_first).astype(BF), rep_count)
    for j in range(1, local_experts):
        y = run_expert(last, j, cross_first, cross_zero)
    total = after(total, y)
    grad_parts += merge_grads(last)
    arrived = swap_y(grad_parts[5], rep_count)
    for g in range(last + 1):
        parts, dgate = merge_group(g, grad_parts[-1])
        result_parts += parts
        dgate_parts.append(dgate)

    def owned_part(grad):
        return lax.psum_scatter(grad, "shard", scatter_dimension=0, tiled=True)

    def wide_grads(j, *others):
        return weight_grads(
            [after(g[0], *others) for g in groups],
            [[g[2][j][3] for g in groups], [g[2][j][4] for g in groups]],
            j,
            None,
        )

    def down_grads(j, *others):
        return weight_grads(
            [after(g[2][j][2], *others) for g in groups], [[g[1] for g in groups]], None, j
        )[0]

    arrived = after(arrived, *result_parts, *dgate_parts)
    made = []
    for k in range(2, planes):
        total = added(grad_parts[2 * k], arrived, total).astype(BF)
        if k < planes - 1:
            total, arrived = together(
                turn_z(total, rep_count), swap_y(after(grad_parts[2 * k + 3], arrived), rep_count)
            )
            if not made:
                made.append(wide_grads(0, grad_parts[-1], *result_parts))
                total, arrived = together(total, arrived, *made[0])[:2]
        else:
            total = turn_z(total, rep_count)
    grad_mid_moe = added(grad_parts[0], cross_zero, total)

    dgates = jnp.swapaxes(jnp.concatenate(dgate_parts), 1, 2)
    dgates = jnp.zeros_like(dgates).at[order_array].set(dgates)
    dgates = lax.all_to_all(dgates, "rep", split_axis=0, concat_axis=0, tiled=True)
    dgates = dgates.reshape(experts, rows_count).T
    named_own = jnp.any(routes[:, :, None] == expert_ids, axis=1)
    logits = dot(mid_b, full_router)
    exps = jnp.exp(logits - jnp.max(logits, axis=-1, keepdims=True))
    probs_own = exps / jnp.sum(exps, axis=-1, keepdims=True)
    chosen_total = jnp.sum(jnp.where(named_own, probs_own, 0.0), axis=1, keepdims=True)
    gates_own = jnp.where(named_own, probs_own, 0.0) / chosen_total
    grad_probs = jnp.where(
        named_own, dgates - jnp.sum(dgates * gates_own, axis=1, keepdims=True), 0.0
    ) / chosen_total
    grad_logits = (
        probs_own * (grad_probs - jnp.sum(probs_own * grad_probs, axis=1, keepdims=True))
    ).astype(BF)
    grad_mid = grad_mid_moe + dot_t(grad_logits, full_router)
    grad_gain_ffn = jnp.sum(grad_mid * normed_mid, axis=0)
    grad_router = t_dot(mid_b, grad_logits)
    grad_out = cotangent.astype(F32)
    grad_state = grad_out + norm_back(grad_mid * gain_ffn, normed_mid, scale_mid)
    grad_state_b = grad_state.astype(BF)

    state_blocks = shard_gather(grad_state_b)
    while len(made) < local_experts:
        made.append(wide_grads(len(made), grad_state_b))
    grad_state_all = jnp.concatenate(state_blocks, axis=0)
    grad_state_all = after(grad_state_all, *made[-1])
    grad_mixed = dot_t(grad_state_all, w_out).astype(BF)
    heads = qkv.shape[1] // (3 * HD)
    grad_qkv, grad_head_gains = attention_backward(qkv, grad_mixed, attn_args, 0, heads)
    grad_columns = t_dot(input_b, grad_qkv).astype(BF)
    grad_out_proj = t_dot(mixed_b, grad_state_all).astype(BF)
    expert_sum = rep_reduce(result_parts, rep_count, grad_mid_moe)
    output = (hidden_state + expert_sum).astype(BF)
    grad_input = dot_t(after(grad_qkv, grad_columns), columns).astype(BF)
    grad_input = shard_reduce(
        [grad_input[i * rows_count : (i + 1) * rows_count] for i in range(shard_count)]
    )
    normed_in = tokens_f * rms_scale(tokens_f)
    tokens_grad = (
        grad_state + norm_back(grad_input * gain_attn, normed_in, rms_scale(tokens_f))
    ).astype(BF)
    sums_gate = [owned_part(after(m[0], state_blocks[2])) for m in made]
    sums_up = [owned_part(after(m[1], state_blocks[2])) for m in made]

    piece = HD // shard_count
    head_columns = jnp.pad(
        grad_head_gains[:2].reshape(2, shard_count, piece), ((0, 0), (0, 0), (0, rows - piece))
    ).reshape(2, width)
    extras = jnp.concatenate(
        [grad_router, grad_gain_ffn[:, None], head_columns.T], axis=1
    )
    extras = jnp.pad(extras, ((0, 0), (0, HD - extras.shape[1]))).astype(BF)
    out_columns = jnp.swapaxes(grad_out_proj.reshape(rows, shard_count, -1), 0, 1)
    out_columns = out_columns.reshape(shard_count, rep_count, part, -1)
    column_parts = grad_columns.reshape(shard_count, rep_count, part, -1)
    extra_parts = extras.reshape(shard_count, rep_count, part, -1)
    to_sum = jnp.concatenate([column_parts, extra_parts, out_columns], axis=3)
    to_sum = [lax.dynamic_index_in_dim(to_sum, r, axis=1, keepdims=False) for r in order]
    half = shard_count // 2
    halves = [
        RepReduce([a[h : h + half] for a in to_sum], rep_count) for h in (0, half)
    ]
    sums_down = []
    part_sum = [None, None]
    while None in part_sum:
        if len(sums_down) < local_experts:
            sums_down.append(owned_part(down_grads(len(sums_down), halves[0].arrived[0])))
        part_sum = [h.step() for h in halves]
    part_sum = jnp.concatenate(part_sum, axis=0).astype(BF)
    while len(sums_down) < local_experts:
        sums_down.append(owned_part(down_grads(len(sums_down), part_sum)))
    grad_gate = jnp.stack(sums_gate).astype(F32)
    grad_up = jnp.stack(sums_up).astype(F32)
    grad_down = jnp.stack(sums_down).astype(F32)
    split = grad_columns.shape[1] + HD
    mine = lax.all_to_all(part_sum[:, :, :split], "shard", split_axis=0, concat_axis=0, tiled=True)
    wide = jnp.swapaxes(mine[:, :, : split - HD], 0, 1).reshape(part, -1)
    extra = jnp.sum(mine[:, :, split - HD :].astype(F32), axis=0).astype(BF)
    out_part = jnp.swapaxes(part_sum[:, :, split:], 0, 1).reshape(part, -1)
    gathered = rep_gather(jnp.concatenate([wide, out_part, extra], axis=1), rep_count)
    gain_rows = norm_attn.astype(F32)[:, None]
    most = rep_count - 3
    held = write_sums(order_array[:most], w_query, w_key, w_value, gain_rows, gathered[:most])
    sum_query, sum_key, sum_value, sum_out, extra = write_sums(
        order_array[most:], w_query, w_key, w_value, gain_rows, gathered[most:], held
    )
    return (
        output,
        tokens_grad,
        sum_query,
        sum_key,
        sum_value,
        sum_out,
        extra[:, :experts],
        extra[:, HD - 1],
        extra[:, experts],
        extra[:piece, experts + 1],
        extra[:piece, experts + 2],
        grad_gate,
        grad_up,
        grad_down,
    )


def solution(mesh):
    return jax.shard_map(
        on_device,
        mesh=mesh,
        in_specs=(
            P(("rep", "shard"), None),
            P("shard", None),
            P("shard", None),
            P("shard", None),
            P("shard", None),
            P("shard", None),
            P("shard"),
            P("shard"),
            P("shard"),
            P("shard"),
            P("rep", "shard", None),
            P("rep", "shard", None),
            P("rep", "shard", None),
            P("rep", None),
            P(("rep", "shard"), None),
            P(("rep", "shard"), None),
        ),
        out_specs=(
            P(("rep", "shard"), None),
            P(("rep", "shard"), None),
            P("shard", None),
            P("shard", None),
            P("shard", None),
            P("shard", None),
            P("shard", None),
            P("shard"),
            P("shard"),
            P("shard"),
            P("shard"),
            P("rep", "shard", None),
            P("rep", "shard", None),
            P("rep", "shard", None),
        ),
        check_vma=False,
    )
```

```python
import functools

import jax
import jax.numpy as jnp
from jax import lax
from jax.experimental import pallas as pl
from jax.experimental.pallas import tpu as pltpu
from jax.sharding import PartitionSpec as P

HEADS = 16
HD = 128
TOP = 8

EPSILON = 1e-05
THETA = 50000.0
MASKED = -1e30
BF = jnp.bfloat16
F32 = jnp.float32
QCHUNK = 256
VMEM = 58 << 20


def rms_scale(values):
    return lax.rsqrt(jnp.mean(values * values, axis=-1, keepdims=True) + EPSILON)


def norm_back(grad, normed, scale):
    return scale * (grad - normed * jnp.mean(grad * normed, axis=-1, keepdims=True))


def dot(left, right):
    return jnp.dot(left, right, preferred_element_type=F32)


def dot_t(left, right):
    return lax.dot_general(left, right, (((1,), (1,)), ((), ())), preferred_element_type=F32)


def t_dot(left, right):
    return lax.dot_general(left, right, (((0,), (0,)), ((), ())), preferred_element_type=F32)


def params(mib=40):
    return pltpu.CompilerParams(vmem_limit_bytes=mib << 20)


def cost(flops, size, transcendentals=0):
    return pl.CostEstimate(
        flops=int(flops), bytes_accessed=int(size), transcendentals=int(transcendentals)
    )


def after(value, *others):
    return lax.optimization_barrier((value,) + others)[0]


def together(*values):
    return lax.optimization_barrier(values)


def pack_columns(q_ref, k_ref, v_ref, out_ref):
    for h in range(q_ref.shape[1] // HD):
        for m, ref in enumerate((q_ref, k_ref, v_ref)):
            start = (3 * h + m) * HD
            out_ref[0, :, start : start + HD] = ref[:, h * HD : (h + 1) * HD]


def packed_columns(w_query, w_key, w_value, shards):
    rows, width = w_query.shape
    part = width // shards
    spec = pl.BlockSpec((rows, part), lambda s: (0, s))
    return pl.pallas_call(
        pack_columns,
        grid=(shards,),
        in_specs=[spec, spec, spec],
        out_specs=pl.BlockSpec((1, rows, 3 * part), lambda s: (s, 0, 0)),
        out_shape=jax.ShapeDtypeStruct((shards, rows, 3 * part), BF),
        compiler_params=params(),
        cost_estimate=cost(0, 12 * rows * width),
    )(w_query, w_key, w_value)


def pack_part(place_ref, q_ref, k_ref, v_ref, out_ref):
    pack_columns(q_ref, k_ref, v_ref, out_ref)


def packed_part(place, w_query, w_key, w_value, shards, part):
    width = w_query.shape[1] // shards
    spec = pl.BlockSpec((part, width), lambda s, n: (n[0], 2 * n[1] + s))
    return pl.pallas_call(
        pack_part,
        grid_spec=pltpu.PrefetchScalarGridSpec(
            num_scalar_prefetch=1,
            grid=(2,),
            in_specs=[spec, spec, spec],
            out_specs=pl.BlockSpec((1, part, 3 * width), lambda s, n: (s, 0, 0)),
        ),
        out_shape=jax.ShapeDtypeStruct((2, part, 3 * width), BF),
        compiler_params=params(58),
        cost_estimate=cost(0, 24 * part * width),
    )(place, w_query, w_key, w_value)


def project_body(parts, order_ref, shard_ref, gain_ref, packed_ref, near_ref, *refs):
    token_refs, far_refs = refs[:4], refs[4 : 4 + parts]
    input_ref, columns_ref, qkv_ref, sem = refs[4 + parts :]
    rows = near_ref.shape[0]
    count = token_refs[0].shape[0]
    part = rows // parts

    def place(start, size):
        return columns_ref.at[pl.ds(pl.multiple_of(start, 16), size)]

    copies = [
        pltpu.make_async_copy(packed_ref.at[shard_ref[0]], place(shard_ref[0] * rows, rows), sem.at[0]),
        pltpu.make_async_copy(near_ref, place(shard_ref[1] * rows, rows), sem.at[1]),
    ]
    for i in range(parts):
        for m in range(2):
            start = shard_ref[2 + m] * rows + order_ref[i] * part
            copies.append(
                pltpu.make_async_copy(
                    far_refs[i].at[m, pl.ds(0, part)], place(start, part), sem.at[2 + 2 * i + m]
                )
            )
    for copy in copies:
        copy.start()
    for i in range(4):
        x = token_refs[i][...].astype(F32)
        input_ref[i * count : (i + 1) * count, :] = (x * rms_scale(x) * gain_ref[...]).astype(BF)
    for copy in copies:
        copy.wait()

    def step(i, carry):
        r = pl.ds(pl.multiple_of(i * count, count), count)
        qkv_ref[r, :] = dot(input_ref[r, :], columns_ref[...])
        return carry

    lax.fori_loop(0, 4, step, 0)


def project(order, shards, gain, packed, near, token_blocks, fars):
    count, width = token_blocks[0].shape
    columns = near.shape[1]
    length = count * len(token_blocks)
    anywhere = pl.BlockSpec(memory_space=pl.ANY)
    whole = lambda *shape: pl.BlockSpec(shape, lambda i, a, b: (0, 0))
    return pl.pallas_call(
        functools.partial(project_body, len(fars)),
        grid_spec=pltpu.PrefetchScalarGridSpec(
            num_scalar_prefetch=2,
            grid=(1,),
            in_specs=[whole(1, width), anywhere, anywhere]
            + [whole(count, width)] * 4
            + [anywhere] * len(fars),
            out_specs=[whole(length, width), whole(width, columns), whole(length, columns)],
            scratch_shapes=[pltpu.SemaphoreType.DMA((2 + 2 * len(fars),))],
        ),
        out_shape=[
            jax.ShapeDtypeStruct((length, width), BF),
            jax.ShapeDtypeStruct((width, columns), BF),
            jax.ShapeDtypeStruct((length, columns), F32),
        ],
        compiler_params=params(56),
        cost_estimate=cost(
            2 * length * width * columns, 4 * length * width + 4 * width * columns + 4 * length * columns
        ),
    )(order, shards, gain, packed, near, *token_blocks, *fars)


def turned(values, cosine, sine):
    return values * cosine + pltpu.roll(values, HD // 2, 1) * sine


def turned_back(grad, cosine, sine):
    return grad * cosine - pltpu.roll(grad, HD // 2, 1) * sine


def weights_of(qb, keys, seg_column, seg_row):
    scores = dot_t(qb, keys) * (HD**-0.5)
    scores = jnp.where(seg_column == seg_row, scores, MASKED)
    shifted = jnp.exp(scores - jnp.max(scores, axis=-1, keepdims=True))
    return shifted * (1.0 / jnp.sum(shifted, axis=-1, keepdims=True))


def attend_forward(qkv_ref, cos_ref, sin_ref, gq_ref, gk_ref, segc_ref, segr_ref, o_ref, kb_ref, vb_ref):
    length = qkv_ref.shape[0]
    k_raw = qkv_ref[:, HD : 2 * HD]
    kb_ref[...] = turned(k_raw * rms_scale(k_raw) * gk_ref[...], cos_ref[...], sin_ref[...]).astype(BF)
    vb_ref[...] = qkv_ref[:, 2 * HD :].astype(BF)

    def step(i, carry):
        rows = pl.ds(pl.multiple_of(i * QCHUNK, QCHUNK), QCHUNK)
        q_raw = qkv_ref[rows, :HD]
        qb = turned(q_raw * rms_scale(q_raw) * gq_ref[...], cos_ref[rows, :], sin_ref[rows, :]).astype(BF)
        probs = weights_of(qb, kb_ref[...], segc_ref[rows, :], segr_ref[...])
        o_ref[rows, :] = dot(probs.astype(BF), vb_ref[...]).astype(BF)
        return carry

    lax.fori_loop(0, length // QCHUNK, step, 0)


def attend_backward(
    qkv_ref,
    do_ref,
    cos_ref,
    sin_ref,
    gq_ref,
    gk_ref,
    segc_ref,
    segr_ref,
    *refs,
):
    grad_ref, gains_ref, kb_ref, vb_ref, dk_acc, dv_acc = refs[-6:]
    length = qkv_ref.shape[0]
    scale = HD**-0.5

    @pl.when(pl.program_id(0) == 0)
    def _():
        gains_ref[...] = jnp.zeros_like(gains_ref)

    k_raw = qkv_ref[:, HD : 2 * HD]
    kb_ref[...] = turned(k_raw * rms_scale(k_raw) * gk_ref[...], cos_ref[...], sin_ref[...]).astype(BF)
    vb_ref[...] = qkv_ref[:, 2 * HD :].astype(BF)
    dk_acc[...] = jnp.zeros_like(dk_acc)
    dv_acc[...] = jnp.zeros_like(dv_acc)

    def step(i, carry):
        rows = pl.ds(pl.multiple_of(i * QCHUNK, QCHUNK), QCHUNK)
        cosine, sine = cos_ref[rows, :], sin_ref[rows, :]
        q_raw = qkv_ref[rows, :HD]
        q_scale = rms_scale(q_raw)
        q_norm = q_raw * q_scale
        qb = turned(q_norm * gq_ref[...], cosine, sine).astype(BF)
        probs = weights_of(qb, kb_ref[...], segc_ref[rows, :], segr_ref[...])
        grad_o = do_ref[rows, :]
        grad_probs = dot_t(grad_o, vb_ref[...])
        dv_acc[...] += t_dot(probs.astype(BF), grad_o)
        weighted = probs * grad_probs
        grad_scores = (weighted - probs * jnp.sum(weighted, axis=-1, keepdims=True)).astype(BF)
        dk_acc[...] += t_dot(grad_scores, qb)
        eq = turned_back(dot(grad_scores, kb_ref[...]) * scale, cosine, sine)
        gains_ref[0:1, :] += jnp.sum(eq * q_norm, axis=0, keepdims=True)
        grad_ref[rows, :HD] = norm_back(eq * gq_ref[...], q_norm, q_scale).astype(BF)
        return carry

    lax.fori_loop(0, length // QCHUNK, step, 0)
    ek = turned_back(dk_acc[...] * scale, cos_ref[...], sin_ref[...])
    k_raw = qkv_ref[:, HD : 2 * HD]
    k_scale = rms_scale(k_raw)
    k_norm = k_raw * k_scale
    gains_ref[1:2, :] += jnp.sum(ek * k_norm, axis=0, keepdims=True)
    grad_ref[:, HD : 2 * HD] = norm_back(ek * gk_ref[...], k_norm, k_scale).astype(BF)
    grad_ref[:, 2 * HD :] = dv_acc[...].astype(BF)


def attention_specs(length):
    table = pl.BlockSpec((length, HD), lambda h: (0, 0))
    gain = pl.BlockSpec((1, HD), lambda h: (0, 0))
    column = pl.BlockSpec((length, 1), lambda h: (0, 0))
    row = pl.BlockSpec((1, length), lambda h: (0, 0))
    return [table, table, gain, gain, column, row]


def attention_forward(qkv, attn_args):
    length = qkv.shape[0]
    heads = qkv.shape[1] // (3 * HD)
    return pl.pallas_call(
        attend_forward,
        grid=(heads,),
        in_specs=[pl.BlockSpec((length, 3 * HD), lambda h: (0, h))] + attention_specs(length),
        out_specs=pl.BlockSpec((length, HD), lambda h: (0, h)),
        out_shape=jax.ShapeDtypeStruct((length, heads * HD), BF),
        scratch_shapes=[pltpu.VMEM((length, HD), BF)] * 2,
        compiler_params=params(),
        cost_estimate=cost(16 * heads * length * length * HD, qkv.size * 5, heads * length * length),
    )(qkv, *attn_args)


def attention_backward(qkv, grad_o, attn_args, first, heads, held=None):
    length = qkv.shape[0]
    wide = pl.BlockSpec((length, 3 * HD), lambda h: (0, first + h))
    return pl.pallas_call(
        attend_backward,
        grid=(heads,),
        in_specs=[wide, pl.BlockSpec((length, HD), lambda h: (0, first + h))]
        + attention_specs(length)
        + [pl.BlockSpec(memory_space=pl.ANY)] * (held is not None),
        out_specs=[wide, pl.BlockSpec((8, HD), lambda h: (0, 0))],
        out_shape=[
            jax.ShapeDtypeStruct(qkv.shape, BF),
            jax.ShapeDtypeStruct((8, HD), F32),
        ],
        scratch_shapes=[pltpu.VMEM((length, HD), BF)] * 2 + [pltpu.VMEM((length, HD), F32)] * 2,
        input_output_aliases={} if held is None else {8: 0},
        compiler_params=params(48),
        cost_estimate=cost(40 * heads * length * length * HD, qkv.size * 3, heads * length * length),
    )(qkv, grad_o, *attn_args, *(() if held is None else (held,)))


def read_names_body(experts, local, first_ref, *refs):
    name_refs, (lanes_ref, slots_ref, named_ref) = refs[:-3], refs[-3:]
    count = lanes_ref.shape[2]
    row = lax.broadcasted_iota(jnp.int32, (count, count), 0)
    column = lax.broadcasted_iota(jnp.int32, (count, count), 1)
    earlier = (row < column).astype(BF)
    expert_row = lax.broadcasted_iota(jnp.int32, (experts, count), 0)
    for b, ref in enumerate(name_refs):
        named = ref[0, ref.shape[1] - experts :, :]
        slots = jnp.where(named > 0, dot(named, earlier), -1.0)
        mine = [
            jnp.sum(jnp.where(expert_row == first_ref[0] + j, slots, 0.0), axis=0, keepdims=True)
            for j in range(local)
        ]
        mine = jnp.concatenate(mine, axis=0)
        lanes_ref[b] = mine.astype(jnp.int32)
        filled = jnp.concatenate([mine, jnp.zeros((HD - local, count), F32)], axis=0)
        slots_ref[b] = filled.T.astype(jnp.int32)
        filled = jnp.concatenate([named.astype(F32), jnp.zeros((HD - experts, count), F32)], axis=0)
        named_ref[b] = filled.T


def read_names(first, blocks, experts, local, count):
    number, height = len(blocks), blocks[0].shape[1]
    whole = lambda *shape: pl.BlockSpec(shape, lambda i, n: (0, 0, 0))
    return pl.pallas_call(
        functools.partial(read_names_body, experts, local),
        grid_spec=pltpu.PrefetchScalarGridSpec(
            num_scalar_prefetch=1,
            grid=(1,),
            in_specs=[whole(1, height, count)] * number,
            out_specs=[whole(number, local, count), whole(number, count, HD), whole(number, count, HD)],
        ),
        out_shape=[
            jax.ShapeDtypeStruct((number, local, count), jnp.int32),
            jax.ShapeDtypeStruct((number, count, HD), jnp.int32),
            jax.ShapeDtypeStruct((number, count, HD), F32),
        ],
        compiler_params=params(),
        cost_estimate=cost(2 * number * experts * count * count, 10 * number * count * HD),
    )(first, *blocks)


def pick_rows(has_input, number_ref, slots_ref, named_ref, router_ref, x_ref, grad_ref, *refs):
    rows_ref, grad_rows_ref, gates_ref = refs[2 * has_input :]
    experts, capacity = slots_ref.shape[1], rows_ref.shape[2]
    count = x_ref.shape[0]
    x = x_ref[...]
    logits = dot(x, router_ref[...])
    lane = lax.broadcasted_iota(jnp.int32, logits.shape, 1)
    logits = jnp.where(lane < number_ref[1], logits, MASKED)
    exps = jnp.exp(logits - jnp.max(logits, axis=-1, keepdims=True))
    probs = exps / jnp.sum(exps, axis=-1, keepdims=True)
    chosen = jnp.where(named_ref[0] > 0.0, probs, 0.0)
    gates = chosen / jnp.sum(chosen, axis=-1, keepdims=True)
    grad = grad_ref[...].astype(F32)
    wanted = lax.broadcasted_iota(jnp.int32, (capacity, count), 0)
    columns = []
    for j in range(experts):
        gate = jnp.sum(jnp.where(lane == number_ref[0] + j, gates, 0.0), axis=1, keepdims=True)
        hot = (wanted == slots_ref[0, j : j + 1, :]).astype(BF)
        rows_ref[j, 0] = dot(hot, x).astype(BF)
        grad_rows_ref[j, 0] = dot(hot, (grad * gate).astype(BF)).astype(BF)
        columns.append(gate)
    gates_ref[...] = jnp.concatenate(columns, axis=1)


def pick(number, slots, named, router, x, grad, held, block, place, blocks, capacity):
    count, width = x.shape
    experts = slots.shape[1]
    lanes = router.shape[1]
    shape = jax.ShapeDtypeStruct((experts, blocks, capacity, width), BF)
    whole = pl.BlockSpec(memory_space=pl.ANY)
    out = pl.BlockSpec((experts, 1, capacity, width), lambda i, n: (0, place, 0, 0))
    return pl.pallas_call(
        functools.partial(pick_rows, held is not None),
        grid_spec=pltpu.PrefetchScalarGridSpec(
            num_scalar_prefetch=1,
            grid=(1,),
            in_specs=[
                pl.BlockSpec((1, experts, count), lambda i, n: (block, 0, 0)),
                pl.BlockSpec((1, count, lanes), lambda i, n: (block, 0, 0)),
                pl.BlockSpec((width, lanes), lambda i, n: (0, 0)),
                pl.BlockSpec((count, width), lambda i, n: (0, 0)),
                pl.BlockSpec((count, width), lambda i, n: (0, 0)),
            ]
            + [whole, whole] * (held is not None),
            out_specs=[out, out, pl.BlockSpec((count, experts), lambda i, n: (0, 0))],
        ),
        out_shape=[shape, shape, jax.ShapeDtypeStruct((count, experts), F32)],
        input_output_aliases={} if held is None else {6: 0, 7: 1},
        compiler_params=params(58),
        cost_estimate=cost(
            4 * experts * capacity * count * width, 4 * width * (count + experts * capacity)
        ),
    )(number, slots, named, router, x, grad, *(held or ()))


def merge_rows_body(blocks, slots_ref, *refs):
    experts = len(refs) - blocks
    rows_refs, out_refs = refs[:experts], refs[experts:]
    capacity = rows_refs[0].shape[0]
    count = out_refs[0].shape[0]
    place = lax.broadcasted_iota(jnp.int32, (count, capacity), 1)
    total = None
    for j in range(experts):
        hot = (place == slots_ref[0, :, j : j + 1]).astype(BF)
        rows = dot(hot, rows_refs[j][...])
        total = rows if total is None else total + rows
    for i in range(blocks):

        @pl.when(pl.program_id(0) == i)
        def _(i=i):
            out_refs[i][...] = total.astype(BF)


def merge_rows(slots, first, rows, blocks):
    count, lanes = slots.shape[1:]
    experts = rows.shape[0]
    capacity = rows.shape[1] // blocks
    width = rows.shape[2]
    return pl.pallas_call(
        functools.partial(merge_rows_body, blocks),
        grid=(blocks,),
        in_specs=[pl.BlockSpec((1, count, lanes), lambda b: (first + b, 0, 0))]
        + [pl.BlockSpec((None, capacity, width), lambda b, j=j: (j, b, 0)) for j in range(experts)],
        out_specs=[pl.BlockSpec((count, width), lambda b: (0, 0))] * blocks,
        out_shape=[jax.ShapeDtypeStruct((count, width), BF)] * blocks,
        compiler_params=params(),
        cost_estimate=cost(
            2 * blocks * experts * capacity * count * width,
            2 * blocks * width * (count + experts * capacity),
        ),
    )(slots, *[rows] * experts)


def merge_results_body(blocks, slots_ref, *refs):
    experts = len(refs) - 3 * blocks - 1
    gates_refs, grad_refs, refs = refs[:blocks], refs[blocks : 2 * blocks], refs[2 * blocks :]
    rows_refs, out_refs, dgate_ref = refs[:experts], refs[experts:-1], refs[-1]
    capacity = rows_refs[0].shape[0]
    count = out_refs[0].shape[0]
    place = lax.broadcasted_iota(jnp.int32, (count, capacity), 1)
    for i in range(blocks):

        @pl.when(pl.program_id(0) == i)
        def _(i=i):
            grad = grad_refs[i][...].astype(F32)
            total = None
            dgates = []
            for j in range(experts):
                hot = (place == slots_ref[0, :, j : j + 1]).astype(BF)
                rows = dot(hot, rows_refs[j][...])
                dgates.append(jnp.sum(rows * grad, axis=1, keepdims=True))
                gated = rows * gates_refs[i][:, j : j + 1]
                total = gated if total is None else total + gated
            out_refs[i][...] = total.astype(BF)
            dgate_ref[0] = jnp.concatenate(dgates, axis=1)


def merge_results(slots, first, gates, grads, rows):
    blocks = len(gates)
    count, lanes = slots.shape[1:]
    experts = rows.shape[0]
    capacity = rows.shape[1] // blocks
    width = rows.shape[2]
    tokens = pl.BlockSpec((count, width), lambda b: (0, 0))
    return pl.pallas_call(
        functools.partial(merge_results_body, blocks),
        grid=(blocks,),
        in_specs=[pl.BlockSpec((1, count, lanes), lambda b: (first + b, 0, 0))]
        + [pl.BlockSpec((count, experts), lambda b: (0, 0))] * blocks
        + [tokens] * blocks
        + [pl.BlockSpec((None, capacity, width), lambda b, j=j: (j, b, 0)) for j in range(experts)],
        out_specs=[tokens] * blocks + [pl.BlockSpec((1, count, experts), lambda b: (b, 0, 0))],
        out_shape=[jax.ShapeDtypeStruct((count, width), BF)] * blocks
        + [jax.ShapeDtypeStruct((blocks, count, experts), F32)],
        compiler_params=params(),
        cost_estimate=cost(
            2 * blocks * experts * capacity * count * width,
            2 * blocks * width * (2 * count + experts * capacity),
        ),
    )(slots, *gates, *grads, *[rows] * experts)


def expert_body(
    sub,
    x_ref,
    dy_ref,
    wg_ref,
    wu_ref,
    wd_ref,
    y_ref,
    dx_ref,
    h_ref,
    dg_ref,
    du_ref,
    y_acc,
    dx_acc,
):
    f = pl.program_id(1)
    last = pl.num_programs(1) - 1

    def step(i, carry):
        r = pl.ds(pl.multiple_of(i * sub, sub), sub)
        x = x_ref[r, :]
        gate = dot(x, wg_ref[...])
        up = dot(x, wu_ref[...])
        grad_hidden = dot_t(dy_ref[r, :], wd_ref[...])
        sigmoid = 1.0 / (1.0 + jnp.exp(-gate))
        activated = gate * sigmoid
        hidden = (activated * up).astype(BF)
        h_ref[r, :] = hidden
        grad_gate = (grad_hidden * up * sigmoid * (1.0 + gate * (1.0 - sigmoid))).astype(BF)
        grad_up = (grad_hidden * activated).astype(BF)
        dg_ref[r, :] = grad_gate
        du_ref[r, :] = grad_up
        y = dot(hidden, wd_ref[...])
        dx = dot_t(grad_gate, wg_ref[...]) + dot_t(grad_up, wu_ref[...])

        @pl.when(f == 0)
        def _():
            y_acc[r, :] = y
            dx_acc[r, :] = dx

        @pl.when((f > 0) & (f < last))
        def _():
            y_acc[r, :] += y
            dx_acc[r, :] += dx

        @pl.when(f == last)
        def _():
            y_ref[r, :] = (y_acc[r, :] + y).astype(BF)
            dx_ref[r, :] = (dx_acc[r, :] + dx).astype(BF)

        return carry

    lax.fori_loop(0, x_ref.shape[0] // sub, step, 0)


def run_experts(x, dy, w_gate, w_up, w_down):
    experts, rows, width = x.shape
    hidden = w_gate.shape[2]
    tile = hidden // 2
    whole = pl.BlockSpec((None, rows, width), lambda j, f: (j, 0, 0))
    part = pl.BlockSpec((None, rows, tile), lambda j, f: (j, 0, f))
    wide = jax.ShapeDtypeStruct((experts, rows, width), BF)
    thin = jax.ShapeDtypeStruct((experts, rows, hidden), BF)
    return pl.pallas_call(
        functools.partial(expert_body, rows // 2),
        grid=(experts, 2),
        in_specs=[
            whole,
            whole,
            pl.BlockSpec((None, width, tile), lambda j, f: (j, 0, f)),
            pl.BlockSpec((None, width, tile), lambda j, f: (j, 0, f)),
            pl.BlockSpec((None, tile, width), lambda j, f: (j, f, 0)),
        ],
        out_specs=[whole, whole, part, part, part],
        out_shape=[wide, wide, thin, thin, thin],
        scratch_shapes=[pltpu.VMEM((rows, width), F32)] * 2,
        compiler_params=params(60),
        cost_estimate=cost(
            12 * experts * rows * width * hidden,
            experts * (8 * rows * width + 6 * rows * hidden + 6 * width * hidden),
            experts * rows * hidden,
        ),
    )(x, dy, w_gate, w_up, w_down)


def weight_grads_body(groups, count, *refs):
    left, rights, outs = refs[:groups], refs[groups : groups + groups * count], refs[-count:]
    for n in range(count):
        total = None
        for g in range(groups):
            part = t_dot(left[g][...], rights[n * groups + g][...])
            total = part if total is None else total + part
        outs[n][...] = total.astype(BF)


def weight_grads(lefts, rights, left_index, right_index):
    groups, count = len(lefts), len(rights)

    def tiled(array, index, tile):
        if array.ndim == 3:
            return pl.BlockSpec((None, array.shape[1], tile), lambda d: (index, 0, d))
        return pl.BlockSpec((array.shape[0], tile), lambda d: (0, d))

    def fixed(array, index):
        if array.ndim == 3:
            return pl.BlockSpec((None,) + array.shape[1:], lambda d: (index, 0, 0))
        return pl.BlockSpec(array.shape, lambda d: (0, 0))

    tall = lefts[0].shape[-1]
    wide = rights[0][0].shape[-1]
    tile = 256
    flat = [r for one in rights for r in one]
    total_rows = sum(a.shape[-2] for a in lefts)
    return pl.pallas_call(
        functools.partial(weight_grads_body, groups, count),
        grid=(tall // tile,),
        in_specs=[tiled(a, left_index, tile) for a in lefts] + [fixed(a, right_index) for a in flat],
        out_specs=[pl.BlockSpec((tile, wide), lambda d: (d, 0))] * count,
        out_shape=[jax.ShapeDtypeStruct((tall, wide), BF)] * count,
        compiler_params=params(48),
        cost_estimate=cost(
            2 * count * total_rows * tall * wide,
            2 * total_rows * (tall + count * wide) + 2 * count * tall * wide,
        ),
    )(*lefts, *flat)


def swap_core(value):
    return lax.ppermute(value, "shard", [(i, i ^ 1) for i in range(4)])


def swap_x(value):
    return lax.ppermute(value, "shard", [(i, i ^ 2) for i in range(4)])


def shard_order(position):
    return [position, position ^ 1, position ^ 2, position ^ 3]


def shard_gather(value):
    far = swap_x(value)
    near = swap_core(value)
    return [value, near, far, swap_core(far)]


def added(*terms):
    total = terms[0].astype(F32)
    for term in terms[1:]:
        total = total + term.astype(F32)
    return total


def shard_reduce(blocks):
    far = added(blocks[2], swap_core(blocks[3])).astype(BF)
    far = swap_x(far)
    near = added(blocks[0], swap_core(blocks[1]))
    return near + far.astype(F32)


def ring_next(count):
    return [(z * 2 + y, ((z + 1) % (count // 2)) * 2 + y) for z in range(count // 2) for y in range(2)]


def swap_y(value, count):
    return lax.ppermute(value, "rep", [(i, i ^ 1) for i in range(count)])


def turn_z(value, count):
    return lax.ppermute(value, "rep", ring_next(count))


def rep_order(rep, count):
    planes = count // 2
    z, y = rep // 2, rep % 2
    return [((z + planes - k) % planes) * 2 + (y ^ w) for k in range(planes) for w in range(2)]


def turn_and_cross(value, count):
    return together(turn_z(value, count), swap_y(value, count))


def rep_gather(value, count, ties=None):
    blocks = []
    held = value
    for k in range(count // 2):
        held = after(held, *(ties or {}).get(k, ()))
        if k < count // 2 - 1:
            nexts, crossed = together(turn_z(held, count), swap_y(held, count))
        else:
            nexts, crossed = None, swap_y(held, count)
        blocks += [held, crossed]
        held = nexts
    return blocks


class RepReduce:
    def __init__(self, blocks, count, *ready):
        self.blocks, self.count = blocks, count
        self.order = list(range(2, count // 2)) + [0]
        self.arrived = (swap_y(after(blocks[3], *ready), count),)
        self.total = None
        self.k = 1

    def step(self, *ready):
        arrived = together(*self.arrived, *ready)[: len(self.arrived)]
        total = added(self.blocks[2 * self.k], *arrived)
        if not self.order:
            return total
        self.k = self.order.pop(0)
        self.sent = total.astype(BF)
        self.arrived = together(
            swap_y(after(self.blocks[2 * self.k + 1], arrived[0]), self.count),
            turn_z(self.sent, self.count),
        )
        return None


def rep_reduce(blocks, count, *ready):
    reduce = RepReduce(blocks, count, *ready)
    while True:
        total = reduce.step()
        if total is not None:
            return total


def write_sums_body(blocks, ids_ref, wq_ref, wk_ref, wv_ref, gain_ref, *refs):
    in_refs, (q_ref, k_ref, v_ref, o_ref, extra_ref) = refs[:blocks], refs[-5:]
    width = q_ref.shape[1]
    heads = width // HD
    for i in range(blocks):

        @pl.when(pl.program_id(0) == i)
        def _(i=i):
            ref = in_refs[i]
            attn = None
            for m, (out, weight) in enumerate(((q_ref, wq_ref), (k_ref, wk_ref), (v_ref, wv_ref))):
                for h in range(heads):
                    start = (3 * h + m) * HD
                    piece = ref[:, start : start + HD].astype(F32)
                    out[:, h * HD : (h + 1) * HD] = piece
                    term = piece * weight[:, h * HD : (h + 1) * HD].astype(F32)
                    attn = term if attn is None else attn + term
            o_ref[...] = ref[:, 3 * width : 4 * width].astype(F32)
            extra = ref[:, 4 * width :].astype(F32)
            attn = jnp.sum(attn, axis=1, keepdims=True) / gain_ref[...]
            lane = lax.broadcasted_iota(jnp.int32, extra.shape, 1)
            extra_ref[...] = jnp.where(lane == extra.shape[1] - 1, attn, extra)


def write_sums(ids, w_query, w_key, w_value, gain, gathered, held=()):
    blocks = len(gathered)
    part, total = gathered[0].shape
    rows, width = w_query.shape
    own = pl.BlockSpec((part, width), lambda b, n: (n[b], 0))
    extra = pl.BlockSpec((part, HD), lambda b, n: (n[b], 0))
    big = jax.ShapeDtypeStruct((rows, width), F32)
    return pl.pallas_call(
        functools.partial(write_sums_body, blocks),
        grid_spec=pltpu.PrefetchScalarGridSpec(
            num_scalar_prefetch=1,
            grid=(blocks,),
            in_specs=[own, own, own, pl.BlockSpec((part, 1), lambda b, n: (n[b], 0))]
            + [pl.BlockSpec((part, total), lambda b, n: (0, 0))] * blocks
            + [pl.BlockSpec(memory_space=pl.ANY)] * len(held),
            out_specs=[own, own, own, own, extra],
        ),
        out_shape=[big, big, big, big, jax.ShapeDtypeStruct((rows, HD), F32)],
        input_output_aliases={5 + blocks + i: i for i in range(len(held))},
        compiler_params=params(52),
        cost_estimate=cost(0, blocks * part * width * 30),
    )(ids, w_query, w_key, w_value, gain, *gathered, *held)


def on_device(
    tokens,
    w_query,
    w_key,
    w_value,
    w_out,
    w_router,
    norm_attn,
    norm_ffn,
    norm_query,
    norm_key,
    w_gate,
    w_up,
    w_down,
    segments,
    routes,
    cotangent,
):
    rows_count, width = tokens.shape
    experts = w_router.shape[1]
    local_experts = w_gate.shape[0]
    rep_count = lax.axis_size("rep")
    shard_count = lax.axis_size("shard")
    position = lax.axis_index("shard")
    rep = lax.axis_index("rep")
    length = rows_count * shard_count
    capacity = max(2, rows_count * TOP * 9 // (8 * experts))
    capacity = -(-capacity // 16) * 16
    rows = w_query.shape[0]
    order = rep_order(rep, rep_count)
    order_in = shard_order(position)
    group_size = 4

    order_array = jnp.stack(order)
    order_in_array = jnp.stack(order_in)
    part = rows // rep_count
    core = position % 2

    far = packed_part(
        jnp.stack([rep, 1 - position // 2]), w_query, w_key, w_value, shard_count, part
    )
    far = swap_x(far)
    far_tokens = swap_x(tokens)
    grad_blocks = [cotangent]
    grad_held, crossed = turn_and_cross(grad_blocks[0], rep_count)
    grad_blocks += [crossed, grad_held]
    full_gate = lax.all_gather(after(w_gate, far, far_tokens, grad_held), "shard", axis=1, tiled=True)
    far = jnp.stack(
        [
            lax.dynamic_index_in_dim(far, core, 0, keepdims=False),
            swap_core(lax.dynamic_index_in_dim(far, 1 - core, 0, keepdims=False)),
        ]
    )
    expert_ids = jnp.arange(experts, dtype=jnp.int32)
    named_own = jnp.any(routes[:, :, None] == expert_ids, axis=1)
    names = jnp.pad(named_own.T.astype(BF), ((0, 0), (0, far.shape[2] - rows_count)))
    names = jnp.stack([names, names])
    full_up = lax.all_gather(
        after(w_up, far, far_tokens, grad_held), "shard", axis=1, tiled=True
    )
    fars = rep_gather(jnp.concatenate([far, names], axis=1), rep_count)
    packed = packed_columns(after(w_query, fars[1]), w_key, w_value, shard_count)
    near = swap_core(lax.dynamic_index_in_dim(packed, position ^ 1, 0, keepdims=False))
    token_blocks = [tokens, swap_core(tokens), far_tokens, swap_core(far_tokens)]
    small = jnp.concatenate(
        [
            w_router,
            norm_attn[:, None],
            norm_ffn[:, None],
            jnp.pad(norm_query, (0, rows - norm_query.shape[0]))[:, None],
            jnp.pad(norm_key, (0, rows - norm_key.shape[0]))[:, None],
        ],
        axis=1,
    )
    small = jnp.pad(small, ((0, 0), (0, HD - small.shape[1])))
    small = jnp.stack(shard_gather(small))
    small = jnp.zeros_like(small).at[order_in_array].set(small)
    head_gains = small[:, : norm_query.shape[0], experts + 2 : experts + 4].astype(F32)
    gain_query = head_gains[:, :, 0].reshape(1, HD)
    gain_key = head_gains[:, :, 1].reshape(1, HD)
    small = small.reshape(width, HD)
    gain_attn = small[:, experts].astype(F32)
    gain_ffn = small[:, experts + 1].astype(F32)
    full_router = small[:, :experts]

    input_b, columns, qkv = project(
        order_array, order_in_array, gain_attn[None, :], packed, near, token_blocks, fars
    )
    places = jnp.concatenate([p * rows_count + jnp.arange(rows_count, dtype=jnp.int32) for p in order_in])
    inverse = THETA ** (-jnp.arange(HD // 2, dtype=F32) * 2.0 / HD)
    angles = places.astype(F32)[:, None] * inverse[None, :]
    cosine, sine = jnp.cos(angles), jnp.sin(angles)
    cosine = jnp.concatenate([cosine, cosine], axis=-1)
    sine = jnp.concatenate([-sine, sine], axis=-1)
    segment_all = jnp.concatenate(
        [lax.dynamic_slice_in_dim(segments[0], p * rows_count, rows_count) for p in order_in]
    )
    attn_args = (cosine, sine, gain_query, gain_key, segment_all[:, None], segment_all[None, :])
    mixed_b = attention_forward(qkv, attn_args)
    planes = rep_count // 2
    for k in range(1, planes - 1):
        grad_held, crossed = turn_and_cross(after(grad_held, fars[-1]), rep_count)
        grad_blocks += [crossed, grad_held]
        if k == 1:
            mixed_b = after(mixed_b, grad_held)
    projected = dot(mixed_b, w_out).astype(BF)
    projected = [projected[i * rows_count : (i + 1) * rows_count] for i in range(shard_count)]
    tokens_f = tokens.astype(F32)
    attended = shard_reduce(projected)
    full_down = lax.all_gather(
        after(w_down, attended, grad_held), "shard", axis=1, tiled=True
    )
    hidden_state = tokens_f + attended

    scale_mid = rms_scale(hidden_state)
    normed_mid = hidden_state * scale_mid
    mid_b = (normed_mid * gain_ffn).astype(BF)
    first_expert = rep * local_experts
    slot_lanes, slots, named_lanes = read_names(
        first_expert[None], fars, experts, local_experts, rows_count
    )
    router_lanes = jnp.pad(full_router, ((0, 0), (0, HD - experts)))
    number = jnp.stack([first_expert, jnp.int32(experts)])
    picked, groups = [], []
    mid_b = after(mid_b, grad_held, slots, slot_lanes, named_lanes)

    def pick_next(block):
        b = len(picked)
        place = b % group_size
        held = picked[-1][:2] if place else None
        picked.append(
            pick(
                number,
                slot_lanes,
                named_lanes,
                router_lanes,
                block,
                grad_blocks[b],
                held,
                b,
                place,
                group_size,
                capacity,
            )
        )
        if place == group_size - 1:
            x, dy = [
                a.reshape(local_experts, group_size * capacity, width) for a in picked[-1][:2]
            ]
            groups.append((x, dy))

    def run_group(group, *others):
        x, dy = groups[group]
        done = run_experts(after(x, *others), dy, full_gate, full_up, full_down)
        groups[group] = (x, dy, done)
        return done[0]

    def merge_grads(group):
        return merge_rows(slots, group * group_size, groups[group][2][1], group_size)

    def merge_group(group, *ready):
        members = slice(group * group_size, (group + 1) * group_size)
        *parts, dgate = merge_results(
            after(slots, *ready),
            group * group_size,
            [p[2] for p in picked[members]],
            grad_blocks[members],
            groups[group][2][0],
        )
        return parts, dgate

    held, crossed, ready = mid_b, None, ()
    for k in range(planes):
        held = after(held, *ready)
        if k < planes - 1:
            nexts, crossing = turn_and_cross(held, rep_count)
        else:
            nexts, crossing = None, swap_y(held, rep_count)
        if k > 0:
            pick_next(crossed)
        pick_next(held)
        ready = (picked[-1][0],)
        held, crossed = nexts, crossing
    grad_blocks.append(swap_y(after(grad_held, crossed), rep_count))
    grad_parts, result_parts, dgate_parts = [], [], []
    last = rep_count // group_size - 1
    ready = ()
    for g in range(last):
        run_group(g, *ready)
        grad_parts += merge_grads(g)
        ready = (grad_parts[-1],)
    cross_first = swap_y(grad_parts[3], rep_count)
    cross_zero = swap_y(grad_parts[1], rep_count)
    pick_next(after(crossed, *ready))
    y = run_group(last)
    cross_first, cross_zero, y = together(cross_first, cross_zero, y)
    total = turn_z(added(grad_parts[2], cross_first).astype(BF), rep_count)
    grad_parts += merge_grads(last)
    arrived = swap_y(grad_parts[5], rep_count)
    for g in range(last + 1):
        parts, dgate = merge_group(g, grad_parts[-1])
        result_parts += parts
        dgate_parts.append(dgate)

    def owned_part(grad):
        return lax.psum_scatter(grad, "shard", scatter_dimension=0, tiled=True)

    def wide_grads(j, *others):
        return weight_grads(
            [after(g[0], *others) for g in groups],
            [[g[2][3] for g in groups], [g[2][4] for g in groups]],
            j,
            j,
        )

    def down_grads(j, *others):
        return weight_grads(
            [after(g[2][2], *others) for g in groups], [[g[1] for g in groups]], j, j
        )[0]

    arrived = after(arrived, *result_parts, *dgate_parts)
    made = []
    for k in range(2, planes):
        total = added(grad_parts[2 * k], arrived, total).astype(BF)
        if k < planes - 1:
            total, arrived = together(
                turn_z(total, rep_count), swap_y(after(grad_parts[2 * k + 3], arrived), rep_count)
            )
            if not made:
                made.append(wide_grads(0, grad_parts[-1], *result_parts))
                total, arrived = together(total, arrived, *made[0])[:2]
        else:
            sent = total
            total = turn_z(total, rep_count)
            while len(made) < local_experts:
                made.append(wide_grads(len(made), sent))
                total = together(total, *made[-1])[0]
    results_sum = RepReduce(result_parts, rep_count, arrived)
    total = after(total, *results_sum.arrived)
    grad_mid_moe = added(grad_parts[0], cross_zero, total)

    dgates = jnp.swapaxes(jnp.concatenate(dgate_parts), 1, 2)
    dgates = jnp.zeros_like(dgates).at[order_array].set(dgates)
    dgates = lax.all_to_all(dgates, "rep", split_axis=0, concat_axis=0, tiled=True)
    dgates = dgates.reshape(experts, rows_count).T
    logits = dot(mid_b, full_router)
    exps = jnp.exp(logits - jnp.max(logits, axis=-1, keepdims=True))
    probs_own = exps / jnp.sum(exps, axis=-1, keepdims=True)
    chosen_total = jnp.sum(jnp.where(named_own, probs_own, 0.0), axis=1, keepdims=True)
    gates_own = jnp.where(named_own, probs_own, 0.0) / chosen_total
    grad_probs = jnp.where(
        named_own, dgates - jnp.sum(dgates * gates_own, axis=1, keepdims=True), 0.0
    ) / chosen_total
    grad_logits = (
        probs_own * (grad_probs - jnp.sum(probs_own * grad_probs, axis=1, keepdims=True))
    ).astype(BF)
    grad_mid = grad_mid_moe + dot_t(grad_logits, full_router)
    grad_gain_ffn = jnp.sum(grad_mid * normed_mid, axis=0)
    grad_router = t_dot(mid_b, grad_logits)
    grad_out = cotangent.astype(F32)
    grad_state = grad_out + norm_back(grad_mid * gain_ffn, normed_mid, scale_mid)
    grad_state_b = grad_state.astype(BF)

    far_state = swap_x(grad_state_b)
    while len(results_sum.order) > 2:
        results_sum.step()
    downs = [down_grads(j, grad_state_b) for j in range(local_experts)]
    far_state = together(far_state, *results_sum.arrived, *downs)[0]
    state_blocks = [grad_state_b, swap_core(grad_state_b), far_state, swap_core(far_state)]
    grad_state_all = jnp.concatenate(state_blocks, axis=0)
    grad_mixed = dot_t(grad_state_all, w_out).astype(BF)
    heads = qkv.shape[1] // (3 * HD)
    results_sum.step()
    grad_qkv, grad_head_gains = attention_backward(qkv, grad_mixed, attn_args, 0, heads)
    grad_qkv, *results_sum.arrived = together(grad_qkv, *results_sum.arrived)
    grad_columns = t_dot(input_b, grad_qkv).astype(BF)
    grad_out_proj = t_dot(mixed_b, grad_state_all).astype(BF)
    grad_input = dot_t(after(grad_qkv, grad_columns), columns).astype(BF)
    grad_input = shard_reduce(
        [grad_input[i * rows_count : (i + 1) * rows_count] for i in range(shard_count)]
    )
    normed_in = tokens_f * rms_scale(tokens_f)
    tokens_grad = (
        grad_state + norm_back(grad_input * gain_attn, normed_in, rms_scale(tokens_f))
    ).astype(BF)
    sums_gate = [owned_part(after(m[0], grad_mixed)) for m in made]
    sums_up = [owned_part(after(m[1], grad_mixed)) for m in made]

    piece = HD // shard_count
    head_columns = jnp.pad(
        grad_head_gains[:2].reshape(2, shard_count, piece), ((0, 0), (0, 0), (0, rows - piece))
    ).reshape(2, width)
    extras = jnp.concatenate(
        [grad_router, grad_gain_ffn[:, None], head_columns.T], axis=1
    )
    extras = jnp.pad(extras, ((0, 0), (0, HD - extras.shape[1]))).astype(BF)
    out_columns = jnp.swapaxes(grad_out_proj.reshape(rows, shard_count, -1), 0, 1)
    out_columns = out_columns.reshape(shard_count, rep_count, part, -1)
    column_parts = grad_columns.reshape(shard_count, rep_count, part, -1)
    extra_parts = extras.reshape(shard_count, rep_count, part, -1)
    to_sum = jnp.concatenate([column_parts, extra_parts, out_columns], axis=3)
    to_sum = [lax.dynamic_index_in_dim(to_sum, r, axis=1, keepdims=False) for r in order]
    sums = RepReduce(to_sum, rep_count)
    expert_sum = None
    while expert_sum is None:
        expert_sum = results_sum.step()
    sums_down = [owned_part(after(d, grad_mixed)) for d in downs]
    part_sum = None
    while part_sum is None:
        part_sum = sums.step()
    part_sum = part_sum.astype(BF)
    output = (hidden_state + expert_sum).astype(BF)
    grad_gate = jnp.stack(sums_gate).astype(F32)
    grad_up = jnp.stack(sums_up).astype(F32)
    grad_down = jnp.stack(sums_down).astype(F32)
    split = grad_columns.shape[1] + HD
    mine = lax.all_to_all(part_sum[:, :, :split], "shard", split_axis=0, concat_axis=0, tiled=True)
    wide = jnp.swapaxes(mine[:, :, : split - HD], 0, 1).reshape(part, -1)
    extra = jnp.sum(mine[:, :, split - HD :].astype(F32), axis=0).astype(BF)
    out_part = jnp.swapaxes(part_sum[:, :, split:], 0, 1).reshape(part, -1)
    gathered = rep_gather(
        jnp.concatenate([wide, out_part, extra], axis=1),
        rep_count,
        {2: (grad_gate, grad_up, output), 3: (grad_down, tokens_grad)},
    )
    gain_rows = norm_attn.astype(F32)[:, None]
    most = rep_count - 1
    held = write_sums(order_array[:most], w_query, w_key, w_value, gain_rows, gathered[:most])
    sum_query, sum_key, sum_value, sum_out, extra = write_sums(
        order_array[most:], w_query, w_key, w_value, gain_rows, gathered[most:], held
    )
    return (
        output,
        tokens_grad,
        sum_query,
        sum_key,
        sum_value,
        sum_out,
        extra[:, :experts],
        extra[:, HD - 1],
        extra[:, experts],
        extra[:piece, experts + 1],
        extra[:piece, experts + 2],
        grad_gate,
        grad_up,
        grad_down,
    )


def solution(mesh):
    return jax.shard_map(
        on_device,
        mesh=mesh,
        in_specs=(
            P(("rep", "shard"), None),
            P("shard", None),
            P("shard", None),
            P("shard", None),
            P("shard", None),
            P("shard", None),
            P("shard"),
            P("shard"),
            P("shard"),
            P("shard"),
            P("rep", "shard", None),
            P("rep", "shard", None),
            P("rep", "shard", None),
            P("rep", None),
            P(("rep", "shard"), None),
            P(("rep", "shard"), None),
        ),
        out_specs=(
            P(("rep", "shard"), None),
            P(("rep", "shard"), None),
            P("shard", None),
            P("shard", None),
            P("shard", None),
            P("shard", None),
            P("shard", None),
            P("shard"),
            P("shard"),
            P("shard"),
            P("shard"),
            P("rep", "shard", None),
            P("rep", "shard", None),
            P("rep", "shard", None),
        ),
        check_vma=False,
    )
```

```python
import functools

import jax
import jax.numpy as jnp
from jax import lax
from jax.experimental import pallas as pl
from jax.experimental.pallas import tpu as pltpu
from jax.sharding import PartitionSpec as P

HEADS = 16
HD = 128
TOP = 8

EPSILON = 1e-05
THETA = 50000.0
MASKED = -1e30
BF = jnp.bfloat16
F32 = jnp.float32
QCHUNK = 256
VMEM = 58 << 20


def rms_scale(values):
    return lax.rsqrt(jnp.mean(values * values, axis=-1, keepdims=True) + EPSILON)


def norm_back(grad, normed, scale):
    return scale * (grad - normed * jnp.mean(grad * normed, axis=-1, keepdims=True))


def dot(left, right):
    return jnp.dot(left, right, preferred_element_type=F32)


def dot_t(left, right):
    return lax.dot_general(left, right, (((1,), (1,)), ((), ())), preferred_element_type=F32)


def t_dot(left, right):
    return lax.dot_general(left, right, (((0,), (0,)), ((), ())), preferred_element_type=F32)


def params(mib=40):
    return pltpu.CompilerParams(vmem_limit_bytes=mib << 20)


def cost(flops, size, transcendentals=0):
    return pl.CostEstimate(
        flops=int(flops), bytes_accessed=int(size), transcendentals=int(transcendentals)
    )


def after(value, *others):
    return lax.optimization_barrier((value,) + others)[0]


def together(*values):
    return lax.optimization_barrier(values)


def pack_columns(q_ref, k_ref, v_ref, out_ref):
    for h in range(q_ref.shape[1] // HD):
        for m, ref in enumerate((q_ref, k_ref, v_ref)):
            start = (3 * h + m) * HD
            out_ref[0, :, start : start + HD] = ref[:, h * HD : (h + 1) * HD]


def packed_columns(w_query, w_key, w_value, shards):
    rows, width = w_query.shape
    part = width // shards
    spec = pl.BlockSpec((rows, part), lambda s: (0, s))
    return pl.pallas_call(
        pack_columns,
        grid=(shards,),
        in_specs=[spec, spec, spec],
        out_specs=pl.BlockSpec((1, rows, 3 * part), lambda s: (s, 0, 0)),
        out_shape=jax.ShapeDtypeStruct((shards, rows, 3 * part), BF),
        compiler_params=params(),
        cost_estimate=cost(0, 12 * rows * width),
    )(w_query, w_key, w_value)


def pack_part(place_ref, q_ref, k_ref, v_ref, out_ref):
    pack_columns(q_ref, k_ref, v_ref, out_ref)


def packed_part(place, w_query, w_key, w_value, shards, part):
    width = w_query.shape[1] // shards
    spec = pl.BlockSpec((part, width), lambda s, n: (n[0], 2 * n[1] + s))
    return pl.pallas_call(
        pack_part,
        grid_spec=pltpu.PrefetchScalarGridSpec(
            num_scalar_prefetch=1,
            grid=(2,),
            in_specs=[spec, spec, spec],
            out_specs=pl.BlockSpec((1, part, 3 * width), lambda s, n: (s, 0, 0)),
        ),
        out_shape=jax.ShapeDtypeStruct((2, part, 3 * width), BF),
        compiler_params=params(58),
        cost_estimate=cost(0, 24 * part * width),
    )(place, w_query, w_key, w_value)


def project_body(parts, order_ref, shard_ref, gain_ref, packed_ref, near_ref, *refs):
    token_refs, far_refs = refs[:4], refs[4 : 4 + parts]
    input_ref, columns_ref, qkv_ref, sem = refs[4 + parts :]
    rows = near_ref.shape[0]
    count = token_refs[0].shape[0]
    part = rows // parts

    def place(start, size):
        return columns_ref.at[pl.ds(pl.multiple_of(start, 16), size)]

    copies = [
        pltpu.make_async_copy(packed_ref.at[shard_ref[0]], place(shard_ref[0] * rows, rows), sem.at[0]),
        pltpu.make_async_copy(near_ref, place(shard_ref[1] * rows, rows), sem.at[1]),
    ]
    for i in range(parts):
        for m in range(2):
            start = shard_ref[2 + m] * rows + order_ref[i] * part
            copies.append(
                pltpu.make_async_copy(
                    far_refs[i].at[m, pl.ds(0, part)], place(start, part), sem.at[2 + 2 * i + m]
                )
            )
    for copy in copies:
        copy.start()
    for i in range(4):
        x = token_refs[i][...].astype(F32)
        input_ref[i * count : (i + 1) * count, :] = (x * rms_scale(x) * gain_ref[...]).astype(BF)
    for copy in copies:
        copy.wait()

    def step(i, carry):
        r = pl.ds(pl.multiple_of(i * count, count), count)
        qkv_ref[r, :] = dot(input_ref[r, :], columns_ref[...])
        return carry

    lax.fori_loop(0, 4, step, 0)


def project(order, shards, gain, packed, near, token_blocks, fars):
    count, width = token_blocks[0].shape
    columns = near.shape[1]
    length = count * len(token_blocks)
    anywhere = pl.BlockSpec(memory_space=pl.ANY)
    whole = lambda *shape: pl.BlockSpec(shape, lambda i, a, b: (0, 0))
    return pl.pallas_call(
        functools.partial(project_body, len(fars)),
        grid_spec=pltpu.PrefetchScalarGridSpec(
            num_scalar_prefetch=2,
            grid=(1,),
            in_specs=[whole(1, width), anywhere, anywhere]
            + [whole(count, width)] * 4
            + [anywhere] * len(fars),
            out_specs=[whole(length, width), whole(width, columns), whole(length, columns)],
            scratch_shapes=[pltpu.SemaphoreType.DMA((2 + 2 * len(fars),))],
        ),
        out_shape=[
            jax.ShapeDtypeStruct((length, width), BF),
            jax.ShapeDtypeStruct((width, columns), BF),
            jax.ShapeDtypeStruct((length, columns), F32),
        ],
        compiler_params=params(56),
        cost_estimate=cost(
            2 * length * width * columns, 4 * length * width + 4 * width * columns + 4 * length * columns
        ),
    )(order, shards, gain, packed, near, *token_blocks, *fars)


def turned(values, cosine, sine):
    return values * cosine + pltpu.roll(values, HD // 2, 1) * sine


def turned_back(grad, cosine, sine):
    return grad * cosine - pltpu.roll(grad, HD // 2, 1) * sine


def weights_of(qb, keys, seg_column, seg_row):
    scores = dot_t(qb, keys) * (HD**-0.5)
    scores = jnp.where(seg_column == seg_row, scores, MASKED)
    shifted = jnp.exp(scores - jnp.max(scores, axis=-1, keepdims=True))
    return shifted * (1.0 / jnp.sum(shifted, axis=-1, keepdims=True))


def attend_forward(qkv_ref, cos_ref, sin_ref, gq_ref, gk_ref, segc_ref, segr_ref, o_ref, kb_ref, vb_ref):
    length = qkv_ref.shape[0]
    k_raw = qkv_ref[:, HD : 2 * HD]
    kb_ref[...] = turned(k_raw * rms_scale(k_raw) * gk_ref[...], cos_ref[...], sin_ref[...]).astype(BF)
    vb_ref[...] = qkv_ref[:, 2 * HD :].astype(BF)

    def step(i, carry):
        rows = pl.ds(pl.multiple_of(i * QCHUNK, QCHUNK), QCHUNK)
        q_raw = qkv_ref[rows, :HD]
        qb = turned(q_raw * rms_scale(q_raw) * gq_ref[...], cos_ref[rows, :], sin_ref[rows, :]).astype(BF)
        probs = weights_of(qb, kb_ref[...], segc_ref[rows, :], segr_ref[...])
        o_ref[rows, :] = dot(probs.astype(BF), vb_ref[...]).astype(BF)
        return carry

    lax.fori_loop(0, length // QCHUNK, step, 0)


def attend_backward(
    qkv_ref,
    do_ref,
    cos_ref,
    sin_ref,
    gq_ref,
    gk_ref,
    segc_ref,
    segr_ref,
    *refs,
):
    grad_ref, gains_ref, kb_ref, vb_ref, dk_acc, dv_acc = refs[-6:]
    length = qkv_ref.shape[0]
    scale = HD**-0.5

    @pl.when(pl.program_id(0) == 0)
    def _():
        gains_ref[...] = jnp.zeros_like(gains_ref)

    k_raw = qkv_ref[:, HD : 2 * HD]
    kb_ref[...] = turned(k_raw * rms_scale(k_raw) * gk_ref[...], cos_ref[...], sin_ref[...]).astype(BF)
    vb_ref[...] = qkv_ref[:, 2 * HD :].astype(BF)
    dk_acc[...] = jnp.zeros_like(dk_acc)
    dv_acc[...] = jnp.zeros_like(dv_acc)

    def step(i, carry):
        rows = pl.ds(pl.multiple_of(i * QCHUNK, QCHUNK), QCHUNK)
        cosine, sine = cos_ref[rows, :], sin_ref[rows, :]
        q_raw = qkv_ref[rows, :HD]
        q_scale = rms_scale(q_raw)
        q_norm = q_raw * q_scale
        qb = turned(q_norm * gq_ref[...], cosine, sine).astype(BF)
        probs = weights_of(qb, kb_ref[...], segc_ref[rows, :], segr_ref[...])
        grad_o = do_ref[rows, :]
        grad_probs = dot_t(grad_o, vb_ref[...])
        dv_acc[...] += t_dot(probs.astype(BF), grad_o)
        weighted = probs * grad_probs
        grad_scores = (weighted - probs * jnp.sum(weighted, axis=-1, keepdims=True)).astype(BF)
        dk_acc[...] += t_dot(grad_scores, qb)
        eq = turned_back(dot(grad_scores, kb_ref[...]) * scale, cosine, sine)
        gains_ref[0:1, :] += jnp.sum(eq * q_norm, axis=0, keepdims=True)
        grad_ref[rows, :HD] = norm_back(eq * gq_ref[...], q_norm, q_scale).astype(BF)
        return carry

    lax.fori_loop(0, length // QCHUNK, step, 0)
    ek = turned_back(dk_acc[...] * scale, cos_ref[...], sin_ref[...])
    k_raw = qkv_ref[:, HD : 2 * HD]
    k_scale = rms_scale(k_raw)
    k_norm = k_raw * k_scale
    gains_ref[1:2, :] += jnp.sum(ek * k_norm, axis=0, keepdims=True)
    grad_ref[:, HD : 2 * HD] = norm_back(ek * gk_ref[...], k_norm, k_scale).astype(BF)
    grad_ref[:, 2 * HD :] = dv_acc[...].astype(BF)


def attention_specs(length):
    table = pl.BlockSpec((length, HD), lambda h: (0, 0))
    gain = pl.BlockSpec((1, HD), lambda h: (0, 0))
    column = pl.BlockSpec((length, 1), lambda h: (0, 0))
    row = pl.BlockSpec((1, length), lambda h: (0, 0))
    return [table, table, gain, gain, column, row]


def attention_forward(qkv, attn_args):
    length = qkv.shape[0]
    heads = qkv.shape[1] // (3 * HD)
    return pl.pallas_call(
        attend_forward,
        grid=(heads,),
        in_specs=[pl.BlockSpec((length, 3 * HD), lambda h: (0, h))] + attention_specs(length),
        out_specs=pl.BlockSpec((length, HD), lambda h: (0, h)),
        out_shape=jax.ShapeDtypeStruct((length, heads * HD), BF),
        scratch_shapes=[pltpu.VMEM((length, HD), BF)] * 2,
        compiler_params=params(),
        cost_estimate=cost(16 * heads * length * length * HD, qkv.size * 5, heads * length * length),
    )(qkv, *attn_args)


def attention_backward(qkv, grad_o, attn_args, first, heads, held=None):
    length = qkv.shape[0]
    wide = pl.BlockSpec((length, 3 * HD), lambda h: (0, first + h))
    return pl.pallas_call(
        attend_backward,
        grid=(heads,),
        in_specs=[wide, pl.BlockSpec((length, HD), lambda h: (0, first + h))]
        + attention_specs(length)
        + [pl.BlockSpec(memory_space=pl.ANY)] * (held is not None),
        out_specs=[wide, pl.BlockSpec((8, HD), lambda h: (0, 0))],
        out_shape=[
            jax.ShapeDtypeStruct(qkv.shape, BF),
            jax.ShapeDtypeStruct((8, HD), F32),
        ],
        scratch_shapes=[pltpu.VMEM((length, HD), BF)] * 2 + [pltpu.VMEM((length, HD), F32)] * 2,
        input_output_aliases={} if held is None else {8: 0},
        compiler_params=params(58),
        cost_estimate=cost(40 * heads * length * length * HD, qkv.size * 3, heads * length * length),
    )(qkv, grad_o, *attn_args, *(() if held is None else (held,)))


def read_names_body(experts, local, first_ref, *refs):
    name_refs, (lanes_ref, slots_ref, named_ref) = refs[:-3], refs[-3:]
    count = lanes_ref.shape[2]
    row = lax.broadcasted_iota(jnp.int32, (count, count), 0)
    column = lax.broadcasted_iota(jnp.int32, (count, count), 1)
    earlier = (row < column).astype(BF)
    expert_row = lax.broadcasted_iota(jnp.int32, (experts, count), 0)
    for b, ref in enumerate(name_refs):
        named = ref[0, ref.shape[1] - experts :, :]
        slots = jnp.where(named > 0, dot(named, earlier), -1.0)
        mine = [
            jnp.sum(jnp.where(expert_row == first_ref[0] + j, slots, 0.0), axis=0, keepdims=True)
            for j in range(local)
        ]
        mine = jnp.concatenate(mine, axis=0)
        lanes_ref[b] = mine.astype(jnp.int32)
        filled = jnp.concatenate([mine, jnp.zeros((HD - local, count), F32)], axis=0)
        slots_ref[b] = filled.T.astype(jnp.int32)
        filled = jnp.concatenate([named.astype(F32), jnp.zeros((HD - experts, count), F32)], axis=0)
        named_ref[b] = filled.T


def read_names(first, blocks, experts, local, count):
    number, height = len(blocks), blocks[0].shape[1]
    whole = lambda *shape: pl.BlockSpec(shape, lambda i, n: (0, 0, 0))
    return pl.pallas_call(
        functools.partial(read_names_body, experts, local),
        grid_spec=pltpu.PrefetchScalarGridSpec(
            num_scalar_prefetch=1,
            grid=(1,),
            in_specs=[whole(1, height, count)] * number,
            out_specs=[whole(number, local, count), whole(number, count, HD), whole(number, count, HD)],
        ),
        out_shape=[
            jax.ShapeDtypeStruct((number, local, count), jnp.int32),
            jax.ShapeDtypeStruct((number, count, HD), jnp.int32),
            jax.ShapeDtypeStruct((number, count, HD), F32),
        ],
        compiler_params=params(),
        cost_estimate=cost(2 * number * experts * count * count, 10 * number * count * HD),
    )(first, *blocks)


def pick_rows(has_input, number_ref, slots_ref, named_ref, router_ref, x_ref, grad_ref, *refs):
    rows_ref, grad_rows_ref, gates_ref = refs[2 * has_input :]
    experts, capacity = slots_ref.shape[1], rows_ref.shape[2]
    count = x_ref.shape[0]
    x = x_ref[...]
    logits = dot(x, router_ref[...])
    lane = lax.broadcasted_iota(jnp.int32, logits.shape, 1)
    logits = jnp.where(lane < number_ref[1], logits, MASKED)
    exps = jnp.exp(logits - jnp.max(logits, axis=-1, keepdims=True))
    probs = exps / jnp.sum(exps, axis=-1, keepdims=True)
    chosen = jnp.where(named_ref[0] > 0.0, probs, 0.0)
    gates = chosen / jnp.sum(chosen, axis=-1, keepdims=True)
    grad = grad_ref[...].astype(F32)
    wanted = lax.broadcasted_iota(jnp.int32, (capacity, count), 0)
    columns = []
    for j in range(experts):
        gate = jnp.sum(jnp.where(lane == number_ref[0] + j, gates, 0.0), axis=1, keepdims=True)
        hot = (wanted == slots_ref[0, j : j + 1, :]).astype(BF)
        rows_ref[j, 0] = dot(hot, x).astype(BF)
        grad_rows_ref[j, 0] = dot(hot, (grad * gate).astype(BF)).astype(BF)
        columns.append(gate)
    gates_ref[...] = jnp.concatenate(columns, axis=1)


def pick(number, slots, named, router, x, grad, held, block, place, blocks, capacity):
    count, width = x.shape
    experts = slots.shape[1]
    lanes = router.shape[1]
    shape = jax.ShapeDtypeStruct((experts, blocks, capacity, width), BF)
    whole = pl.BlockSpec(memory_space=pl.ANY)
    out = pl.BlockSpec((experts, 1, capacity, width), lambda i, n: (0, place, 0, 0))
    return pl.pallas_call(
        functools.partial(pick_rows, held is not None),
        grid_spec=pltpu.PrefetchScalarGridSpec(
            num_scalar_prefetch=1,
            grid=(1,),
            in_specs=[
                pl.BlockSpec((1, experts, count), lambda i, n: (block, 0, 0)),
                pl.BlockSpec((1, count, lanes), lambda i, n: (block, 0, 0)),
                pl.BlockSpec((width, lanes), lambda i, n: (0, 0)),
                pl.BlockSpec((count, width), lambda i, n: (0, 0)),
                pl.BlockSpec((count, width), lambda i, n: (0, 0)),
            ]
            + [whole, whole] * (held is not None),
            out_specs=[out, out, pl.BlockSpec((count, experts), lambda i, n: (0, 0))],
        ),
        out_shape=[shape, shape, jax.ShapeDtypeStruct((count, experts), F32)],
        input_output_aliases={} if held is None else {6: 0, 7: 1},
        compiler_params=params(58),
        cost_estimate=cost(
            4 * experts * capacity * count * width, 4 * width * (count + experts * capacity)
        ),
    )(number, slots, named, router, x, grad, *(held or ()))


def merge_rows_body(blocks, slots_ref, *refs):
    experts = len(refs) - blocks
    rows_refs, out_refs = refs[:experts], refs[experts:]
    capacity = rows_refs[0].shape[0]
    count = out_refs[0].shape[0]
    place = lax.broadcasted_iota(jnp.int32, (count, capacity), 1)
    total = None
    for j in range(experts):
        hot = (place == slots_ref[0, :, j : j + 1]).astype(BF)
        rows = dot(hot, rows_refs[j][...])
        total = rows if total is None else total + rows
    for i in range(blocks):

        @pl.when(pl.program_id(0) == i)
        def _(i=i):
            out_refs[i][...] = total.astype(BF)


def merge_rows(slots, first, rows, blocks):
    count, lanes = slots.shape[1:]
    experts = rows.shape[0]
    capacity = rows.shape[1] // blocks
    width = rows.shape[2]
    return pl.pallas_call(
        functools.partial(merge_rows_body, blocks),
        grid=(blocks,),
        in_specs=[pl.BlockSpec((1, count, lanes), lambda b: (first + b, 0, 0))]
        + [pl.BlockSpec((None, capacity, width), lambda b, j=j: (j, b, 0)) for j in range(experts)],
        out_specs=[pl.BlockSpec((count, width), lambda b: (0, 0))] * blocks,
        out_shape=[jax.ShapeDtypeStruct((count, width), BF)] * blocks,
        compiler_params=params(),
        cost_estimate=cost(
            2 * blocks * experts * capacity * count * width,
            2 * blocks * width * (count + experts * capacity),
        ),
    )(slots, *[rows] * experts)


def merge_results_body(blocks, slots_ref, *refs):
    experts = len(refs) - 3 * blocks - 1
    gates_refs, grad_refs, refs = refs[:blocks], refs[blocks : 2 * blocks], refs[2 * blocks :]
    rows_refs, out_refs, dgate_ref = refs[:experts], refs[experts:-1], refs[-1]
    capacity = rows_refs[0].shape[0]
    count = out_refs[0].shape[0]
    place = lax.broadcasted_iota(jnp.int32, (count, capacity), 1)
    for i in range(blocks):

        @pl.when(pl.program_id(0) == i)
        def _(i=i):
            grad = grad_refs[i][...].astype(F32)
            total = None
            dgates = []
            for j in range(experts):
                hot = (place == slots_ref[0, :, j : j + 1]).astype(BF)
                rows = dot(hot, rows_refs[j][...])
                dgates.append(jnp.sum(rows * grad, axis=1, keepdims=True))
                gated = rows * gates_refs[i][:, j : j + 1]
                total = gated if total is None else total + gated
            out_refs[i][...] = total.astype(BF)
            dgate_ref[0] = jnp.concatenate(dgates, axis=1)


def merge_results(slots, first, gates, grads, rows):
    blocks = len(gates)
    count, lanes = slots.shape[1:]
    experts = rows.shape[0]
    capacity = rows.shape[1] // blocks
    width = rows.shape[2]
    tokens = pl.BlockSpec((count, width), lambda b: (0, 0))
    return pl.pallas_call(
        functools.partial(merge_results_body, blocks),
        grid=(blocks,),
        in_specs=[pl.BlockSpec((1, count, lanes), lambda b: (first + b, 0, 0))]
        + [pl.BlockSpec((count, experts), lambda b: (0, 0))] * blocks
        + [tokens] * blocks
        + [pl.BlockSpec((None, capacity, width), lambda b, j=j: (j, b, 0)) for j in range(experts)],
        out_specs=[tokens] * blocks + [pl.BlockSpec((1, count, experts), lambda b: (b, 0, 0))],
        out_shape=[jax.ShapeDtypeStruct((count, width), BF)] * blocks
        + [jax.ShapeDtypeStruct((blocks, count, experts), F32)],
        compiler_params=params(),
        cost_estimate=cost(
            2 * blocks * experts * capacity * count * width,
            2 * blocks * width * (2 * count + experts * capacity),
        ),
    )(slots, *gates, *grads, *[rows] * experts)


def expert_body(
    sub,
    x_ref,
    dy_ref,
    wg_ref,
    wu_ref,
    wd_ref,
    y_ref,
    dx_ref,
    h_ref,
    dg_ref,
    du_ref,
    y_acc,
    dx_acc,
):
    f = pl.program_id(1)
    last = pl.num_programs(1) - 1

    def step(i, carry):
        r = pl.ds(pl.multiple_of(i * sub, sub), sub)
        x = x_ref[r, :]
        gate = dot(x, wg_ref[...])
        up = dot(x, wu_ref[...])
        grad_hidden = dot_t(dy_ref[r, :], wd_ref[...])
        sigmoid = 1.0 / (1.0 + jnp.exp(-gate))
        activated = gate * sigmoid
        hidden = (activated * up).astype(BF)
        h_ref[r, :] = hidden
        grad_gate = (grad_hidden * up * sigmoid * (1.0 + gate * (1.0 - sigmoid))).astype(BF)
        grad_up = (grad_hidden * activated).astype(BF)
        dg_ref[r, :] = grad_gate
        du_ref[r, :] = grad_up
        y = dot(hidden, wd_ref[...])
        dx = dot_t(grad_gate, wg_ref[...]) + dot_t(grad_up, wu_ref[...])

        @pl.when(f == 0)
        def _():
            y_acc[r, :] = y
            dx_acc[r, :] = dx

        @pl.when((f > 0) & (f < last))
        def _():
            y_acc[r, :] += y
            dx_acc[r, :] += dx

        @pl.when(f == last)
        def _():
            y_ref[r, :] = (y_acc[r, :] + y).astype(BF)
            dx_ref[r, :] = (dx_acc[r, :] + dx).astype(BF)

        return carry

    lax.fori_loop(0, x_ref.shape[0] // sub, step, 0)


def run_experts(x, dy, w_gate, w_up, w_down):
    experts, rows, width = x.shape
    hidden = w_gate.shape[2]
    tile = hidden // 2
    whole = pl.BlockSpec((None, rows, width), lambda j, f: (j, 0, 0))
    part = pl.BlockSpec((None, rows, tile), lambda j, f: (j, 0, f))
    wide = jax.ShapeDtypeStruct((experts, rows, width), BF)
    thin = jax.ShapeDtypeStruct((experts, rows, hidden), BF)
    return pl.pallas_call(
        functools.partial(expert_body, rows // 2),
        grid=(experts, 2),
        in_specs=[
            whole,
            whole,
            pl.BlockSpec((None, width, tile), lambda j, f: (j, 0, f)),
            pl.BlockSpec((None, width, tile), lambda j, f: (j, 0, f)),
            pl.BlockSpec((None, tile, width), lambda j, f: (j, f, 0)),
        ],
        out_specs=[whole, whole, part, part, part],
        out_shape=[wide, wide, thin, thin, thin],
        scratch_shapes=[pltpu.VMEM((rows, width), F32)] * 2,
        compiler_params=params(60),
        cost_estimate=cost(
            12 * experts * rows * width * hidden,
            experts * (8 * rows * width + 6 * rows * hidden + 6 * width * hidden),
            experts * rows * hidden,
        ),
    )(x, dy, w_gate, w_up, w_down)


def weight_grads_body(groups, count, *refs):
    left, rights, outs = refs[:groups], refs[groups : groups + groups * count], refs[-count:]
    for n in range(count):
        total = None
        for g in range(groups):
            part = t_dot(left[g][...], rights[n * groups + g][...])
            total = part if total is None else total + part
        outs[n][...] = total.astype(BF)


def weight_grads(lefts, rights, left_index, right_index):
    groups, count = len(lefts), len(rights)

    def tiled(array, index, tile):
        if array.ndim == 3:
            return pl.BlockSpec((None, array.shape[1], tile), lambda d: (index, 0, d))
        return pl.BlockSpec((array.shape[0], tile), lambda d: (0, d))

    def fixed(array, index):
        if array.ndim == 3:
            return pl.BlockSpec((None,) + array.shape[1:], lambda d: (index, 0, 0))
        return pl.BlockSpec(array.shape, lambda d: (0, 0))

    tall = lefts[0].shape[-1]
    wide = rights[0][0].shape[-1]
    tile = 256
    flat = [r for one in rights for r in one]
    total_rows = sum(a.shape[-2] for a in lefts)
    return pl.pallas_call(
        functools.partial(weight_grads_body, groups, count),
        grid=(tall // tile,),
        in_specs=[tiled(a, left_index, tile) for a in lefts] + [fixed(a, right_index) for a in flat],
        out_specs=[pl.BlockSpec((tile, wide), lambda d: (d, 0))] * count,
        out_shape=[jax.ShapeDtypeStruct((tall, wide), BF)] * count,
        compiler_params=params(48),
        cost_estimate=cost(
            2 * count * total_rows * tall * wide,
            2 * total_rows * (tall + count * wide) + 2 * count * tall * wide,
        ),
    )(*lefts, *flat)


def swap_core(value):
    return lax.ppermute(value, "shard", [(i, i ^ 1) for i in range(4)])


def swap_x(value):
    return lax.ppermute(value, "shard", [(i, i ^ 2) for i in range(4)])


def shard_order(position):
    return [position, position ^ 1, position ^ 2, position ^ 3]


def shard_gather(value):
    far = swap_x(value)
    near = swap_core(value)
    return [value, near, far, swap_core(far)]


def added(*terms):
    total = terms[0].astype(F32)
    for term in terms[1:]:
        total = total + term.astype(F32)
    return total


def shard_reduce(blocks):
    far = added(blocks[2], swap_core(blocks[3])).astype(BF)
    far = swap_x(far)
    near = added(blocks[0], swap_core(blocks[1]))
    return near + far.astype(F32)


def ring_next(count):
    return [(z * 2 + y, ((z + 1) % (count // 2)) * 2 + y) for z in range(count // 2) for y in range(2)]


def swap_y(value, count):
    return lax.ppermute(value, "rep", [(i, i ^ 1) for i in range(count)])


def turn_z(value, count):
    return lax.ppermute(value, "rep", ring_next(count))


def rep_order(rep, count):
    planes = count // 2
    z, y = rep // 2, rep % 2
    return [((z + planes - k) % planes) * 2 + (y ^ w) for k in range(planes) for w in range(2)]


def turn_and_cross(value, count):
    return together(turn_z(value, count), swap_y(value, count))


def last_crossing(held, before, count):
    half = held.shape[0] // 2
    return jnp.concatenate(together(swap_y(held[:half], count), turn_z(before[half:], count)), axis=0)


def rep_gather(value, count, ties=None):
    blocks = []
    held = value
    for k in range(count // 2):
        held = after(held, *(ties or {}).get(k, ()))
        if k < count // 2 - 1:
            nexts, crossed = together(turn_z(held, count), swap_y(held, count))
        else:
            nexts, crossed = None, last_crossing(held, blocks[-1], count)
        blocks += [held, crossed]
        held = nexts
    return blocks


class RepReduce:
    def __init__(self, blocks, count, *ready, split=False):
        self.blocks, self.count = list(blocks), count
        self.order = list(range(2, count // 2)) + [0]
        self.half = blocks[3].shape[0] // 2 if split else None
        first = after(blocks[3], *ready)
        if split:
            self.arrived = together(
                swap_y(first[: self.half], count), turn_z(first[self.half :], count)
            )
        else:
            self.arrived = (swap_y(first, count),)
        self.total = None
        self.k = 1

    def step(self, *ready):
        arrived = together(*self.arrived, *ready)[: len(self.arrived)]
        if self.half is not None and self.k == 1:
            half, (near, far) = self.half, arrived
            total = self.blocks[2].at[:half].add(near)
            self.blocks[5] = self.blocks[5].at[half:].add(far)
        else:
            total = added(self.blocks[2 * self.k], *arrived)
        if not self.order:
            return total
        self.k = self.order.pop(0)
        self.sent = total.astype(BF)
        self.arrived = together(
            swap_y(after(self.blocks[2 * self.k + 1], arrived[0]), self.count),
            turn_z(self.sent, self.count),
        )
        return None


def rep_reduce(blocks, count, *ready):
    reduce = RepReduce(blocks, count, *ready)
    while True:
        total = reduce.step()
        if total is not None:
            return total


def write_sums_body(blocks, ids_ref, wq_ref, wk_ref, wv_ref, gain_ref, *refs):
    in_refs, (q_ref, k_ref, v_ref, o_ref, extra_ref) = refs[:blocks], refs[-5:]
    width = q_ref.shape[1]
    heads = width // HD
    for i in range(blocks):

        @pl.when(pl.program_id(0) == i)
        def _(i=i):
            ref = in_refs[i]
            attn = None
            for m, (out, weight) in enumerate(((q_ref, wq_ref), (k_ref, wk_ref), (v_ref, wv_ref))):
                for h in range(heads):
                    start = (3 * h + m) * HD
                    piece = ref[:, start : start + HD].astype(F32)
                    out[:, h * HD : (h + 1) * HD] = piece
                    term = piece * weight[:, h * HD : (h + 1) * HD].astype(F32)
                    attn = term if attn is None else attn + term
            o_ref[...] = ref[:, 3 * width : 4 * width].astype(F32)
            extra = ref[:, 4 * width :].astype(F32)
            attn = jnp.sum(attn, axis=1, keepdims=True) / gain_ref[...]
            lane = lax.broadcasted_iota(jnp.int32, extra.shape, 1)
            extra_ref[...] = jnp.where(lane == extra.shape[1] - 1, attn, extra)


def write_sums(ids, w_query, w_key, w_value, gain, gathered, held=()):
    blocks = len(gathered)
    part, total = gathered[0].shape
    rows, width = w_query.shape
    own = pl.BlockSpec((part, width), lambda b, n: (n[b], 0))
    extra = pl.BlockSpec((part, HD), lambda b, n: (n[b], 0))
    big = jax.ShapeDtypeStruct((rows, width), F32)
    return pl.pallas_call(
        functools.partial(write_sums_body, blocks),
        grid_spec=pltpu.PrefetchScalarGridSpec(
            num_scalar_prefetch=1,
            grid=(blocks,),
            in_specs=[own, own, own, pl.BlockSpec((part, 1), lambda b, n: (n[b], 0))]
            + [pl.BlockSpec((part, total), lambda b, n: (0, 0))] * blocks
            + [pl.BlockSpec(memory_space=pl.ANY)] * len(held),
            out_specs=[own, own, own, own, extra],
        ),
        out_shape=[big, big, big, big, jax.ShapeDtypeStruct((rows, HD), F32)],
        input_output_aliases={5 + blocks + i: i for i in range(len(held))},
        compiler_params=params(52),
        cost_estimate=cost(0, blocks * part * width * 30),
    )(ids, w_query, w_key, w_value, gain, *gathered, *held)


def on_device(
    tokens,
    w_query,
    w_key,
    w_value,
    w_out,
    w_router,
    norm_attn,
    norm_ffn,
    norm_query,
    norm_key,
    w_gate,
    w_up,
    w_down,
    segments,
    routes,
    cotangent,
):
    rows_count, width = tokens.shape
    experts = w_router.shape[1]
    local_experts = w_gate.shape[0]
    rep_count = lax.axis_size("rep")
    shard_count = lax.axis_size("shard")
    position = lax.axis_index("shard")
    rep = lax.axis_index("rep")
    length = rows_count * shard_count
    capacity = max(2, rows_count * TOP * 9 // (8 * experts))
    capacity = -(-capacity // 16) * 16
    rows = w_query.shape[0]
    order = rep_order(rep, rep_count)
    order_in = shard_order(position)
    group_size = 4

    order_array = jnp.stack(order)
    order_in_array = jnp.stack(order_in)
    part = rows // rep_count
    core = position % 2

    far = packed_part(
        jnp.stack([rep, 1 - position // 2]), w_query, w_key, w_value, shard_count, part
    )
    far = swap_x(far)
    far_tokens = swap_x(tokens)
    grad_blocks = [cotangent]
    grad_held, crossed = turn_and_cross(grad_blocks[0], rep_count)
    grad_blocks += [crossed, grad_held]
    full_gate = lax.all_gather(after(w_gate, far, far_tokens, grad_held), "shard", axis=1, tiled=True)
    far = jnp.stack(
        [
            lax.dynamic_index_in_dim(far, core, 0, keepdims=False),
            swap_core(lax.dynamic_index_in_dim(far, 1 - core, 0, keepdims=False)),
        ]
    )
    expert_ids = jnp.arange(experts, dtype=jnp.int32)
    named_own = jnp.any(routes[:, :, None] == expert_ids, axis=1)
    names = jnp.pad(named_own.T.astype(BF), ((0, 0), (0, far.shape[2] - rows_count)))
    names = jnp.stack([names, names])
    full_up = lax.all_gather(
        after(w_up, far, far_tokens, grad_held), "shard", axis=1, tiled=True
    )
    fars = rep_gather(jnp.concatenate([far, names], axis=1), rep_count)
    packed = packed_columns(after(w_query, fars[1]), w_key, w_value, shard_count)
    near = swap_core(lax.dynamic_index_in_dim(packed, position ^ 1, 0, keepdims=False))
    token_blocks = [tokens, swap_core(tokens), far_tokens, swap_core(far_tokens)]
    small = jnp.concatenate(
        [
            w_router,
            norm_attn[:, None],
            norm_ffn[:, None],
            jnp.pad(norm_query, (0, rows - norm_query.shape[0]))[:, None],
            jnp.pad(norm_key, (0, rows - norm_key.shape[0]))[:, None],
        ],
        axis=1,
    )
    small = jnp.pad(small, ((0, 0), (0, HD - small.shape[1])))
    small = jnp.stack(shard_gather(small))
    small = jnp.zeros_like(small).at[order_in_array].set(small)
    head_gains = small[:, : norm_query.shape[0], experts + 2 : experts + 4].astype(F32)
    gain_query = head_gains[:, :, 0].reshape(1, HD)
    gain_key = head_gains[:, :, 1].reshape(1, HD)
    small = small.reshape(width, HD)
    gain_attn = small[:, experts].astype(F32)
    gain_ffn = small[:, experts + 1].astype(F32)
    full_router = small[:, :experts]

    input_b, columns, qkv = project(
        order_array, order_in_array, gain_attn[None, :], packed, near, token_blocks, fars
    )
    places = jnp.concatenate([p * rows_count + jnp.arange(rows_count, dtype=jnp.int32) for p in order_in])
    inverse = THETA ** (-jnp.arange(HD // 2, dtype=F32) * 2.0 / HD)
    angles = places.astype(F32)[:, None] * inverse[None, :]
    cosine, sine = jnp.cos(angles), jnp.sin(angles)
    cosine = jnp.concatenate([cosine, cosine], axis=-1)
    sine = jnp.concatenate([-sine, sine], axis=-1)
    segment_all = jnp.concatenate(
        [lax.dynamic_slice_in_dim(segments[0], p * rows_count, rows_count) for p in order_in]
    )
    attn_args = (cosine, sine, gain_query, gain_key, segment_all[:, None], segment_all[None, :])
    mixed_b = attention_forward(qkv, attn_args)
    planes = rep_count // 2
    for k in range(1, planes - 1):
        grad_held, crossed = turn_and_cross(after(grad_held, fars[-1]), rep_count)
        grad_blocks += [crossed, grad_held]
        if k == 1:
            mixed_b = after(mixed_b, grad_held)
    projected = dot(mixed_b, w_out).astype(BF)
    projected = [projected[i * rows_count : (i + 1) * rows_count] for i in range(shard_count)]
    tokens_f = tokens.astype(F32)
    attended = shard_reduce(projected)
    full_down = lax.all_gather(
        after(w_down, attended, grad_held), "shard", axis=1, tiled=True
    )
    hidden_state = tokens_f + attended

    scale_mid = rms_scale(hidden_state)
    normed_mid = hidden_state * scale_mid
    mid_b = (normed_mid * gain_ffn).astype(BF)
    first_expert = rep * local_experts
    slot_lanes, slots, named_lanes = read_names(
        first_expert[None], fars, experts, local_experts, rows_count
    )
    router_lanes = jnp.pad(full_router, ((0, 0), (0, HD - experts)))
    number = jnp.stack([first_expert, jnp.int32(experts)])
    picked, groups = [], []
    mid_b = after(mid_b, grad_held, slots, slot_lanes, named_lanes)

    def pick_next(block):
        b = len(picked)
        place = b % group_size
        held = picked[-1][:2] if place else None
        picked.append(
            pick(
                number,
                slot_lanes,
                named_lanes,
                router_lanes,
                block,
                grad_blocks[b],
                held,
                b,
                place,
                group_size,
                capacity,
            )
        )
        if place == group_size - 1:
            x, dy = [
                a.reshape(local_experts, group_size * capacity, width) for a in picked[-1][:2]
            ]
            groups.append((x, dy))

    def run_group(group, *others):
        x, dy = groups[group]
        done = run_experts(after(x, *others), dy, full_gate, full_up, full_down)
        groups[group] = (x, dy, done)
        return done[0]

    def merge_grads(group):
        return merge_rows(slots, group * group_size, groups[group][2][1], group_size)

    def merge_group(group, *ready):
        members = slice(group * group_size, (group + 1) * group_size)
        *parts, dgate = merge_results(
            after(slots, *ready),
            group * group_size,
            [p[2] for p in picked[members]],
            grad_blocks[members],
            groups[group][2][0],
        )
        return parts, dgate

    held, crossed = mid_b, None
    for k in range(planes):
        if k > 0:
            held, x = together(held, picked[-1][0])
            picked[-1] = (x,) + picked[-1][1:]
        if k < planes - 1:
            nexts, crossing = turn_and_cross(held, rep_count)
        else:
            nexts, crossing = None, last_crossing(held, crossed, rep_count)
        if k > 0:
            pick_next(crossed)
        pick_next(held)
        held, crossed = nexts, crossing
    grad_blocks.append(swap_y(after(grad_held, crossed), rep_count))
    grad_parts, result_parts, dgate_parts = [], [], []
    last = rep_count // group_size - 1
    ready = ()
    for g in range(last):
        run_group(g, *ready)
        grad_parts += merge_grads(g)
        ready = (grad_parts[-1],)
    cross_first = swap_y(grad_parts[3], rep_count)
    cross_zero = swap_y(grad_parts[1], rep_count)
    pick_next(after(crossed, *ready))
    y = run_group(last)
    cross_first, cross_zero, y = together(cross_first, cross_zero, y)
    total = turn_z(added(grad_parts[2], cross_first).astype(BF), rep_count)
    grad_parts += merge_grads(last)
    arrived = swap_y(grad_parts[5], rep_count)
    for g in range(last + 1):
        parts, dgate = merge_group(g, grad_parts[-1])
        result_parts += parts
        dgate_parts.append(dgate)

    def owned_part(grad):
        return lax.psum_scatter(grad, "shard", scatter_dimension=0, tiled=True)

    def wide_grads(j, *others):
        return weight_grads(
            [after(g[0], *others) for g in groups],
            [[g[2][3] for g in groups], [g[2][4] for g in groups]],
            j,
            j,
        )

    def down_grads(j, *others):
        return weight_grads(
            [after(g[2][2], *others) for g in groups], [[g[1] for g in groups]], j, j
        )[0]

    arrived = after(arrived, *result_parts, *dgate_parts)
    dgates = jnp.swapaxes(jnp.concatenate(dgate_parts), 1, 2)
    dgates = jnp.zeros_like(dgates).at[order_array].set(dgates)
    made = []
    for k in range(2, planes):
        total = added(grad_parts[2 * k], arrived, total).astype(BF)
        if k == 2:
            total, dgates = together(total, dgates)
        if k < planes - 1:
            total, arrived = together(
                turn_z(total, rep_count), swap_y(after(grad_parts[2 * k + 3], arrived), rep_count)
            )
            if not made:
                made.append(wide_grads(0, grad_parts[-1], *result_parts))
                total, arrived = together(total, arrived, *made[0])[:2]
        else:
            sent = total
            total = turn_z(total, rep_count)
            while len(made) < local_experts:
                made.append(wide_grads(len(made), sent))
                total = together(total, *made[-1])[0]
    results_sum = RepReduce(result_parts, rep_count, arrived)
    total = after(total, *results_sum.arrived)
    grad_mid_moe = added(grad_parts[0], cross_zero, total)

    dgates = lax.all_to_all(dgates, "rep", split_axis=0, concat_axis=0, tiled=True)
    dgates = dgates.reshape(experts, rows_count).T
    logits = dot(mid_b, full_router)
    exps = jnp.exp(logits - jnp.max(logits, axis=-1, keepdims=True))
    probs_own = exps / jnp.sum(exps, axis=-1, keepdims=True)
    chosen_total = jnp.sum(jnp.where(named_own, probs_own, 0.0), axis=1, keepdims=True)
    gates_own = jnp.where(named_own, probs_own, 0.0) / chosen_total
    grad_probs = jnp.where(
        named_own, dgates - jnp.sum(dgates * gates_own, axis=1, keepdims=True), 0.0
    ) / chosen_total
    grad_logits = (
        probs_own * (grad_probs - jnp.sum(probs_own * grad_probs, axis=1, keepdims=True))
    ).astype(BF)
    grad_mid = grad_mid_moe + dot_t(grad_logits, full_router)
    grad_gain_ffn = jnp.sum(grad_mid * normed_mid, axis=0)
    grad_router = t_dot(mid_b, grad_logits)
    grad_out = cotangent.astype(F32)
    grad_state = grad_out + norm_back(grad_mid * gain_ffn, normed_mid, scale_mid)
    grad_state_b = grad_state.astype(BF)

    far_state = swap_x(grad_state_b)
    while len(results_sum.order) > 2:
        results_sum.step()
    downs = [down_grads(j, grad_state_b) for j in range(local_experts)]
    far_state, *both = together(far_state, *results_sum.arrived, *downs)
    results_sum.arrived, downs = tuple(both[:2]), both[2:]
    state_blocks = [grad_state_b, swap_core(grad_state_b), far_state, swap_core(far_state)]
    grad_state_all = jnp.concatenate(state_blocks, axis=0)
    grad_mixed = dot_t(grad_state_all, w_out).astype(BF)
    heads = qkv.shape[1] // (3 * HD)
    results_sum.step()
    grad_qkv, grad_head_gains = attention_backward(qkv, grad_mixed, attn_args, 0, heads)
    grad_qkv, *results_sum.arrived = together(grad_qkv, *results_sum.arrived)
    grad_columns = t_dot(input_b, grad_qkv).astype(BF)
    grad_out_proj = t_dot(mixed_b, grad_state_all).astype(BF)
    grad_input = dot_t(after(grad_qkv, grad_columns), columns).astype(BF)
    grad_input = shard_reduce(
        [grad_input[i * rows_count : (i + 1) * rows_count] for i in range(shard_count)]
    )
    normed_in = tokens_f * rms_scale(tokens_f)
    tokens_grad = (
        grad_state + norm_back(grad_input * gain_attn, normed_in, rms_scale(tokens_f))
    ).astype(BF)
    sums_gate = [owned_part(after(m[0], grad_mixed)) for m in made]
    sums_up = [owned_part(after(m[1], grad_mixed)) for m in made]

    piece = HD // shard_count
    head_columns = jnp.pad(
        grad_head_gains[:2].reshape(2, shard_count, piece), ((0, 0), (0, 0), (0, rows - piece))
    ).reshape(2, width)
    extras = jnp.concatenate(
        [grad_router, grad_gain_ffn[:, None], head_columns.T], axis=1
    )
    extras = jnp.pad(extras, ((0, 0), (0, HD - extras.shape[1]))).astype(BF)
    out_columns = jnp.swapaxes(grad_out_proj.reshape(rows, shard_count, -1), 0, 1)
    out_columns = out_columns.reshape(shard_count, rep_count, part, -1)
    column_parts = grad_columns.reshape(shard_count, rep_count, part, -1)
    extra_parts = extras.reshape(shard_count, rep_count, part, -1)
    to_sum = jnp.concatenate([column_parts, extra_parts, out_columns], axis=3)
    to_sum = [lax.dynamic_index_in_dim(to_sum, r, axis=1, keepdims=False) for r in order]
    sums = RepReduce(to_sum, rep_count, split=True)
    expert_sum = None
    while expert_sum is None:
        expert_sum = results_sum.step()
    sums_down = [owned_part(after(d, grad_mixed)) for d in downs]
    part_sum = None
    while part_sum is None:
        part_sum = sums.step()
    part_sum = part_sum.astype(BF)
    output = (hidden_state + expert_sum).astype(BF)
    grad_gate = jnp.stack(sums_gate).astype(F32)
    grad_up = jnp.stack(sums_up).astype(F32)
    grad_down = jnp.stack(sums_down).astype(F32)
    split = grad_columns.shape[1] + HD
    mine = lax.all_to_all(part_sum[:, :, :split], "shard", split_axis=0, concat_axis=0, tiled=True)
    wide = jnp.swapaxes(mine[:, :, : split - HD], 0, 1).reshape(part, -1)
    extra = jnp.sum(mine[:, :, split - HD :].astype(F32), axis=0).astype(BF)
    out_part = jnp.swapaxes(part_sum[:, :, split:], 0, 1).reshape(part, -1)
    gathered = rep_gather(
        jnp.concatenate([wide, out_part, extra], axis=1),
        rep_count,
        {2: (grad_gate, grad_up, output), 3: (grad_down, tokens_grad)},
    )
    gain_rows = norm_attn.astype(F32)[:, None]
    most = rep_count - 1
    held = write_sums(order_array[:most], w_query, w_key, w_value, gain_rows, gathered[:most])
    sum_query, sum_key, sum_value, sum_out, extra = write_sums(
        order_array[most:], w_query, w_key, w_value, gain_rows, gathered[most:], held
    )
    return (
        output,
        tokens_grad,
        sum_query,
        sum_key,
        sum_value,
        sum_out,
        extra[:, :experts],
        extra[:, HD - 1],
        extra[:, experts],
        extra[:piece, experts + 1],
        extra[:piece, experts + 2],
        grad_gate,
        grad_up,
        grad_down,
    )


def solution(mesh):
    return jax.shard_map(
        on_device,
        mesh=mesh,
        in_specs=(
            P(("rep", "shard"), None),
            P("shard", None),
            P("shard", None),
            P("shard", None),
            P("shard", None),
            P("shard", None),
            P("shard"),
            P("shard"),
            P("shard"),
            P("shard"),
            P("rep", "shard", None),
            P("rep", "shard", None),
            P("rep", "shard", None),
            P("rep", None),
            P(("rep", "shard"), None),
            P(("rep", "shard"), None),
        ),
        out_specs=(
            P(("rep", "shard"), None),
            P(("rep", "shard"), None),
            P("shard", None),
            P("shard", None),
            P("shard", None),
            P("shard", None),
            P("shard", None),
            P("shard"),
            P("shard"),
            P("shard"),
            P("shard"),
            P("rep", "shard", None),
            P("rep", "shard", None),
            P("rep", "shard", None),
        ),
        check_vma=False,
    )
```

```python
import functools

import jax
import jax.numpy as jnp
from jax import lax
from jax.experimental import pallas as pl
from jax.experimental.pallas import tpu as pltpu
from jax.sharding import PartitionSpec as P

HEADS = 16
HD = 128
TOP = 8

EPSILON = 1e-05
THETA = 50000.0
MASKED = -1e30
BF = jnp.bfloat16
F32 = jnp.float32
QCHUNK = 256
VMEM = 58 << 20


def rms_scale(values):
    return lax.rsqrt(jnp.mean(values * values, axis=-1, keepdims=True) + EPSILON)


def norm_back(grad, normed, scale):
    return scale * (grad - normed * jnp.mean(grad * normed, axis=-1, keepdims=True))


def dot(left, right):
    return jnp.dot(left, right, preferred_element_type=F32)


def dot_t(left, right):
    return lax.dot_general(left, right, (((1,), (1,)), ((), ())), preferred_element_type=F32)


def t_dot(left, right):
    return lax.dot_general(left, right, (((0,), (0,)), ((), ())), preferred_element_type=F32)


def params(mib=40):
    return pltpu.CompilerParams(vmem_limit_bytes=mib << 20)


def cost(flops, size, transcendentals=0):
    return pl.CostEstimate(
        flops=int(flops), bytes_accessed=int(size), transcendentals=int(transcendentals)
    )


def after(value, *others):
    return lax.optimization_barrier((value,) + others)[0]


def together(*values):
    return lax.optimization_barrier(values)


def pack_columns(q_ref, k_ref, v_ref, out_ref):
    for h in range(q_ref.shape[1] // HD):
        for m, ref in enumerate((q_ref, k_ref, v_ref)):
            start = (3 * h + m) * HD
            out_ref[0, :, start : start + HD] = ref[:, h * HD : (h + 1) * HD]


def packed_columns(w_query, w_key, w_value, shards):
    rows, width = w_query.shape
    part = width // shards
    spec = pl.BlockSpec((rows, part), lambda s: (0, s))
    return pl.pallas_call(
        pack_columns,
        grid=(shards,),
        in_specs=[spec, spec, spec],
        out_specs=pl.BlockSpec((1, rows, 3 * part), lambda s: (s, 0, 0)),
        out_shape=jax.ShapeDtypeStruct((shards, rows, 3 * part), BF),
        compiler_params=params(),
        cost_estimate=cost(0, 12 * rows * width),
    )(w_query, w_key, w_value)


def pack_part(place_ref, q_ref, k_ref, v_ref, out_ref):
    pack_columns(q_ref, k_ref, v_ref, out_ref)


def packed_part(place, w_query, w_key, w_value, shards, part):
    width = w_query.shape[1] // shards
    spec = pl.BlockSpec((part, width), lambda s, n: (n[0], 2 * n[1] + s))
    return pl.pallas_call(
        pack_part,
        grid_spec=pltpu.PrefetchScalarGridSpec(
            num_scalar_prefetch=1,
            grid=(2,),
            in_specs=[spec, spec, spec],
            out_specs=pl.BlockSpec((1, part, 3 * width), lambda s, n: (s, 0, 0)),
        ),
        out_shape=jax.ShapeDtypeStruct((2, part, 3 * width), BF),
        compiler_params=params(58),
        cost_estimate=cost(0, 24 * part * width),
    )(place, w_query, w_key, w_value)


def project_body(parts, order_ref, shard_ref, gain_ref, packed_ref, near_ref, *refs):
    token_refs, far_refs = refs[:4], refs[4 : 4 + parts]
    input_ref, columns_ref, qkv_ref, sem = refs[4 + parts :]
    rows = near_ref.shape[0]
    count = token_refs[0].shape[0]
    part = rows // parts

    def place(start, size):
        return columns_ref.at[pl.ds(pl.multiple_of(start, 16), size)]

    copies = [
        pltpu.make_async_copy(packed_ref.at[shard_ref[0]], place(shard_ref[0] * rows, rows), sem.at[0]),
        pltpu.make_async_copy(near_ref, place(shard_ref[1] * rows, rows), sem.at[1]),
    ]
    for i in range(parts):
        for m in range(2):
            start = shard_ref[2 + m] * rows + order_ref[i] * part
            copies.append(
                pltpu.make_async_copy(
                    far_refs[i].at[m, pl.ds(0, part)], place(start, part), sem.at[2 + 2 * i + m]
                )
            )
    for copy in copies:
        copy.start()
    for i in range(4):
        x = token_refs[i][...].astype(F32)
        input_ref[i * count : (i + 1) * count, :] = (x * rms_scale(x) * gain_ref[...]).astype(BF)
    for copy in copies:
        copy.wait()

    def step(i, carry):
        r = pl.ds(pl.multiple_of(i * count, count), count)
        qkv_ref[r, :] = dot(input_ref[r, :], columns_ref[...])
        return carry

    lax.fori_loop(0, 4, step, 0)


def project(order, shards, gain, packed, near, token_blocks, fars):
    count, width = token_blocks[0].shape
    columns = near.shape[1]
    length = count * len(token_blocks)
    anywhere = pl.BlockSpec(memory_space=pl.ANY)
    whole = lambda *shape: pl.BlockSpec(shape, lambda i, a, b: (0, 0))
    return pl.pallas_call(
        functools.partial(project_body, len(fars)),
        grid_spec=pltpu.PrefetchScalarGridSpec(
            num_scalar_prefetch=2,
            grid=(1,),
            in_specs=[whole(1, width), anywhere, anywhere]
            + [whole(count, width)] * 4
            + [anywhere] * len(fars),
            out_specs=[whole(length, width), whole(width, columns), whole(length, columns)],
            scratch_shapes=[pltpu.SemaphoreType.DMA((2 + 2 * len(fars),))],
        ),
        out_shape=[
            jax.ShapeDtypeStruct((length, width), BF),
            jax.ShapeDtypeStruct((width, columns), BF),
            jax.ShapeDtypeStruct((length, columns), F32),
        ],
        compiler_params=params(56),
        cost_estimate=cost(
            2 * length * width * columns, 4 * length * width + 4 * width * columns + 4 * length * columns
        ),
    )(order, shards, gain, packed, near, *token_blocks, *fars)


def turned(values, cosine, sine):
    return values * cosine + pltpu.roll(values, HD // 2, 1) * sine


def turned_back(grad, cosine, sine):
    return grad * cosine - pltpu.roll(grad, HD // 2, 1) * sine


def weights_of(qb, keys, seg_column, seg_row):
    scores = dot_t(qb, keys) * (HD**-0.5)
    scores = jnp.where(seg_column == seg_row, scores, MASKED)
    shifted = jnp.exp(scores - jnp.max(scores, axis=-1, keepdims=True))
    return shifted * (1.0 / jnp.sum(shifted, axis=-1, keepdims=True))


def attend_forward(qkv_ref, cos_ref, sin_ref, gq_ref, gk_ref, segc_ref, segr_ref, o_ref, kb_ref, vb_ref):
    length = qkv_ref.shape[0]
    k_raw = qkv_ref[:, HD : 2 * HD]
    kb_ref[...] = turned(k_raw * rms_scale(k_raw) * gk_ref[...], cos_ref[...], sin_ref[...]).astype(BF)
    vb_ref[...] = qkv_ref[:, 2 * HD :].astype(BF)

    def step(i, carry):
        rows = pl.ds(pl.multiple_of(i * QCHUNK, QCHUNK), QCHUNK)
        q_raw = qkv_ref[rows, :HD]
        qb = turned(q_raw * rms_scale(q_raw) * gq_ref[...], cos_ref[rows, :], sin_ref[rows, :]).astype(BF)
        probs = weights_of(qb, kb_ref[...], segc_ref[rows, :], segr_ref[...])
        o_ref[rows, :] = dot(probs.astype(BF), vb_ref[...]).astype(BF)
        return carry

    lax.fori_loop(0, length // QCHUNK, step, 0)


def attend_backward(
    qkv_ref,
    do_ref,
    cos_ref,
    sin_ref,
    gq_ref,
    gk_ref,
    segc_ref,
    segr_ref,
    *refs,
):
    grad_ref, gains_ref, kb_ref, vb_ref, dk_acc, dv_acc = refs[-6:]
    length = qkv_ref.shape[0]
    scale = HD**-0.5

    @pl.when(pl.program_id(0) == 0)
    def _():
        gains_ref[...] = jnp.zeros_like(gains_ref)

    k_raw = qkv_ref[:, HD : 2 * HD]
    kb_ref[...] = turned(k_raw * rms_scale(k_raw) * gk_ref[...], cos_ref[...], sin_ref[...]).astype(BF)
    vb_ref[...] = qkv_ref[:, 2 * HD :].astype(BF)
    dk_acc[...] = jnp.zeros_like(dk_acc)
    dv_acc[...] = jnp.zeros_like(dv_acc)

    def step(i, carry):
        rows = pl.ds(pl.multiple_of(i * QCHUNK, QCHUNK), QCHUNK)
        cosine, sine = cos_ref[rows, :], sin_ref[rows, :]
        q_raw = qkv_ref[rows, :HD]
        q_scale = rms_scale(q_raw)
        q_norm = q_raw * q_scale
        qb = turned(q_norm * gq_ref[...], cosine, sine).astype(BF)
        probs = weights_of(qb, kb_ref[...], segc_ref[rows, :], segr_ref[...])
        grad_o = do_ref[rows, :]
        grad_probs = dot_t(grad_o, vb_ref[...])
        dv_acc[...] += t_dot(probs.astype(BF), grad_o)
        weighted = probs * grad_probs
        grad_scores = (weighted - probs * jnp.sum(weighted, axis=-1, keepdims=True)).astype(BF)
        dk_acc[...] += t_dot(grad_scores, qb)
        eq = turned_back(dot(grad_scores, kb_ref[...]) * scale, cosine, sine)
        gains_ref[0:1, :] += jnp.sum(eq * q_norm, axis=0, keepdims=True)
        grad_ref[rows, :HD] = norm_back(eq * gq_ref[...], q_norm, q_scale).astype(BF)
        return carry

    lax.fori_loop(0, length // QCHUNK, step, 0)
    ek = turned_back(dk_acc[...] * scale, cos_ref[...], sin_ref[...])
    k_raw = qkv_ref[:, HD : 2 * HD]
    k_scale = rms_scale(k_raw)
    k_norm = k_raw * k_scale
    gains_ref[1:2, :] += jnp.sum(ek * k_norm, axis=0, keepdims=True)
    grad_ref[:, HD : 2 * HD] = norm_back(ek * gk_ref[...], k_norm, k_scale).astype(BF)
    grad_ref[:, 2 * HD :] = dv_acc[...].astype(BF)


def attention_specs(length):
    table = pl.BlockSpec((length, HD), lambda h: (0, 0))
    gain = pl.BlockSpec((1, HD), lambda h: (0, 0))
    column = pl.BlockSpec((length, 1), lambda h: (0, 0))
    row = pl.BlockSpec((1, length), lambda h: (0, 0))
    return [table, table, gain, gain, column, row]


def attention_forward(qkv, attn_args):
    length = qkv.shape[0]
    heads = qkv.shape[1] // (3 * HD)
    return pl.pallas_call(
        attend_forward,
        grid=(heads,),
        in_specs=[pl.BlockSpec((length, 3 * HD), lambda h: (0, h))] + attention_specs(length),
        out_specs=pl.BlockSpec((length, HD), lambda h: (0, h)),
        out_shape=jax.ShapeDtypeStruct((length, heads * HD), BF),
        scratch_shapes=[pltpu.VMEM((length, HD), BF)] * 2,
        compiler_params=params(58),
        cost_estimate=cost(16 * heads * length * length * HD, qkv.size * 5, heads * length * length),
    )(qkv, *attn_args)


def attention_backward(qkv, grad_o, attn_args, first, heads, held=None):
    length = qkv.shape[0]
    wide = pl.BlockSpec((length, 3 * HD), lambda h: (0, first + h))
    return pl.pallas_call(
        attend_backward,
        grid=(heads,),
        in_specs=[wide, pl.BlockSpec((length, HD), lambda h: (0, first + h))]
        + attention_specs(length)
        + [pl.BlockSpec(memory_space=pl.ANY)] * (held is not None),
        out_specs=[wide, pl.BlockSpec((8, HD), lambda h: (0, 0))],
        out_shape=[
            jax.ShapeDtypeStruct(qkv.shape, BF),
            jax.ShapeDtypeStruct((8, HD), F32),
        ],
        scratch_shapes=[pltpu.VMEM((length, HD), BF)] * 2 + [pltpu.VMEM((length, HD), F32)] * 2,
        input_output_aliases={} if held is None else {8: 0},
        compiler_params=params(58),
        cost_estimate=cost(40 * heads * length * length * HD, qkv.size * 3, heads * length * length),
    )(qkv, grad_o, *attn_args, *(() if held is None else (held,)))


def read_names_body(experts, local, first_ref, *refs):
    name_refs, (lanes_ref, slots_ref, named_ref) = refs[:-3], refs[-3:]
    count = lanes_ref.shape[2]
    row = lax.broadcasted_iota(jnp.int32, (count, count), 0)
    column = lax.broadcasted_iota(jnp.int32, (count, count), 1)
    earlier = (row < column).astype(BF)
    expert_row = lax.broadcasted_iota(jnp.int32, (experts, count), 0)
    for b, ref in enumerate(name_refs):
        named = ref[0, ref.shape[1] - experts :, :]
        slots = jnp.where(named > 0, dot(named, earlier), -1.0)
        mine = [
            jnp.sum(jnp.where(expert_row == first_ref[0] + j, slots, 0.0), axis=0, keepdims=True)
            for j in range(local)
        ]
        mine = jnp.concatenate(mine, axis=0)
        lanes_ref[b] = mine.astype(jnp.int32)
        filled = jnp.concatenate([mine, jnp.zeros((HD - local, count), F32)], axis=0)
        slots_ref[b] = filled.T.astype(jnp.int32)
        filled = jnp.concatenate([named.astype(F32), jnp.zeros((HD - experts, count), F32)], axis=0)
        named_ref[b] = filled.T


def read_names(first, blocks, experts, local, count):
    number, height = len(blocks), blocks[0].shape[1]
    whole = lambda *shape: pl.BlockSpec(shape, lambda i, n: (0, 0, 0))
    return pl.pallas_call(
        functools.partial(read_names_body, experts, local),
        grid_spec=pltpu.PrefetchScalarGridSpec(
            num_scalar_prefetch=1,
            grid=(1,),
            in_specs=[whole(1, height, count)] * number,
            out_specs=[whole(number, local, count), whole(number, count, HD), whole(number, count, HD)],
        ),
        out_shape=[
            jax.ShapeDtypeStruct((number, local, count), jnp.int32),
            jax.ShapeDtypeStruct((number, count, HD), jnp.int32),
            jax.ShapeDtypeStruct((number, count, HD), F32),
        ],
        compiler_params=params(),
        cost_estimate=cost(2 * number * experts * count * count, 10 * number * count * HD),
    )(first, *blocks)


def pick_rows(has_input, number_ref, slots_ref, named_ref, router_ref, x_ref, grad_ref, *refs):
    rows_ref, grad_rows_ref, gates_ref = refs[2 * has_input :]
    experts, capacity = slots_ref.shape[1], rows_ref.shape[2]
    count = x_ref.shape[0]
    x = x_ref[...]
    logits = dot(x, router_ref[...])
    lane = lax.broadcasted_iota(jnp.int32, logits.shape, 1)
    logits = jnp.where(lane < number_ref[1], logits, MASKED)
    exps = jnp.exp(logits - jnp.max(logits, axis=-1, keepdims=True))
    probs = exps / jnp.sum(exps, axis=-1, keepdims=True)
    chosen = jnp.where(named_ref[0] > 0.0, probs, 0.0)
    gates = chosen / jnp.sum(chosen, axis=-1, keepdims=True)
    grad = grad_ref[...].astype(F32)
    wanted = lax.broadcasted_iota(jnp.int32, (capacity, count), 0)
    columns = []
    for j in range(experts):
        gate = jnp.sum(jnp.where(lane == number_ref[0] + j, gates, 0.0), axis=1, keepdims=True)
        hot = (wanted == slots_ref[0, j : j + 1, :]).astype(BF)
        rows_ref[j, 0] = dot(hot, x).astype(BF)
        grad_rows_ref[j, 0] = dot(hot, (grad * gate).astype(BF)).astype(BF)
        columns.append(gate)
    gates_ref[...] = jnp.concatenate(columns, axis=1)


def pick(number, slots, named, router, x, grad, held, block, place, blocks, capacity):
    count, width = x.shape
    experts = slots.shape[1]
    lanes = router.shape[1]
    shape = jax.ShapeDtypeStruct((experts, blocks, capacity, width), BF)
    whole = pl.BlockSpec(memory_space=pl.ANY)
    out = pl.BlockSpec((experts, 1, capacity, width), lambda i, n: (0, place, 0, 0))
    return pl.pallas_call(
        functools.partial(pick_rows, held is not None),
        grid_spec=pltpu.PrefetchScalarGridSpec(
            num_scalar_prefetch=1,
            grid=(1,),
            in_specs=[
                pl.BlockSpec((1, experts, count), lambda i, n: (block, 0, 0)),
                pl.BlockSpec((1, count, lanes), lambda i, n: (block, 0, 0)),
                pl.BlockSpec((width, lanes), lambda i, n: (0, 0)),
                pl.BlockSpec((count, width), lambda i, n: (0, 0)),
                pl.BlockSpec((count, width), lambda i, n: (0, 0)),
            ]
            + [whole, whole] * (held is not None),
            out_specs=[out, out, pl.BlockSpec((count, experts), lambda i, n: (0, 0))],
        ),
        out_shape=[shape, shape, jax.ShapeDtypeStruct((count, experts), F32)],
        input_output_aliases={} if held is None else {6: 0, 7: 1},
        compiler_params=params(58),
        cost_estimate=cost(
            4 * experts * capacity * count * width, 4 * width * (count + experts * capacity)
        ),
    )(number, slots, named, router, x, grad, *(held or ()))


def merge_rows_body(blocks, slots_ref, *refs):
    experts = len(refs) - blocks
    rows_refs, out_refs = refs[:experts], refs[experts:]
    capacity = rows_refs[0].shape[0]
    count = out_refs[0].shape[0]
    place = lax.broadcasted_iota(jnp.int32, (count, capacity), 1)
    total = None
    for j in range(experts):
        hot = (place == slots_ref[0, :, j : j + 1]).astype(BF)
        rows = dot(hot, rows_refs[j][...])
        total = rows if total is None else total + rows
    for i in range(blocks):

        @pl.when(pl.program_id(0) == i)
        def _(i=i):
            out_refs[i][...] = total.astype(BF)


def merge_rows(slots, first, rows, blocks):
    count, lanes = slots.shape[1:]
    experts = rows.shape[0]
    capacity = rows.shape[1] // blocks
    width = rows.shape[2]
    return pl.pallas_call(
        functools.partial(merge_rows_body, blocks),
        grid=(blocks,),
        in_specs=[pl.BlockSpec((1, count, lanes), lambda b: (first + b, 0, 0))]
        + [pl.BlockSpec((None, capacity, width), lambda b, j=j: (j, b, 0)) for j in range(experts)],
        out_specs=[pl.BlockSpec((count, width), lambda b: (0, 0))] * blocks,
        out_shape=[jax.ShapeDtypeStruct((count, width), BF)] * blocks,
        compiler_params=params(58),
        cost_estimate=cost(
            2 * blocks * experts * capacity * count * width,
            2 * blocks * width * (count + experts * capacity),
        ),
    )(slots, *[rows] * experts)


def merge_results_body(blocks, slots_ref, *refs):
    experts = len(refs) - 3 * blocks - 1
    gates_refs, grad_refs, refs = refs[:blocks], refs[blocks : 2 * blocks], refs[2 * blocks :]
    rows_refs, out_refs, dgate_ref = refs[:experts], refs[experts:-1], refs[-1]
    capacity = rows_refs[0].shape[0]
    count = out_refs[0].shape[0]
    place = lax.broadcasted_iota(jnp.int32, (count, capacity), 1)
    for i in range(blocks):

        @pl.when(pl.program_id(0) == i)
        def _(i=i):
            grad = grad_refs[i][...].astype(F32)
            total = None
            dgates = []
            for j in range(experts):
                hot = (place == slots_ref[0, :, j : j + 1]).astype(BF)
                rows = dot(hot, rows_refs[j][...])
                dgates.append(jnp.sum(rows * grad, axis=1, keepdims=True))
                gated = rows * gates_refs[i][:, j : j + 1]
                total = gated if total is None else total + gated
            out_refs[i][...] = total.astype(BF)
            dgate_ref[0] = jnp.concatenate(dgates, axis=1)


def merge_results(slots, first, gates, grads, rows):
    blocks = len(gates)
    count, lanes = slots.shape[1:]
    experts = rows.shape[0]
    capacity = rows.shape[1] // blocks
    width = rows.shape[2]
    tokens = pl.BlockSpec((count, width), lambda b: (0, 0))
    return pl.pallas_call(
        functools.partial(merge_results_body, blocks),
        grid=(blocks,),
        in_specs=[pl.BlockSpec((1, count, lanes), lambda b: (first + b, 0, 0))]
        + [pl.BlockSpec((count, experts), lambda b: (0, 0))] * blocks
        + [tokens] * blocks
        + [pl.BlockSpec((None, capacity, width), lambda b, j=j: (j, b, 0)) for j in range(experts)],
        out_specs=[tokens] * blocks + [pl.BlockSpec((1, count, experts), lambda b: (b, 0, 0))],
        out_shape=[jax.ShapeDtypeStruct((count, width), BF)] * blocks
        + [jax.ShapeDtypeStruct((blocks, count, experts), F32)],
        compiler_params=params(58),
        cost_estimate=cost(
            2 * blocks * experts * capacity * count * width,
            2 * blocks * width * (2 * count + experts * capacity),
        ),
    )(slots, *gates, *grads, *[rows] * experts)


def expert_body(
    sub,
    x_ref,
    dy_ref,
    wg_ref,
    wu_ref,
    wd_ref,
    y_ref,
    dx_ref,
    h_ref,
    dg_ref,
    du_ref,
    y_acc,
    dx_acc,
):
    f = pl.program_id(1)
    last = pl.num_programs(1) - 1

    def step(i, carry):
        r = pl.ds(pl.multiple_of(i * sub, sub), sub)
        x = x_ref[r, :]
        gate = dot(x, wg_ref[...])
        up = dot(x, wu_ref[...])
        grad_hidden = dot_t(dy_ref[r, :], wd_ref[...])
        sigmoid = 1.0 / (1.0 + jnp.exp(-gate))
        activated = gate * sigmoid
        hidden = (activated * up).astype(BF)
        h_ref[r, :] = hidden
        grad_gate = (grad_hidden * up * sigmoid * (1.0 + gate * (1.0 - sigmoid))).astype(BF)
        grad_up = (grad_hidden * activated).astype(BF)
        dg_ref[r, :] = grad_gate
        du_ref[r, :] = grad_up
        y = dot(hidden, wd_ref[...])
        dx = dot_t(grad_gate, wg_ref[...]) + dot_t(grad_up, wu_ref[...])

        @pl.when(f == 0)
        def _():
            y_acc[r, :] = y
            dx_acc[r, :] = dx

        @pl.when((f > 0) & (f < last))
        def _():
            y_acc[r, :] += y
            dx_acc[r, :] += dx

        @pl.when(f == last)
        def _():
            y_ref[r, :] = (y_acc[r, :] + y).astype(BF)
            dx_ref[r, :] = (dx_acc[r, :] + dx).astype(BF)

        return carry

    lax.fori_loop(0, x_ref.shape[0] // sub, step, 0)


def run_experts(x, dy, w_gate, w_up, w_down):
    experts, rows, width = x.shape
    hidden = w_gate.shape[2]
    tile = hidden // 2
    whole = pl.BlockSpec((None, rows, width), lambda j, f: (j, 0, 0))
    part = pl.BlockSpec((None, rows, tile), lambda j, f: (j, 0, f))
    wide = jax.ShapeDtypeStruct((experts, rows, width), BF)
    thin = jax.ShapeDtypeStruct((experts, rows, hidden), BF)
    return pl.pallas_call(
        functools.partial(expert_body, rows // 2),
        grid=(experts, 2),
        in_specs=[
            whole,
            whole,
            pl.BlockSpec((None, width, tile), lambda j, f: (j, 0, f)),
            pl.BlockSpec((None, width, tile), lambda j, f: (j, 0, f)),
            pl.BlockSpec((None, tile, width), lambda j, f: (j, f, 0)),
        ],
        out_specs=[whole, whole, part, part, part],
        out_shape=[wide, wide, thin, thin, thin],
        scratch_shapes=[pltpu.VMEM((rows, width), F32)] * 2,
        compiler_params=params(60),
        cost_estimate=cost(
            12 * experts * rows * width * hidden,
            experts * (8 * rows * width + 6 * rows * hidden + 6 * width * hidden),
            experts * rows * hidden,
        ),
    )(x, dy, w_gate, w_up, w_down)


def weight_grads_body(groups, count, *refs):
    left, rights, outs = refs[:groups], refs[groups : groups + groups * count], refs[-count:]
    for n in range(count):
        total = None
        for g in range(groups):
            part = t_dot(left[g][...], rights[n * groups + g][...])
            total = part if total is None else total + part
        outs[n][...] = total.astype(BF)


def weight_grads(lefts, rights, left_index, right_index):
    groups, count = len(lefts), len(rights)

    def tiled(array, index, tile):
        if array.ndim == 3:
            return pl.BlockSpec((None, array.shape[1], tile), lambda d: (index, 0, d))
        return pl.BlockSpec((array.shape[0], tile), lambda d: (0, d))

    def fixed(array, index):
        if array.ndim == 3:
            return pl.BlockSpec((None,) + array.shape[1:], lambda d: (index, 0, 0))
        return pl.BlockSpec(array.shape, lambda d: (0, 0))

    tall = lefts[0].shape[-1]
    wide = rights[0][0].shape[-1]
    tile = 256
    flat = [r for one in rights for r in one]
    total_rows = sum(a.shape[-2] for a in lefts)
    return pl.pallas_call(
        functools.partial(weight_grads_body, groups, count),
        grid=(tall // tile,),
        in_specs=[tiled(a, left_index, tile) for a in lefts] + [fixed(a, right_index) for a in flat],
        out_specs=[pl.BlockSpec((tile, wide), lambda d: (d, 0))] * count,
        out_shape=[jax.ShapeDtypeStruct((tall, wide), BF)] * count,
        compiler_params=params(58),
        cost_estimate=cost(
            2 * count * total_rows * tall * wide,
            2 * total_rows * (tall + count * wide) + 2 * count * tall * wide,
        ),
    )(*lefts, *flat)


def swap_core(value):
    return lax.ppermute(value, "shard", [(i, i ^ 1) for i in range(4)])


def swap_x(value):
    return lax.ppermute(value, "shard", [(i, i ^ 2) for i in range(4)])


def shard_order(position):
    return [position, position ^ 1, position ^ 2, position ^ 3]


def shard_gather(value):
    far = swap_x(value)
    near = swap_core(value)
    return [value, near, far, swap_core(far)]


def added(*terms):
    total = terms[0].astype(F32)
    for term in terms[1:]:
        total = total + term.astype(F32)
    return total


def shard_reduce(blocks):
    far = added(blocks[2], swap_core(blocks[3])).astype(BF)
    far = swap_x(far)
    near = added(blocks[0], swap_core(blocks[1]))
    return near + far.astype(F32)


def ring_next(count):
    return [(z * 2 + y, ((z + 1) % (count // 2)) * 2 + y) for z in range(count // 2) for y in range(2)]


def swap_y(value, count):
    return lax.ppermute(value, "rep", [(i, i ^ 1) for i in range(count)])


def turn_z(value, count):
    return lax.ppermute(value, "rep", ring_next(count))


def rep_order(rep, count):
    planes = count // 2
    z, y = rep // 2, rep % 2
    return [((z + planes - k) % planes) * 2 + (y ^ w) for k in range(planes) for w in range(2)]


def turn_and_cross(value, count):
    return together(turn_z(value, count), swap_y(value, count))


def last_crossing(held, before, count):
    half = held.shape[0] // 2
    return jnp.concatenate(together(swap_y(held[:half], count), turn_z(before[half:], count)), axis=0)


def rep_gather(value, count, ties=None):
    blocks = []
    held = value
    for k in range(count // 2):
        held = after(held, *(ties or {}).get(k, ()))
        if k < count // 2 - 1:
            nexts, crossed = together(turn_z(held, count), swap_y(held, count))
        else:
            nexts, crossed = None, last_crossing(held, blocks[-1], count)
        blocks += [held, crossed]
        held = nexts
    return blocks


class RepReduce:
    def __init__(self, blocks, count, *ready, split=False):
        self.blocks, self.count = list(blocks), count
        self.order = list(range(2, count // 2)) + [0]
        self.half = blocks[3].shape[0] // 2 if split else None
        first = after(blocks[3], *ready)
        if split:
            self.arrived = together(
                swap_y(first[: self.half], count), turn_z(first[self.half :], count)
            )
        else:
            self.arrived = (swap_y(first, count),)
        self.total = None
        self.k = 1

    def step(self, *ready):
        arrived = together(*self.arrived, *ready)[: len(self.arrived)]
        if self.half is not None and self.k == 1:
            half, (near, far) = self.half, arrived
            total = self.blocks[2].at[:half].add(near)
            self.blocks[5] = self.blocks[5].at[half:].add(far)
        else:
            total = added(self.blocks[2 * self.k], *arrived)
        if not self.order:
            return total
        self.k = self.order.pop(0)
        self.sent = total.astype(BF)
        self.arrived = together(
            swap_y(after(self.blocks[2 * self.k + 1], arrived[0]), self.count),
            turn_z(self.sent, self.count),
        )
        return None


def rep_reduce(blocks, count, *ready):
    reduce = RepReduce(blocks, count, *ready)
    while True:
        total = reduce.step()
        if total is not None:
            return total


def write_sums_body(blocks, ids_ref, wq_ref, wk_ref, wv_ref, gain_ref, *refs):
    in_refs, (q_ref, k_ref, v_ref, o_ref, extra_ref) = refs[:blocks], refs[-5:]
    width = q_ref.shape[1]
    heads = width // HD
    for i in range(blocks):

        @pl.when(pl.program_id(0) == i)
        def _(i=i):
            ref = in_refs[i]
            attn = None
            for m, (out, weight) in enumerate(((q_ref, wq_ref), (k_ref, wk_ref), (v_ref, wv_ref))):
                for h in range(heads):
                    start = (3 * h + m) * HD
                    piece = ref[:, start : start + HD].astype(F32)
                    out[:, h * HD : (h + 1) * HD] = piece
                    term = piece * weight[:, h * HD : (h + 1) * HD].astype(F32)
                    attn = term if attn is None else attn + term
            o_ref[...] = ref[:, 3 * width : 4 * width].astype(F32)
            extra = ref[:, 4 * width :].astype(F32)
            attn = jnp.sum(attn, axis=1, keepdims=True) / gain_ref[...]
            lane = lax.broadcasted_iota(jnp.int32, extra.shape, 1)
            extra_ref[...] = jnp.where(lane == extra.shape[1] - 1, attn, extra)


def write_sums(ids, w_query, w_key, w_value, gain, gathered, held=()):
    blocks = len(gathered)
    part, total = gathered[0].shape
    rows, width = w_query.shape
    own = pl.BlockSpec((part, width), lambda b, n: (n[b], 0))
    extra = pl.BlockSpec((part, HD), lambda b, n: (n[b], 0))
    big = jax.ShapeDtypeStruct((rows, width), F32)
    return pl.pallas_call(
        functools.partial(write_sums_body, blocks),
        grid_spec=pltpu.PrefetchScalarGridSpec(
            num_scalar_prefetch=1,
            grid=(blocks,),
            in_specs=[own, own, own, pl.BlockSpec((part, 1), lambda b, n: (n[b], 0))]
            + [pl.BlockSpec((part, total), lambda b, n: (0, 0))] * blocks
            + [pl.BlockSpec(memory_space=pl.ANY)] * len(held),
            out_specs=[own, own, own, own, extra],
        ),
        out_shape=[big, big, big, big, jax.ShapeDtypeStruct((rows, HD), F32)],
        input_output_aliases={5 + blocks + i: i for i in range(len(held))},
        compiler_params=params(52),
        cost_estimate=cost(0, blocks * part * width * 30),
    )(ids, w_query, w_key, w_value, gain, *gathered, *held)


def on_device(
    tokens,
    w_query,
    w_key,
    w_value,
    w_out,
    w_router,
    norm_attn,
    norm_ffn,
    norm_query,
    norm_key,
    w_gate,
    w_up,
    w_down,
    segments,
    routes,
    cotangent,
):
    rows_count, width = tokens.shape
    experts = w_router.shape[1]
    local_experts = w_gate.shape[0]
    rep_count = lax.axis_size("rep")
    shard_count = lax.axis_size("shard")
    position = lax.axis_index("shard")
    rep = lax.axis_index("rep")
    length = rows_count * shard_count
    capacity = max(2, rows_count * TOP * 9 // (8 * experts))
    capacity = -(-capacity // 16) * 16
    rows = w_query.shape[0]
    order = rep_order(rep, rep_count)
    order_in = shard_order(position)
    group_size = 4

    order_array = jnp.stack(order)
    order_in_array = jnp.stack(order_in)
    part = rows // rep_count
    core = position % 2

    far = packed_part(
        jnp.stack([rep, 1 - position // 2]), w_query, w_key, w_value, shard_count, part
    )
    far = swap_x(far)
    far_tokens = swap_x(tokens)
    grad_blocks = [cotangent]
    grad_held, crossed = turn_and_cross(grad_blocks[0], rep_count)
    grad_blocks += [crossed, grad_held]
    full_gate = lax.all_gather(after(w_gate, far, far_tokens, grad_held), "shard", axis=1, tiled=True)
    far = jnp.stack(
        [
            lax.dynamic_index_in_dim(far, core, 0, keepdims=False),
            swap_core(lax.dynamic_index_in_dim(far, 1 - core, 0, keepdims=False)),
        ]
    )
    expert_ids = jnp.arange(experts, dtype=jnp.int32)
    named_own = jnp.any(routes[:, :, None] == expert_ids, axis=1)
    names = jnp.pad(named_own.T.astype(BF), ((0, 0), (0, far.shape[2] - rows_count)))
    names = jnp.stack([names, names])
    full_up = lax.all_gather(
        after(w_up, far, far_tokens, grad_held), "shard", axis=1, tiled=True
    )
    fars = rep_gather(jnp.concatenate([far, names], axis=1), rep_count)
    packed = packed_columns(after(w_query, fars[1]), w_key, w_value, shard_count)
    near = swap_core(lax.dynamic_index_in_dim(packed, position ^ 1, 0, keepdims=False))
    token_blocks = [tokens, swap_core(tokens), far_tokens, swap_core(far_tokens)]
    small = jnp.concatenate(
        [
            w_router,
            norm_attn[:, None],
            norm_ffn[:, None],
            jnp.pad(norm_query, (0, rows - norm_query.shape[0]))[:, None],
            jnp.pad(norm_key, (0, rows - norm_key.shape[0]))[:, None],
        ],
        axis=1,
    )
    small = jnp.pad(small, ((0, 0), (0, HD - small.shape[1])))
    small = jnp.stack(shard_gather(small))
    small = jnp.zeros_like(small).at[order_in_array].set(small)
    head_gains = small[:, : norm_query.shape[0], experts + 2 : experts + 4].astype(F32)
    gain_query = head_gains[:, :, 0].reshape(1, HD)
    gain_key = head_gains[:, :, 1].reshape(1, HD)
    small = small.reshape(width, HD)
    gain_attn = small[:, experts].astype(F32)
    gain_ffn = small[:, experts + 1].astype(F32)
    full_router = small[:, :experts]

    input_b, columns, qkv = project(
        order_array, order_in_array, gain_attn[None, :], packed, near, token_blocks, fars
    )
    places = jnp.concatenate([p * rows_count + jnp.arange(rows_count, dtype=jnp.int32) for p in order_in])
    inverse = THETA ** (-jnp.arange(HD // 2, dtype=F32) * 2.0 / HD)
    angles = places.astype(F32)[:, None] * inverse[None, :]
    cosine, sine = jnp.cos(angles), jnp.sin(angles)
    cosine = jnp.concatenate([cosine, cosine], axis=-1)
    sine = jnp.concatenate([-sine, sine], axis=-1)
    segment_all = jnp.concatenate(
        [lax.dynamic_slice_in_dim(segments[0], p * rows_count, rows_count) for p in order_in]
    )
    attn_args = (cosine, sine, gain_query, gain_key, segment_all[:, None], segment_all[None, :])
    mixed_b = attention_forward(qkv, attn_args)
    planes = rep_count // 2
    for k in range(1, planes - 1):
        grad_held, crossed = turn_and_cross(after(grad_held, fars[-1]), rep_count)
        grad_blocks += [crossed, grad_held]
        if k == 1:
            mixed_b = after(mixed_b, grad_held)
    projected = dot(mixed_b, w_out).astype(BF)
    projected = [projected[i * rows_count : (i + 1) * rows_count] for i in range(shard_count)]
    tokens_f = tokens.astype(F32)
    attended = shard_reduce(projected)
    full_down = lax.all_gather(
        after(w_down, attended, grad_held), "shard", axis=1, tiled=True
    )
    hidden_state = tokens_f + attended

    scale_mid = rms_scale(hidden_state)
    normed_mid = hidden_state * scale_mid
    mid_b = (normed_mid * gain_ffn).astype(BF)
    first_expert = rep * local_experts
    slot_lanes, slots, named_lanes = read_names(
        first_expert[None], fars, experts, local_experts, rows_count
    )
    router_lanes = jnp.pad(full_router, ((0, 0), (0, HD - experts)))
    number = jnp.stack([first_expert, jnp.int32(experts)])
    picked, groups = [], []
    mid_b = after(mid_b, grad_held, slots, slot_lanes, named_lanes)

    def pick_next(block):
        b = len(picked)
        place = b % group_size
        held = picked[-1][:2] if place else None
        picked.append(
            pick(
                number,
                slot_lanes,
                named_lanes,
                router_lanes,
                block,
                grad_blocks[b],
                held,
                b,
                place,
                group_size,
                capacity,
            )
        )
        if place == group_size - 1:
            x, dy = [
                a.reshape(local_experts, group_size * capacity, width) for a in picked[-1][:2]
            ]
            groups.append((x, dy))

    def run_group(group, *others):
        x, dy = groups[group]
        done = run_experts(after(x, *others), dy, full_gate, full_up, full_down)
        groups[group] = (x, dy, done)
        return done[0]

    def merge_grads(group):
        return merge_rows(slots, group * group_size, groups[group][2][1], group_size)

    def merge_group(group, *ready):
        members = slice(group * group_size, (group + 1) * group_size)
        *parts, dgate = merge_results(
            after(slots, *ready),
            group * group_size,
            [p[2] for p in picked[members]],
            grad_blocks[members],
            groups[group][2][0],
        )
        return parts, dgate

    held, crossed = mid_b, None
    for k in range(planes):
        if k > 0:
            held, x = together(held, picked[-1][0])
            picked[-1] = (x,) + picked[-1][1:]
        if k < planes - 1:
            nexts, crossing = turn_and_cross(held, rep_count)
        else:
            nexts, crossing = None, last_crossing(held, crossed, rep_count)
        if k > 0:
            pick_next(crossed)
        pick_next(held)
        held, crossed = nexts, crossing
    grad_blocks.append(swap_y(after(grad_held, crossed), rep_count))
    grad_parts, result_parts, dgate_parts = [], [], []
    last = rep_count // group_size - 1
    ready = ()
    for g in range(last):
        run_group(g, *ready)
        grad_parts += merge_grads(g)
        ready = (grad_parts[-1],)
    cross_first = swap_y(grad_parts[3], rep_count)
    cross_zero = swap_y(grad_parts[1], rep_count)
    pick_next(after(crossed, *ready))
    y = run_group(last)
    cross_first, cross_zero, y = together(cross_first, cross_zero, y)
    total = turn_z(added(grad_parts[2], cross_first).astype(BF), rep_count)
    grad_parts += merge_grads(last)
    arrived = swap_y(grad_parts[5], rep_count)
    for g in range(last + 1):
        parts, dgate = merge_group(g, grad_parts[-1])
        result_parts += parts
        dgate_parts.append(dgate)

    def owned_part(grad):
        return lax.psum_scatter(grad, "shard", scatter_dimension=0, tiled=True)

    def wide_grads(j, *others):
        return weight_grads(
            [after(g[0], *others) for g in groups],
            [[g[2][3] for g in groups], [g[2][4] for g in groups]],
            j,
            j,
        )

    def down_grads(j, *others):
        return weight_grads(
            [after(g[2][2], *others) for g in groups], [[g[1] for g in groups]], j, j
        )[0]

    arrived = after(arrived, *result_parts, *dgate_parts)
    dgates = jnp.swapaxes(jnp.concatenate(dgate_parts), 1, 2)
    dgates = jnp.zeros_like(dgates).at[order_array].set(dgates)
    made = []
    for k in range(2, planes):
        total = added(grad_parts[2 * k], arrived, total).astype(BF)
        if k == 2:
            total, dgates = together(total, dgates)
        if k < planes - 1:
            total, arrived = together(
                turn_z(total, rep_count), swap_y(after(grad_parts[2 * k + 3], arrived), rep_count)
            )
            if not made:
                made.append(wide_grads(0, grad_parts[-1], *result_parts))
                total, arrived = together(total, arrived, *made[0])[:2]
        else:
            sent = total
            total = turn_z(total, rep_count)
            while len(made) < local_experts:
                made.append(wide_grads(len(made), sent))
                total = together(total, *made[-1])[0]
    results_sum = RepReduce(result_parts, rep_count, arrived)
    total = after(total, *results_sum.arrived)
    grad_mid_moe = added(grad_parts[0], cross_zero, total)

    dgates = lax.all_to_all(dgates, "rep", split_axis=0, concat_axis=0, tiled=True)
    dgates = dgates.reshape(experts, rows_count).T
    logits = dot(mid_b, full_router)
    exps = jnp.exp(logits - jnp.max(logits, axis=-1, keepdims=True))
    probs_own = exps / jnp.sum(exps, axis=-1, keepdims=True)
    chosen_total = jnp.sum(jnp.where(named_own, probs_own, 0.0), axis=1, keepdims=True)
    gates_own = jnp.where(named_own, probs_own, 0.0) / chosen_total
    grad_probs = jnp.where(
        named_own, dgates - jnp.sum(dgates * gates_own, axis=1, keepdims=True), 0.0
    ) / chosen_total
    grad_logits = (
        probs_own * (grad_probs - jnp.sum(probs_own * grad_probs, axis=1, keepdims=True))
    ).astype(BF)
    grad_mid = grad_mid_moe + dot_t(grad_logits, full_router)
    grad_gain_ffn = jnp.sum(grad_mid * normed_mid, axis=0)
    grad_router = t_dot(mid_b, grad_logits)
    grad_out = cotangent.astype(F32)
    grad_state = grad_out + norm_back(grad_mid * gain_ffn, normed_mid, scale_mid)
    grad_state_b = grad_state.astype(BF)

    far_state = swap_x(grad_state_b)
    while len(results_sum.order) > 2:
        results_sum.step()
    downs = [down_grads(j, grad_state_b) for j in range(local_experts)]
    far_state, *both = together(far_state, *results_sum.arrived, *downs)
    results_sum.arrived, downs = tuple(both[:2]), both[2:]
    state_blocks = [grad_state_b, swap_core(grad_state_b), far_state, swap_core(far_state)]
    grad_state_all = jnp.concatenate(state_blocks, axis=0)
    grad_mixed = dot_t(grad_state_all, w_out).astype(BF)
    heads = qkv.shape[1] // (3 * HD)
    results_sum.step()
    grad_qkv, grad_head_gains = attention_backward(qkv, grad_mixed, attn_args, 0, heads)
    grad_qkv, *results_sum.arrived = together(grad_qkv, *results_sum.arrived)
    grad_columns = t_dot(input_b, grad_qkv).astype(BF)
    grad_out_proj = t_dot(mixed_b, grad_state_all).astype(BF)
    grad_input = dot_t(after(grad_qkv, grad_columns), columns).astype(BF)
    grad_input = shard_reduce(
        [grad_input[i * rows_count : (i + 1) * rows_count] for i in range(shard_count)]
    )
    normed_in = tokens_f * rms_scale(tokens_f)
    tokens_grad = (
        grad_state + norm_back(grad_input * gain_attn, normed_in, rms_scale(tokens_f))
    ).astype(BF)
    sums_gate = [owned_part(after(m[0], grad_mixed)) for m in made]
    sums_up = [owned_part(after(m[1], grad_mixed)) for m in made]

    piece = HD // shard_count
    head_columns = jnp.pad(
        grad_head_gains[:2].reshape(2, shard_count, piece), ((0, 0), (0, 0), (0, rows - piece))
    ).reshape(2, width)
    extras = jnp.concatenate(
        [grad_router, grad_gain_ffn[:, None], head_columns.T], axis=1
    )
    extras = jnp.pad(extras, ((0, 0), (0, HD - extras.shape[1]))).astype(BF)
    out_columns = jnp.swapaxes(grad_out_proj.reshape(rows, shard_count, -1), 0, 1)
    out_columns = out_columns.reshape(shard_count, rep_count, part, -1)
    column_parts = grad_columns.reshape(shard_count, rep_count, part, -1)
    extra_parts = extras.reshape(shard_count, rep_count, part, -1)
    to_sum = jnp.concatenate([column_parts, extra_parts, out_columns], axis=3)
    to_sum = [lax.dynamic_index_in_dim(to_sum, r, axis=1, keepdims=False) for r in order]
    sums = RepReduce(to_sum, rep_count, split=True)
    expert_sum = None
    while expert_sum is None:
        expert_sum = results_sum.step()
    sums_down = [owned_part(after(d, grad_mixed)) for d in downs]
    part_sum = None
    while part_sum is None:
        part_sum = sums.step()
    part_sum = part_sum.astype(BF)
    output = (hidden_state + expert_sum).astype(BF)
    grad_gate = jnp.stack(sums_gate).astype(F32)
    grad_up = jnp.stack(sums_up).astype(F32)
    grad_down = jnp.stack(sums_down).astype(F32)
    split = grad_columns.shape[1] + HD
    mine = lax.all_to_all(part_sum[:, :, :split], "shard", split_axis=0, concat_axis=0, tiled=True)
    wide = jnp.swapaxes(mine[:, :, : split - HD], 0, 1).reshape(part, -1)
    extra = jnp.sum(mine[:, :, split - HD :].astype(F32), axis=0).astype(BF)
    out_part = jnp.swapaxes(part_sum[:, :, split:], 0, 1).reshape(part, -1)
    gathered = rep_gather(
        jnp.concatenate([wide, out_part, extra], axis=1),
        rep_count,
        {2: (grad_gate, grad_up, output), 3: (grad_down, tokens_grad)},
    )
    gain_rows = norm_attn.astype(F32)[:, None]
    most = rep_count - 1
    held = write_sums(order_array[:most], w_query, w_key, w_value, gain_rows, gathered[:most])
    sum_query, sum_key, sum_value, sum_out, extra = write_sums(
        order_array[most:], w_query, w_key, w_value, gain_rows, gathered[most:], held
    )
    return (
        output,
        tokens_grad,
        sum_query,
        sum_key,
        sum_value,
        sum_out,
        extra[:, :experts],
        extra[:, HD - 1],
        extra[:, experts],
        extra[:piece, experts + 1],
        extra[:piece, experts + 2],
        grad_gate,
        grad_up,
        grad_down,
    )


def solution(mesh):
    return jax.shard_map(
        on_device,
        mesh=mesh,
        in_specs=(
            P(("rep", "shard"), None),
            P("shard", None),
            P("shard", None),
            P("shard", None),
            P("shard", None),
            P("shard", None),
            P("shard"),
            P("shard"),
            P("shard"),
            P("shard"),
            P("rep", "shard", None),
            P("rep", "shard", None),
            P("rep", "shard", None),
            P("rep", None),
            P(("rep", "shard"), None),
            P(("rep", "shard"), None),
        ),
        out_specs=(
            P(("rep", "shard"), None),
            P(("rep", "shard"), None),
            P("shard", None),
            P("shard", None),
            P("shard", None),
            P("shard", None),
            P("shard", None),
            P("shard"),
            P("shard"),
            P("shard"),
            P("shard"),
            P("rep", "shard", None),
            P("rep", "shard", None),
            P("rep", "shard", None),
        ),
        check_vma=False,
    )
```

```python
import functools

import jax
import jax.numpy as jnp
from jax import lax
from jax.experimental import pallas as pl
from jax.experimental.pallas import tpu as pltpu
from jax.sharding import PartitionSpec as P

HEADS = 16
HD = 128
TOP = 8

EPSILON = 1e-05
THETA = 50000.0
MASKED = -1e30
BF = jnp.bfloat16
F32 = jnp.float32
QCHUNK = 256
VMEM = 58 << 20


def rms_scale(values):
    return lax.rsqrt(jnp.mean(values * values, axis=-1, keepdims=True) + EPSILON)


def norm_back(grad, normed, scale):
    return scale * (grad - normed * jnp.mean(grad * normed, axis=-1, keepdims=True))


def dot(left, right):
    return jnp.dot(left, right, preferred_element_type=F32)


def dot_t(left, right):
    return lax.dot_general(left, right, (((1,), (1,)), ((), ())), preferred_element_type=F32)


def t_dot(left, right):
    return lax.dot_general(left, right, (((0,), (0,)), ((), ())), preferred_element_type=F32)


def params(mib=40):
    return pltpu.CompilerParams(vmem_limit_bytes=mib << 20)


def cost(flops, size, transcendentals=0):
    return pl.CostEstimate(
        flops=int(flops), bytes_accessed=int(size), transcendentals=int(transcendentals)
    )


def after(value, *others):
    return lax.optimization_barrier((value,) + others)[0]


def together(*values):
    return lax.optimization_barrier(values)


def pack_columns(q_ref, k_ref, v_ref, out_ref):
    for h in range(q_ref.shape[1] // HD):
        for m, ref in enumerate((q_ref, k_ref, v_ref)):
            start = (3 * h + m) * HD
            out_ref[0, :, start : start + HD] = ref[:, h * HD : (h + 1) * HD]


def packed_columns(w_query, w_key, w_value, shards):
    rows, width = w_query.shape
    part = width // shards
    spec = pl.BlockSpec((rows, part), lambda s: (0, s))
    return pl.pallas_call(
        pack_columns,
        grid=(shards,),
        in_specs=[spec, spec, spec],
        out_specs=pl.BlockSpec((1, rows, 3 * part), lambda s: (s, 0, 0)),
        out_shape=jax.ShapeDtypeStruct((shards, rows, 3 * part), BF),
        compiler_params=params(),
        cost_estimate=cost(0, 12 * rows * width),
    )(w_query, w_key, w_value)


def pack_part(place_ref, q_ref, k_ref, v_ref, out_ref):
    pack_columns(q_ref, k_ref, v_ref, out_ref)


def packed_part(place, w_query, w_key, w_value, shards, part):
    width = w_query.shape[1] // shards
    spec = pl.BlockSpec((part, width), lambda s, n: (n[0], 2 * n[1] + s))
    return pl.pallas_call(
        pack_part,
        grid_spec=pltpu.PrefetchScalarGridSpec(
            num_scalar_prefetch=1,
            grid=(2,),
            in_specs=[spec, spec, spec],
            out_specs=pl.BlockSpec((1, part, 3 * width), lambda s, n: (s, 0, 0)),
        ),
        out_shape=jax.ShapeDtypeStruct((2, part, 3 * width), BF),
        compiler_params=params(58),
        cost_estimate=cost(0, 24 * part * width),
    )(place, w_query, w_key, w_value)


def project_body(parts, order_ref, shard_ref, gain_ref, packed_ref, near_ref, *refs):
    token_refs, far_refs = refs[:4], refs[4 : 4 + parts]
    input_ref, columns_ref, qkv_ref, sem = refs[4 + parts :]
    rows = near_ref.shape[0]
    count = token_refs[0].shape[0]
    part = rows // parts

    def place(start, size):
        return columns_ref.at[pl.ds(pl.multiple_of(start, 16), size)]

    copies = [
        pltpu.make_async_copy(packed_ref.at[shard_ref[0]], place(shard_ref[0] * rows, rows), sem.at[0]),
        pltpu.make_async_copy(near_ref, place(shard_ref[1] * rows, rows), sem.at[1]),
    ]
    for i in range(parts):
        for m in range(2):
            start = shard_ref[2 + m] * rows + order_ref[i] * part
            copies.append(
                pltpu.make_async_copy(
                    far_refs[i].at[m, pl.ds(0, part)], place(start, part), sem.at[2 + 2 * i + m]
                )
            )
    for copy in copies:
        copy.start()
    for i in range(4):
        x = token_refs[i][...].astype(F32)
        input_ref[i * count : (i + 1) * count, :] = (x * rms_scale(x) * gain_ref[...]).astype(BF)
    for copy in copies:
        copy.wait()

    def step(i, carry):
        r = pl.ds(pl.multiple_of(i * count, count), count)
        qkv_ref[r, :] = dot(input_ref[r, :], columns_ref[...])
        return carry

    lax.fori_loop(0, 4, step, 0)


def project(order, shards, gain, packed, near, token_blocks, fars):
    count, width = token_blocks[0].shape
    columns = near.shape[1]
    length = count * len(token_blocks)
    anywhere = pl.BlockSpec(memory_space=pl.ANY)
    whole = lambda *shape: pl.BlockSpec(shape, lambda i, a, b: (0, 0))
    return pl.pallas_call(
        functools.partial(project_body, len(fars)),
        grid_spec=pltpu.PrefetchScalarGridSpec(
            num_scalar_prefetch=2,
            grid=(1,),
            in_specs=[whole(1, width), anywhere, anywhere]
            + [whole(count, width)] * 4
            + [anywhere] * len(fars),
            out_specs=[whole(length, width), whole(width, columns), whole(length, columns)],
            scratch_shapes=[pltpu.SemaphoreType.DMA((2 + 2 * len(fars),))],
        ),
        out_shape=[
            jax.ShapeDtypeStruct((length, width), BF),
            jax.ShapeDtypeStruct((width, columns), BF),
            jax.ShapeDtypeStruct((length, columns), F32),
        ],
        compiler_params=params(56),
        cost_estimate=cost(
            2 * length * width * columns, 4 * length * width + 4 * width * columns + 4 * length * columns
        ),
    )(order, shards, gain, packed, near, *token_blocks, *fars)


def turned(values, cosine, sine):
    return values * cosine + pltpu.roll(values, HD // 2, 1) * sine


def turned_back(grad, cosine, sine):
    return grad * cosine - pltpu.roll(grad, HD // 2, 1) * sine


def weights_of(qb, keys, seg_column, seg_row):
    scores = dot_t(qb, keys) * (HD**-0.5)
    scores = jnp.where(seg_column == seg_row, scores, MASKED)
    shifted = jnp.exp(scores - jnp.max(scores, axis=-1, keepdims=True))
    return shifted * (1.0 / jnp.sum(shifted, axis=-1, keepdims=True))


def attend_forward(qkv_ref, cos_ref, sin_ref, gq_ref, gk_ref, segc_ref, segr_ref, o_ref, kb_ref, vb_ref):
    length = qkv_ref.shape[0]
    k_raw = qkv_ref[:, HD : 2 * HD]
    kb_ref[...] = turned(k_raw * rms_scale(k_raw) * gk_ref[...], cos_ref[...], sin_ref[...]).astype(BF)
    vb_ref[...] = qkv_ref[:, 2 * HD :].astype(BF)

    def step(i, carry):
        rows = pl.ds(pl.multiple_of(i * QCHUNK, QCHUNK), QCHUNK)
        q_raw = qkv_ref[rows, :HD]
        qb = turned(q_raw * rms_scale(q_raw) * gq_ref[...], cos_ref[rows, :], sin_ref[rows, :]).astype(BF)
        probs = weights_of(qb, kb_ref[...], segc_ref[rows, :], segr_ref[...])
        o_ref[rows, :] = dot(probs.astype(BF), vb_ref[...]).astype(BF)
        return carry

    lax.fori_loop(0, length // QCHUNK, step, 0)


def attend_backward(
    qkv_ref,
    do_ref,
    cos_ref,
    sin_ref,
    gq_ref,
    gk_ref,
    segc_ref,
    segr_ref,
    *refs,
):
    grad_ref, gains_ref, kb_ref, vb_ref, dk_acc, dv_acc = refs[-6:]
    length = qkv_ref.shape[0]
    scale = HD**-0.5

    @pl.when(pl.program_id(0) == 0)
    def _():
        gains_ref[...] = jnp.zeros_like(gains_ref)

    k_raw = qkv_ref[:, HD : 2 * HD]
    kb_ref[...] = turned(k_raw * rms_scale(k_raw) * gk_ref[...], cos_ref[...], sin_ref[...]).astype(BF)
    vb_ref[...] = qkv_ref[:, 2 * HD :].astype(BF)
    dk_acc[...] = jnp.zeros_like(dk_acc)
    dv_acc[...] = jnp.zeros_like(dv_acc)

    def step(i, carry):
        rows = pl.ds(pl.multiple_of(i * QCHUNK, QCHUNK), QCHUNK)
        cosine, sine = cos_ref[rows, :], sin_ref[rows, :]
        q_raw = qkv_ref[rows, :HD]
        q_scale = rms_scale(q_raw)
        q_norm = q_raw * q_scale
        qb = turned(q_norm * gq_ref[...], cosine, sine).astype(BF)
        probs = weights_of(qb, kb_ref[...], segc_ref[rows, :], segr_ref[...])
        grad_o = do_ref[rows, :]
        grad_probs = dot_t(grad_o, vb_ref[...])
        dv_acc[...] += t_dot(probs.astype(BF), grad_o)
        weighted = probs * grad_probs
        grad_scores = (weighted - probs * jnp.sum(weighted, axis=-1, keepdims=True)).astype(BF)
        dk_acc[...] += t_dot(grad_scores, qb)
        eq = turned_back(dot(grad_scores, kb_ref[...]) * scale, cosine, sine)
        gains_ref[0:1, :] += jnp.sum(eq * q_norm, axis=0, keepdims=True)
        grad_ref[rows, :HD] = norm_back(eq * gq_ref[...], q_norm, q_scale).astype(BF)
        return carry

    lax.fori_loop(0, length // QCHUNK, step, 0)
    ek = turned_back(dk_acc[...] * scale, cos_ref[...], sin_ref[...])
    k_raw = qkv_ref[:, HD : 2 * HD]
    k_scale = rms_scale(k_raw)
    k_norm = k_raw * k_scale
    gains_ref[1:2, :] += jnp.sum(ek * k_norm, axis=0, keepdims=True)
    grad_ref[:, HD : 2 * HD] = norm_back(ek * gk_ref[...], k_norm, k_scale).astype(BF)
    grad_ref[:, 2 * HD :] = dv_acc[...].astype(BF)


def attention_specs(length):
    table = pl.BlockSpec((length, HD), lambda h: (0, 0))
    gain = pl.BlockSpec((1, HD), lambda h: (0, 0))
    column = pl.BlockSpec((length, 1), lambda h: (0, 0))
    row = pl.BlockSpec((1, length), lambda h: (0, 0))
    return [table, table, gain, gain, column, row]


def attention_forward(qkv, attn_args):
    length = qkv.shape[0]
    heads = qkv.shape[1] // (3 * HD)
    return pl.pallas_call(
        attend_forward,
        grid=(heads,),
        in_specs=[pl.BlockSpec((length, 3 * HD), lambda h: (0, h))] + attention_specs(length),
        out_specs=pl.BlockSpec((length, HD), lambda h: (0, h)),
        out_shape=jax.ShapeDtypeStruct((length, heads * HD), BF),
        scratch_shapes=[pltpu.VMEM((length, HD), BF)] * 2,
        compiler_params=params(58),
        cost_estimate=cost(16 * heads * length * length * HD, qkv.size * 5, heads * length * length),
    )(qkv, *attn_args)


def attention_backward(qkv, grad_o, attn_args, first, heads, held=None):
    length = qkv.shape[0]
    wide = pl.BlockSpec((length, 3 * HD), lambda h: (0, first + h))
    return pl.pallas_call(
        attend_backward,
        grid=(heads,),
        in_specs=[wide, pl.BlockSpec((length, HD), lambda h: (0, first + h))]
        + attention_specs(length)
        + [pl.BlockSpec(memory_space=pl.ANY)] * (held is not None),
        out_specs=[wide, pl.BlockSpec((8, HD), lambda h: (0, 0))],
        out_shape=[
            jax.ShapeDtypeStruct(qkv.shape, BF),
            jax.ShapeDtypeStruct((8, HD), F32),
        ],
        scratch_shapes=[pltpu.VMEM((length, HD), BF)] * 2 + [pltpu.VMEM((length, HD), F32)] * 2,
        input_output_aliases={} if held is None else {8: 0},
        compiler_params=params(58),
        cost_estimate=cost(40 * heads * length * length * HD, qkv.size * 3, heads * length * length),
    )(qkv, grad_o, *attn_args, *(() if held is None else (held,)))


def read_names_body(experts, local, first_ref, *refs):
    name_refs, (lanes_ref, slots_ref, named_ref) = refs[:-3], refs[-3:]
    count = lanes_ref.shape[2]
    row = lax.broadcasted_iota(jnp.int32, (count, count), 0)
    column = lax.broadcasted_iota(jnp.int32, (count, count), 1)
    earlier = (row < column).astype(BF)
    expert_row = lax.broadcasted_iota(jnp.int32, (experts, count), 0)
    for b, ref in enumerate(name_refs):
        named = ref[0, ref.shape[1] - experts :, :]
        slots = jnp.where(named > 0, dot(named, earlier), -1.0)
        mine = [
            jnp.sum(jnp.where(expert_row == first_ref[0] + j, slots, 0.0), axis=0, keepdims=True)
            for j in range(local)
        ]
        mine = jnp.concatenate(mine, axis=0)
        lanes_ref[b] = mine.astype(jnp.int32)
        filled = jnp.concatenate([mine, jnp.zeros((HD - local, count), F32)], axis=0)
        slots_ref[b] = filled.T.astype(jnp.int32)
        filled = jnp.concatenate([named.astype(F32), jnp.zeros((HD - experts, count), F32)], axis=0)
        named_ref[b] = filled.T


def read_names(first, blocks, experts, local, count):
    number, height = len(blocks), blocks[0].shape[1]
    whole = lambda *shape: pl.BlockSpec(shape, lambda i, n: (0, 0, 0))
    return pl.pallas_call(
        functools.partial(read_names_body, experts, local),
        grid_spec=pltpu.PrefetchScalarGridSpec(
            num_scalar_prefetch=1,
            grid=(1,),
            in_specs=[whole(1, height, count)] * number,
            out_specs=[whole(number, local, count), whole(number, count, HD), whole(number, count, HD)],
        ),
        out_shape=[
            jax.ShapeDtypeStruct((number, local, count), jnp.int32),
            jax.ShapeDtypeStruct((number, count, HD), jnp.int32),
            jax.ShapeDtypeStruct((number, count, HD), F32),
        ],
        compiler_params=params(),
        cost_estimate=cost(2 * number * experts * count * count, 10 * number * count * HD),
    )(first, *blocks)


def pick_rows(has_input, number_ref, slots_ref, named_ref, router_ref, x_ref, grad_ref, *refs):
    rows_ref, grad_rows_ref, gates_ref = refs[2 * has_input :]
    experts, capacity = slots_ref.shape[1], rows_ref.shape[2]
    count = x_ref.shape[0]
    x = x_ref[...]
    logits = dot(x, router_ref[...])
    lane = lax.broadcasted_iota(jnp.int32, logits.shape, 1)
    logits = jnp.where(lane < number_ref[1], logits, MASKED)
    exps = jnp.exp(logits - jnp.max(logits, axis=-1, keepdims=True))
    probs = exps / jnp.sum(exps, axis=-1, keepdims=True)
    chosen = jnp.where(named_ref[0] > 0.0, probs, 0.0)
    gates = chosen / jnp.sum(chosen, axis=-1, keepdims=True)
    grad = grad_ref[...].astype(F32)
    wanted = lax.broadcasted_iota(jnp.int32, (capacity, count), 0)
    columns = []
    for j in range(experts):
        gate = jnp.sum(jnp.where(lane == number_ref[0] + j, gates, 0.0), axis=1, keepdims=True)
        hot = (wanted == slots_ref[0, j : j + 1, :]).astype(BF)
        rows_ref[j, 0] = dot(hot, x).astype(BF)
        grad_rows_ref[j, 0] = dot(hot, (grad * gate).astype(BF)).astype(BF)
        columns.append(gate)
    gates_ref[...] = jnp.concatenate(columns, axis=1)


def pick(number, slots, named, router, x, grad, held, block, place, blocks, capacity):
    count, width = x.shape
    experts = slots.shape[1]
    lanes = router.shape[1]
    shape = jax.ShapeDtypeStruct((experts, blocks, capacity, width), BF)
    whole = pl.BlockSpec(memory_space=pl.ANY)
    out = pl.BlockSpec((experts, 1, capacity, width), lambda i, n: (0, place, 0, 0))
    return pl.pallas_call(
        functools.partial(pick_rows, held is not None),
        grid_spec=pltpu.PrefetchScalarGridSpec(
            num_scalar_prefetch=1,
            grid=(1,),
            in_specs=[
                pl.BlockSpec((1, experts, count), lambda i, n: (block, 0, 0)),
                pl.BlockSpec((1, count, lanes), lambda i, n: (block, 0, 0)),
                pl.BlockSpec((width, lanes), lambda i, n: (0, 0)),
                pl.BlockSpec((count, width), lambda i, n: (0, 0)),
                pl.BlockSpec((count, width), lambda i, n: (0, 0)),
            ]
            + [whole, whole] * (held is not None),
            out_specs=[out, out, pl.BlockSpec((count, experts), lambda i, n: (0, 0))],
        ),
        out_shape=[shape, shape, jax.ShapeDtypeStruct((count, experts), F32)],
        input_output_aliases={} if held is None else {6: 0, 7: 1},
        compiler_params=params(58),
        cost_estimate=cost(
            4 * experts * capacity * count * width, 4 * width * (count + experts * capacity)
        ),
    )(number, slots, named, router, x, grad, *(held or ()))


def merge_rows_body(blocks, slots_ref, *refs):
    experts = len(refs) - blocks
    rows_refs, out_refs = refs[:experts], refs[experts:]
    capacity = rows_refs[0].shape[0]
    count = out_refs[0].shape[0]
    place = lax.broadcasted_iota(jnp.int32, (count, capacity), 1)
    total = None
    for j in range(experts):
        hot = (place == slots_ref[0, :, j : j + 1]).astype(BF)
        rows = dot(hot, rows_refs[j][...])
        total = rows if total is None else total + rows
    for i in range(blocks):

        @pl.when(pl.program_id(0) == i)
        def _(i=i):
            out_refs[i][...] = total.astype(BF)


def merge_rows(slots, first, rows, blocks):
    count, lanes = slots.shape[1:]
    experts = rows.shape[0]
    capacity = rows.shape[1] // blocks
    width = rows.shape[2]
    return pl.pallas_call(
        functools.partial(merge_rows_body, blocks),
        grid=(blocks,),
        in_specs=[pl.BlockSpec((1, count, lanes), lambda b: (first + b, 0, 0))]
        + [pl.BlockSpec((None, capacity, width), lambda b, j=j: (j, b, 0)) for j in range(experts)],
        out_specs=[pl.BlockSpec((count, width), lambda b: (0, 0))] * blocks,
        out_shape=[jax.ShapeDtypeStruct((count, width), BF)] * blocks,
        compiler_params=params(58),
        cost_estimate=cost(
            2 * blocks * experts * capacity * count * width,
            2 * blocks * width * (count + experts * capacity),
        ),
    )(slots, *[rows] * experts)


def merge_results_body(blocks, slots_ref, *refs):
    experts = len(refs) - 3 * blocks - 1
    gates_refs, grad_refs, refs = refs[:blocks], refs[blocks : 2 * blocks], refs[2 * blocks :]
    rows_refs, out_refs, dgate_ref = refs[:experts], refs[experts:-1], refs[-1]
    capacity = rows_refs[0].shape[0]
    count = out_refs[0].shape[0]
    place = lax.broadcasted_iota(jnp.int32, (count, capacity), 1)
    for i in range(blocks):

        @pl.when(pl.program_id(0) == i)
        def _(i=i):
            grad = grad_refs[i][...].astype(F32)
            total = None
            dgates = []
            for j in range(experts):
                hot = (place == slots_ref[0, :, j : j + 1]).astype(BF)
                rows = dot(hot, rows_refs[j][...])
                dgates.append(jnp.sum(rows * grad, axis=1, keepdims=True))
                gated = rows * gates_refs[i][:, j : j + 1]
                total = gated if total is None else total + gated
            out_refs[i][...] = total.astype(BF)
            dgate_ref[0] = jnp.concatenate(dgates, axis=1)


def merge_results(slots, first, gates, grads, rows):
    blocks = len(gates)
    count, lanes = slots.shape[1:]
    experts = rows.shape[0]
    capacity = rows.shape[1] // blocks
    width = rows.shape[2]
    tokens = pl.BlockSpec((count, width), lambda b: (0, 0))
    return pl.pallas_call(
        functools.partial(merge_results_body, blocks),
        grid=(blocks,),
        in_specs=[pl.BlockSpec((1, count, lanes), lambda b: (first + b, 0, 0))]
        + [pl.BlockSpec((count, experts), lambda b: (0, 0))] * blocks
        + [tokens] * blocks
        + [pl.BlockSpec((None, capacity, width), lambda b, j=j: (j, b, 0)) for j in range(experts)],
        out_specs=[tokens] * blocks + [pl.BlockSpec((1, count, experts), lambda b: (b, 0, 0))],
        out_shape=[jax.ShapeDtypeStruct((count, width), BF)] * blocks
        + [jax.ShapeDtypeStruct((blocks, count, experts), F32)],
        compiler_params=params(58),
        cost_estimate=cost(
            2 * blocks * experts * capacity * count * width,
            2 * blocks * width * (2 * count + experts * capacity),
        ),
    )(slots, *gates, *grads, *[rows] * experts)


def expert_body(
    sub,
    x_ref,
    dy_ref,
    wg_ref,
    wu_ref,
    wd_ref,
    y_ref,
    dx_ref,
    h_ref,
    dg_ref,
    du_ref,
    y_acc,
    dx_acc,
):
    f = pl.program_id(1)
    last = pl.num_programs(1) - 1

    def step(i, carry):
        r = pl.ds(pl.multiple_of(i * sub, sub), sub)
        x = x_ref[r, :]
        gate = dot(x, wg_ref[...])
        up = dot(x, wu_ref[...])
        grad_hidden = dot_t(dy_ref[r, :], wd_ref[...])
        sigmoid = 1.0 / (1.0 + jnp.exp(-gate))
        activated = gate * sigmoid
        hidden = (activated * up).astype(BF)
        h_ref[r, :] = hidden
        grad_gate = (grad_hidden * up * sigmoid * (1.0 + gate * (1.0 - sigmoid))).astype(BF)
        grad_up = (grad_hidden * activated).astype(BF)
        dg_ref[r, :] = grad_gate
        du_ref[r, :] = grad_up
        y = dot(hidden, wd_ref[...])
        dx = dot_t(grad_gate, wg_ref[...]) + dot_t(grad_up, wu_ref[...])

        @pl.when(f == 0)
        def _():
            y_acc[r, :] = y
            dx_acc[r, :] = dx

        @pl.when((f > 0) & (f < last))
        def _():
            y_acc[r, :] += y
            dx_acc[r, :] += dx

        @pl.when(f == last)
        def _():
            y_ref[r, :] = (y_acc[r, :] + y).astype(BF)
            dx_ref[r, :] = (dx_acc[r, :] + dx).astype(BF)

        return carry

    lax.fori_loop(0, x_ref.shape[0] // sub, step, 0)


def run_experts(x, dy, w_gate, w_up, w_down):
    experts, rows, width = x.shape
    hidden = w_gate.shape[2]
    tile = hidden // 2
    whole = pl.BlockSpec((None, rows, width), lambda j, f: (j, 0, 0))
    part = pl.BlockSpec((None, rows, tile), lambda j, f: (j, 0, f))
    wide = jax.ShapeDtypeStruct((experts, rows, width), BF)
    thin = jax.ShapeDtypeStruct((experts, rows, hidden), BF)
    return pl.pallas_call(
        functools.partial(expert_body, rows // 2),
        grid=(experts, 2),
        in_specs=[
            whole,
            whole,
            pl.BlockSpec((None, width, tile), lambda j, f: (j, 0, f)),
            pl.BlockSpec((None, width, tile), lambda j, f: (j, 0, f)),
            pl.BlockSpec((None, tile, width), lambda j, f: (j, f, 0)),
        ],
        out_specs=[whole, whole, part, part, part],
        out_shape=[wide, wide, thin, thin, thin],
        scratch_shapes=[pltpu.VMEM((rows, width), F32)] * 2,
        compiler_params=params(60),
        cost_estimate=cost(
            12 * experts * rows * width * hidden,
            experts * (8 * rows * width + 6 * rows * hidden + 6 * width * hidden),
            experts * rows * hidden,
        ),
    )(x, dy, w_gate, w_up, w_down)


def weight_grads_body(groups, count, *refs):
    left, rights, outs = refs[:groups], refs[groups : groups + groups * count], refs[-count:]
    for n in range(count):
        total = None
        for g in range(groups):
            part = t_dot(left[g][...], rights[n * groups + g][...])
            total = part if total is None else total + part
        outs[n][...] = total.astype(BF)


def weight_grads(lefts, rights, left_index, right_index):
    groups, count = len(lefts), len(rights)

    def tiled(array, index, tile):
        if array.ndim == 3:
            return pl.BlockSpec((None, array.shape[1], tile), lambda d: (index, 0, d))
        return pl.BlockSpec((array.shape[0], tile), lambda d: (0, d))

    def fixed(array, index):
        if array.ndim == 3:
            return pl.BlockSpec((None,) + array.shape[1:], lambda d: (index, 0, 0))
        return pl.BlockSpec(array.shape, lambda d: (0, 0))

    tall = lefts[0].shape[-1]
    wide = rights[0][0].shape[-1]
    tile = 256
    flat = [r for one in rights for r in one]
    total_rows = sum(a.shape[-2] for a in lefts)
    return pl.pallas_call(
        functools.partial(weight_grads_body, groups, count),
        grid=(tall // tile,),
        in_specs=[tiled(a, left_index, tile) for a in lefts] + [fixed(a, right_index) for a in flat],
        out_specs=[pl.BlockSpec((tile, wide), lambda d: (d, 0))] * count,
        out_shape=[jax.ShapeDtypeStruct((tall, wide), BF)] * count,
        compiler_params=params(58),
        cost_estimate=cost(
            2 * count * total_rows * tall * wide,
            2 * total_rows * (tall + count * wide) + 2 * count * tall * wide,
        ),
    )(*lefts, *flat)


def swap_core(value):
    return lax.ppermute(value, "shard", [(i, i ^ 1) for i in range(4)])


def swap_x(value):
    return lax.ppermute(value, "shard", [(i, i ^ 2) for i in range(4)])


def shard_order(position):
    return [position, position ^ 1, position ^ 2, position ^ 3]


def shard_gather(value):
    far = swap_x(value)
    near = swap_core(value)
    return [value, near, far, swap_core(far)]


def added(*terms):
    total = terms[0].astype(F32)
    for term in terms[1:]:
        total = total + term.astype(F32)
    return total


def shard_reduce(blocks):
    far = added(blocks[2], swap_core(blocks[3])).astype(BF)
    far = swap_x(far)
    near = added(blocks[0], swap_core(blocks[1]))
    return near + far.astype(F32)


def ring_next(count):
    return [(z * 2 + y, ((z + 1) % (count // 2)) * 2 + y) for z in range(count // 2) for y in range(2)]


def swap_y(value, count):
    return lax.ppermute(value, "rep", [(i, i ^ 1) for i in range(count)])


def turn_z(value, count):
    return lax.ppermute(value, "rep", ring_next(count))


def rep_order(rep, count):
    planes = count // 2
    z, y = rep // 2, rep % 2
    return [((z + planes - k) % planes) * 2 + (y ^ w) for k in range(planes) for w in range(2)]


def turn_and_cross(value, count):
    return together(turn_z(value, count), swap_y(value, count))


def last_crossing(held, before, count):
    half = held.shape[0] // 2
    return jnp.concatenate(together(swap_y(held[:half], count), turn_z(before[half:], count)), axis=0)


def rep_gather(value, count, ties=None):
    blocks = []
    held = value
    for k in range(count // 2):
        held = after(held, *(ties or {}).get(k, ()))
        if k < count // 2 - 1:
            nexts, crossed = together(turn_z(held, count), swap_y(held, count))
        else:
            nexts, crossed = None, last_crossing(held, blocks[-1], count)
        blocks += [held, crossed]
        held = nexts
    return blocks


class RepReduce:
    def __init__(self, blocks, count, *ready, split=False):
        self.blocks, self.count = list(blocks), count
        self.order = list(range(2, count // 2)) + [0]
        self.half = blocks[3].shape[0] // 2 if split else None
        first = after(blocks[3], *ready)
        if split:
            self.arrived = together(
                swap_y(first[: self.half], count), turn_z(first[self.half :], count)
            )
        else:
            self.arrived = (swap_y(first, count),)
        self.total = None
        self.k = 1

    def step(self, *ready):
        arrived = together(*self.arrived, *ready)[: len(self.arrived)]
        if self.half is not None and self.k == 1:
            half, (near, far) = self.half, arrived
            total = self.blocks[2].at[:half].add(near)
            self.blocks[5] = self.blocks[5].at[half:].add(far)
        else:
            total = added(self.blocks[2 * self.k], *arrived)
        if not self.order:
            return total
        self.k = self.order.pop(0)
        self.sent = total.astype(BF)
        self.arrived = together(
            swap_y(after(self.blocks[2 * self.k + 1], arrived[0]), self.count),
            turn_z(self.sent, self.count),
        )
        return None


def rep_reduce(blocks, count, *ready):
    reduce = RepReduce(blocks, count, *ready)
    while True:
        total = reduce.step()
        if total is not None:
            return total


def write_sums_body(blocks, ids_ref, wq_ref, wk_ref, wv_ref, gain_ref, *refs):
    in_refs, (q_ref, k_ref, v_ref, o_ref, extra_ref) = refs[:blocks], refs[-5:]
    width = q_ref.shape[1]
    heads = width // HD
    for i in range(blocks):

        @pl.when(pl.program_id(0) == i)
        def _(i=i):
            ref = in_refs[i]
            attn = None
            for m, (out, weight) in enumerate(((q_ref, wq_ref), (k_ref, wk_ref), (v_ref, wv_ref))):
                for h in range(heads):
                    start = (3 * h + m) * HD
                    piece = ref[:, start : start + HD].astype(F32)
                    out[:, h * HD : (h + 1) * HD] = piece
                    term = piece * weight[:, h * HD : (h + 1) * HD].astype(F32)
                    attn = term if attn is None else attn + term
            o_ref[...] = ref[:, 3 * width : 4 * width].astype(F32)
            extra = ref[:, 4 * width :].astype(F32)
            attn = jnp.sum(attn, axis=1, keepdims=True) / gain_ref[...]
            lane = lax.broadcasted_iota(jnp.int32, extra.shape, 1)
            extra_ref[...] = jnp.where(lane == extra.shape[1] - 1, attn, extra)


def write_sums(ids, w_query, w_key, w_value, gain, gathered, held=()):
    blocks = len(gathered)
    part, total = gathered[0].shape
    rows, width = w_query.shape
    own = pl.BlockSpec((part, width), lambda b, n: (n[b], 0))
    extra = pl.BlockSpec((part, HD), lambda b, n: (n[b], 0))
    big = jax.ShapeDtypeStruct((rows, width), F32)
    return pl.pallas_call(
        functools.partial(write_sums_body, blocks),
        grid_spec=pltpu.PrefetchScalarGridSpec(
            num_scalar_prefetch=1,
            grid=(blocks,),
            in_specs=[own, own, own, pl.BlockSpec((part, 1), lambda b, n: (n[b], 0))]
            + [pl.BlockSpec((part, total), lambda b, n: (0, 0))] * blocks
            + [pl.BlockSpec(memory_space=pl.ANY)] * len(held),
            out_specs=[own, own, own, own, extra],
        ),
        out_shape=[big, big, big, big, jax.ShapeDtypeStruct((rows, HD), F32)],
        input_output_aliases={5 + blocks + i: i for i in range(len(held))},
        compiler_params=params(58),
        cost_estimate=cost(0, blocks * part * width * 30),
    )(ids, w_query, w_key, w_value, gain, *gathered, *held)


def on_device(
    tokens,
    w_query,
    w_key,
    w_value,
    w_out,
    w_router,
    norm_attn,
    norm_ffn,
    norm_query,
    norm_key,
    w_gate,
    w_up,
    w_down,
    segments,
    routes,
    cotangent,
):
    rows_count, width = tokens.shape
    experts = w_router.shape[1]
    local_experts = w_gate.shape[0]
    rep_count = lax.axis_size("rep")
    shard_count = lax.axis_size("shard")
    position = lax.axis_index("shard")
    rep = lax.axis_index("rep")
    length = rows_count * shard_count
    capacity = max(2, rows_count * TOP * 9 // (8 * experts))
    capacity = -(-capacity // 16) * 16
    rows = w_query.shape[0]
    order = rep_order(rep, rep_count)
    order_in = shard_order(position)
    group_size = 4

    order_array = jnp.stack(order)
    order_in_array = jnp.stack(order_in)
    part = rows // rep_count
    core = position % 2

    far = packed_part(
        jnp.stack([rep, 1 - position // 2]), w_query, w_key, w_value, shard_count, part
    )
    far = swap_x(far)
    far_tokens = swap_x(tokens)
    grad_blocks = [cotangent]
    grad_held, crossed = turn_and_cross(grad_blocks[0], rep_count)
    grad_blocks += [crossed, grad_held]
    full_gate = lax.all_gather(after(w_gate, far, far_tokens, grad_held), "shard", axis=1, tiled=True)
    far = jnp.stack(
        [
            lax.dynamic_index_in_dim(far, core, 0, keepdims=False),
            swap_core(lax.dynamic_index_in_dim(far, 1 - core, 0, keepdims=False)),
        ]
    )
    expert_ids = jnp.arange(experts, dtype=jnp.int32)
    named_own = jnp.any(routes[:, :, None] == expert_ids, axis=1)
    names = jnp.pad(named_own.T.astype(BF), ((0, 0), (0, far.shape[2] - rows_count)))
    names = jnp.stack([names, names])
    full_up = lax.all_gather(
        after(w_up, far, far_tokens, grad_held), "shard", axis=1, tiled=True
    )
    fars = rep_gather(jnp.concatenate([far, names], axis=1), rep_count)
    packed = packed_columns(after(w_query, fars[1]), w_key, w_value, shard_count)
    near = swap_core(lax.dynamic_index_in_dim(packed, position ^ 1, 0, keepdims=False))
    token_blocks = [tokens, swap_core(tokens), far_tokens, swap_core(far_tokens)]
    small = jnp.concatenate(
        [
            w_router,
            norm_attn[:, None],
            norm_ffn[:, None],
            jnp.pad(norm_query, (0, rows - norm_query.shape[0]))[:, None],
            jnp.pad(norm_key, (0, rows - norm_key.shape[0]))[:, None],
        ],
        axis=1,
    )
    small = jnp.pad(small, ((0, 0), (0, HD - small.shape[1])))
    small = jnp.stack(shard_gather(small))
    small = jnp.zeros_like(small).at[order_in_array].set(small)
    head_gains = small[:, : norm_query.shape[0], experts + 2 : experts + 4].astype(F32)
    gain_query = head_gains[:, :, 0].reshape(1, HD)
    gain_key = head_gains[:, :, 1].reshape(1, HD)
    small = small.reshape(width, HD)
    gain_attn = small[:, experts].astype(F32)
    gain_ffn = small[:, experts + 1].astype(F32)
    full_router = small[:, :experts]

    input_b, columns, qkv = project(
        order_array, order_in_array, gain_attn[None, :], packed, near, token_blocks, fars
    )
    places = jnp.concatenate([p * rows_count + jnp.arange(rows_count, dtype=jnp.int32) for p in order_in])
    inverse = THETA ** (-jnp.arange(HD // 2, dtype=F32) * 2.0 / HD)
    angles = places.astype(F32)[:, None] * inverse[None, :]
    cosine, sine = jnp.cos(angles), jnp.sin(angles)
    cosine = jnp.concatenate([cosine, cosine], axis=-1)
    sine = jnp.concatenate([-sine, sine], axis=-1)
    segment_all = jnp.concatenate(
        [lax.dynamic_slice_in_dim(segments[0], p * rows_count, rows_count) for p in order_in]
    )
    attn_args = (cosine, sine, gain_query, gain_key, segment_all[:, None], segment_all[None, :])
    mixed_b = attention_forward(qkv, attn_args)
    planes = rep_count // 2
    for k in range(1, planes - 1):
        grad_held, crossed = turn_and_cross(after(grad_held, fars[-1]), rep_count)
        grad_blocks += [crossed, grad_held]
        if k == 1:
            mixed_b = after(mixed_b, grad_held)
    projected = dot(mixed_b, w_out).astype(BF)
    projected = [projected[i * rows_count : (i + 1) * rows_count] for i in range(shard_count)]
    tokens_f = tokens.astype(F32)
    attended = shard_reduce(projected)
    full_down = lax.all_gather(
        after(w_down, attended, grad_held), "shard", axis=1, tiled=True
    )
    hidden_state = tokens_f + attended

    scale_mid = rms_scale(hidden_state)
    normed_mid = hidden_state * scale_mid
    mid_b = (normed_mid * gain_ffn).astype(BF)
    first_expert = rep * local_experts
    slot_lanes, slots, named_lanes = read_names(
        first_expert[None], fars, experts, local_experts, rows_count
    )
    router_lanes = jnp.pad(full_router, ((0, 0), (0, HD - experts)))
    number = jnp.stack([first_expert, jnp.int32(experts)])
    picked, groups = [], []
    mid_b = after(mid_b, grad_held, slots, slot_lanes, named_lanes)

    def pick_next(block):
        b = len(picked)
        place = b % group_size
        held = picked[-1][:2] if place else None
        picked.append(
            pick(
                number,
                slot_lanes,
                named_lanes,
                router_lanes,
                block,
                grad_blocks[b],
                held,
                b,
                place,
                group_size,
                capacity,
            )
        )
        if place == group_size - 1:
            x, dy = [
                a.reshape(local_experts, group_size * capacity, width) for a in picked[-1][:2]
            ]
            groups.append((x, dy))

    def run_group(group, *others):
        x, dy = groups[group]
        done = run_experts(after(x, *others), dy, full_gate, full_up, full_down)
        groups[group] = (x, dy, done)
        return done[0]

    def merge_grads(group):
        return merge_rows(slots, group * group_size, groups[group][2][1], group_size)

    def merge_group(group, *ready):
        members = slice(group * group_size, (group + 1) * group_size)
        *parts, dgate = merge_results(
            after(slots, *ready),
            group * group_size,
            [p[2] for p in picked[members]],
            grad_blocks[members],
            groups[group][2][0],
        )
        return parts, dgate

    held, crossed = mid_b, None
    for k in range(planes):
        if k > 0:
            held, x = together(held, picked[-1][0])
            picked[-1] = (x,) + picked[-1][1:]
        if k < planes - 1:
            nexts, crossing = turn_and_cross(held, rep_count)
        else:
            nexts, crossing = None, last_crossing(held, crossed, rep_count)
        if k > 0:
            pick_next(crossed)
        pick_next(held)
        held, crossed = nexts, crossing
    grad_blocks.append(swap_y(after(grad_held, crossed), rep_count))
    grad_parts, result_parts, dgate_parts = [], [], []
    last = rep_count // group_size - 1
    ready = ()
    for g in range(last):
        run_group(g, *ready)
        grad_parts += merge_grads(g)
        ready = (grad_parts[-1],)
    cross_first = swap_y(grad_parts[3], rep_count)
    cross_zero = swap_y(grad_parts[1], rep_count)
    pick_next(after(crossed, *ready))
    y = run_group(last)
    cross_first, cross_zero, y = together(cross_first, cross_zero, y)
    total = turn_z(added(grad_parts[2], cross_first).astype(BF), rep_count)
    grad_parts += merge_grads(last)
    arrived = swap_y(grad_parts[5], rep_count)
    for g in range(last + 1):
        parts, dgate = merge_group(g, grad_parts[-1])
        result_parts += parts
        dgate_parts.append(dgate)

    def owned_part(grad):
        return lax.psum_scatter(grad, "shard", scatter_dimension=0, tiled=True)

    def wide_grads(j, *others):
        return weight_grads(
            [after(g[0], *others) for g in groups],
            [[g[2][3] for g in groups], [g[2][4] for g in groups]],
            j,
            j,
        )

    def down_grads(j, *others):
        return weight_grads(
            [after(g[2][2], *others) for g in groups], [[g[1] for g in groups]], j, j
        )[0]

    arrived = after(arrived, *result_parts, *dgate_parts)
    dgates = jnp.swapaxes(jnp.concatenate(dgate_parts), 1, 2)
    dgates = jnp.zeros_like(dgates).at[order_array].set(dgates)
    made = []
    for k in range(2, planes):
        total = added(grad_parts[2 * k], arrived, total).astype(BF)
        if k == 2:
            total, dgates = together(total, dgates)
        if k < planes - 1:
            total, arrived = together(
                turn_z(total, rep_count), swap_y(after(grad_parts[2 * k + 3], arrived), rep_count)
            )
            if not made:
                made.append(wide_grads(0, grad_parts[-1], *result_parts))
                total, arrived = together(total, arrived, *made[0])[:2]
        else:
            sent = total
            total = turn_z(total, rep_count)
            while len(made) < local_experts:
                made.append(wide_grads(len(made), sent))
                total = together(total, *made[-1])[0]
    results_sum = RepReduce(result_parts, rep_count, arrived)
    total = after(total, *results_sum.arrived)
    grad_mid_moe = added(grad_parts[0], cross_zero, total)

    dgates = lax.all_to_all(dgates, "rep", split_axis=0, concat_axis=0, tiled=True)
    dgates = dgates.reshape(experts, rows_count).T
    logits = dot(mid_b, full_router)
    exps = jnp.exp(logits - jnp.max(logits, axis=-1, keepdims=True))
    probs_own = exps / jnp.sum(exps, axis=-1, keepdims=True)
    chosen_total = jnp.sum(jnp.where(named_own, probs_own, 0.0), axis=1, keepdims=True)
    gates_own = jnp.where(named_own, probs_own, 0.0) / chosen_total
    grad_probs = jnp.where(
        named_own, dgates - jnp.sum(dgates * gates_own, axis=1, keepdims=True), 0.0
    ) / chosen_total
    grad_logits = (
        probs_own * (grad_probs - jnp.sum(probs_own * grad_probs, axis=1, keepdims=True))
    ).astype(BF)
    grad_mid = grad_mid_moe + dot_t(grad_logits, full_router)
    grad_gain_ffn = jnp.sum(grad_mid * normed_mid, axis=0)
    grad_router = t_dot(mid_b, grad_logits)
    grad_out = cotangent.astype(F32)
    grad_state = grad_out + norm_back(grad_mid * gain_ffn, normed_mid, scale_mid)
    grad_state_b = grad_state.astype(BF)

    far_state = swap_x(grad_state_b)
    while len(results_sum.order) > 2:
        results_sum.step()
    downs = [down_grads(j, grad_state_b) for j in range(local_experts)]
    far_state, *both = together(far_state, *results_sum.arrived, *downs)
    results_sum.arrived, downs = tuple(both[:2]), both[2:]
    state_blocks = [grad_state_b, swap_core(grad_state_b), far_state, swap_core(far_state)]
    grad_state_all = jnp.concatenate(state_blocks, axis=0)
    grad_mixed = dot_t(grad_state_all, w_out).astype(BF)
    heads = qkv.shape[1] // (3 * HD)
    results_sum.step()
    grad_qkv, grad_head_gains = attention_backward(qkv, grad_mixed, attn_args, 0, heads)
    grad_qkv, *results_sum.arrived = together(grad_qkv, *results_sum.arrived)
    grad_columns = t_dot(input_b, grad_qkv).astype(BF)
    grad_out_proj = t_dot(mixed_b, grad_state_all).astype(BF)
    grad_input = dot_t(after(grad_qkv, grad_columns), columns).astype(BF)
    grad_input = shard_reduce(
        [grad_input[i * rows_count : (i + 1) * rows_count] for i in range(shard_count)]
    )
    normed_in = tokens_f * rms_scale(tokens_f)
    tokens_grad = (
        grad_state + norm_back(grad_input * gain_attn, normed_in, rms_scale(tokens_f))
    ).astype(BF)
    sums_gate = [owned_part(after(m[0], grad_mixed)) for m in made]
    sums_up = [owned_part(after(m[1], grad_mixed)) for m in made]

    piece = HD // shard_count
    head_columns = jnp.pad(
        grad_head_gains[:2].reshape(2, shard_count, piece), ((0, 0), (0, 0), (0, rows - piece))
    ).reshape(2, width)
    extras = jnp.concatenate(
        [grad_router, grad_gain_ffn[:, None], head_columns.T], axis=1
    )
    extras = jnp.pad(extras, ((0, 0), (0, HD - extras.shape[1]))).astype(BF)
    out_columns = jnp.swapaxes(grad_out_proj.reshape(rows, shard_count, -1), 0, 1)
    out_columns = out_columns.reshape(shard_count, rep_count, part, -1)
    column_parts = grad_columns.reshape(shard_count, rep_count, part, -1)
    extra_parts = extras.reshape(shard_count, rep_count, part, -1)
    to_sum = jnp.concatenate([column_parts, extra_parts, out_columns], axis=3)
    to_sum = [lax.dynamic_index_in_dim(to_sum, r, axis=1, keepdims=False) for r in order]
    sums = RepReduce(to_sum, rep_count, split=True)
    expert_sum = None
    while expert_sum is None:
        expert_sum = results_sum.step()
    sums_down = [owned_part(after(d, grad_mixed)) for d in downs]
    part_sum = None
    while part_sum is None:
        part_sum = sums.step()
    part_sum = part_sum.astype(BF)
    output = (hidden_state + expert_sum).astype(BF)
    grad_gate = jnp.stack(sums_gate).astype(F32)
    grad_up = jnp.stack(sums_up).astype(F32)
    grad_down = jnp.stack(sums_down).astype(F32)
    split = grad_columns.shape[1] + HD
    mine = lax.all_to_all(part_sum[:, :, :split], "shard", split_axis=0, concat_axis=0, tiled=True)
    wide = jnp.swapaxes(mine[:, :, : split - HD], 0, 1).reshape(part, -1)
    extra = jnp.sum(mine[:, :, split - HD :].astype(F32), axis=0).astype(BF)
    out_part = jnp.swapaxes(part_sum[:, :, split:], 0, 1).reshape(part, -1)
    gathered = rep_gather(
        jnp.concatenate([wide, out_part, extra], axis=1),
        rep_count,
        {2: (grad_gate, grad_up, output), 3: (tokens_grad,)},
    )
    gain_rows = norm_attn.astype(F32)[:, None]
    most = rep_count - 1
    held = write_sums(order_array[:most], w_query, w_key, w_value, gain_rows, gathered[:most])
    sum_query, sum_key, sum_value, sum_out, extra = write_sums(
        order_array[most:], w_query, w_key, w_value, gain_rows, gathered[most:], held
    )
    return (
        output,
        tokens_grad,
        sum_query,
        sum_key,
        sum_value,
        sum_out,
        extra[:, :experts],
        extra[:, HD - 1],
        extra[:, experts],
        extra[:piece, experts + 1],
        extra[:piece, experts + 2],
        grad_gate,
        grad_up,
        grad_down,
    )


def solution(mesh):
    return jax.shard_map(
        on_device,
        mesh=mesh,
        in_specs=(
            P(("rep", "shard"), None),
            P("shard", None),
            P("shard", None),
            P("shard", None),
            P("shard", None),
            P("shard", None),
            P("shard"),
            P("shard"),
            P("shard"),
            P("shard"),
            P("rep", "shard", None),
            P("rep", "shard", None),
            P("rep", "shard", None),
            P("rep", None),
            P(("rep", "shard"), None),
            P(("rep", "shard"), None),
        ),
        out_specs=(
            P(("rep", "shard"), None),
            P(("rep", "shard"), None),
            P("shard", None),
            P("shard", None),
            P("shard", None),
            P("shard", None),
            P("shard", None),
            P("shard"),
            P("shard"),
            P("shard"),
            P("shard"),
            P("rep", "shard", None),
            P("rep", "shard", None),
            P("rep", "shard", None),
        ),
        check_vma=False,
    )
```
